32 devices in a mesh: shard: 4 (over y, core), context: 2 (over x), tensor: 4 (over z).
Axes of the slice: x: 2, y: 2, z: 4, core: 2. Of those that a mesh axis runs over, the one named last changes fastest.
Arguments:
- block_input: bfloat16 [8192, 1536], P(('shard', 'context')), may hold values from -6 to 6
- norm_gain: float32 [1536], replicated, may hold values from 0.5 to 1.5
- w_z: bfloat16 [1536, 3072], P('shard', 'tensor'), may hold values from -0.15625 to 0.15625
- w_x: bfloat16 [1536, 3072], P('shard', 'tensor'), may hold values from -0.15625 to 0.15625
- w_bc: bfloat16 [1536, 256], P('shard'), may hold values from -0.15625 to 0.15625
- w_dt: bfloat16 [1536, 48], P('shard', 'tensor'), may hold values from -0.15625 to 0.15625
- conv_x_weight: float32 [4, 3072], P(None, 'tensor'), may hold values from -3 to 3
- conv_x_bias: float32 [3072], P('tensor'), may hold values from -1.5 to 1.5
- conv_bc_weight: float32 [4, 256], replicated, may hold values from -3 to 3
- conv_bc_bias: float32 [256], replicated, may hold values from -1.5 to 1.5
- dt_bias: float32 [48], P('tensor'), may hold values from -4 to -1
- a_log: float32 [48], P('tensor'), may hold values from -9 to 0
- d_skip: float32 [48], P('tensor'), may hold values from 0.5 to 1.5
- gate_gain: float32 [3072], P('tensor'), may hold values from 0.5 to 1.5
- w_out: bfloat16 [3072, 1536], P('tensor', 'shard'), may hold values from -0.109375 to 0.109375
- out_cotangent: bfloat16 [8192, 1536], P(('shard', 'context')), may hold values from -6 to 6
Outputs:
- block_output: bfloat16 [8192, 1536], P(('shard', 'context'))
- input_grad: float32 [8192, 1536], P(('shard', 'context'))
- grad_w_z: float32 [1536, 3072], P(('shard', 'context'), 'tensor')
- grad_w_x: float32 [1536, 3072], P(('shard', 'context'), 'tensor')
- grad_w_bc: float32 [1536, 256], P(('shard', 'context'))
- grad_w_dt: float32 [1536, 48], P(('shard', 'context'), 'tensor')
- grad_w_out: float32 [3072, 1536], P('tensor', ('shard', 'context'))
- grad_norm_gain: float32 [1536], replicated
- grad_conv_x_weight: float32 [4, 3072], P(None, 'tensor')
- grad_conv_x_bias: float32 [3072], P('tensor')
- grad_conv_bc_weight: float32 [4, 256], replicated
- grad_conv_bc_bias: float32 [256], replicated
- grad_dt_bias: float32 [48], P('tensor')
- grad_a_log: float32 [48], P('tensor')
- grad_d_skip: float32 [48], P('tensor')
- grad_gate_gain: float32 [3072], P('tensor')
The draws below stay inside these ranges and needn't reach their ends.
All inputs are finite; a program needn't handle non-finite values.
Results may differ from the reference program's by a relative error of at most 0.0021.
The reference program's roundings to bfloat16 on the way (of `normed`, `x_raw`, `bc_raw`, `gated_out`, `grad_z`, `grad_x_raw`, `grad_bc_raw` and `grad_dt_raw`) count: a program that leaves them out, or rounds other values in their place, can miss the bound.
Values may be sent and summed in bfloat16 or wider, within the bound.
No kernel may reach another device: no remote copies, remote signals or barrier semaphores. Data moves between devices by JAX's collectives and lax.ppermute only.
A program may use at most 192 MiB of HBM per device.

```python
import jax
import jax.numpy as jnp
from jax import lax

D = 1536
HEADS = 48
HEAD_DIM = 64
STATE = 128
CONV = 4
GROUP = 256
SEQ_LEN = 2048
DI = 3072
TOKENS = 8192
N_SHARD = 4


def steps_of(key, extent, cuts, smallest, largest):
    loudness = 1.0
    for position, parts in cuts:
        draws = jax.random.uniform(jax.random.fold_in(jax.random.fold_in(key, 6), position), (parts,), jnp.float32, smallest / len(cuts), largest / len(cuts))
        loudness = loudness * jnp.repeat(jnp.exp(draws), extent[position] // parts).reshape((-1,) + (1,) * (len(extent) - 1 - position))
    return loudness


def gaussian(stream_key, dims, deviation, limit, split=(), held_as=jnp.bfloat16):
    values = deviation * jax.random.normal(stream_key, dims, jnp.float32)
    if split:
        values = values * steps_of(stream_key, dims, split, -0.22, 0.18)
    return jnp.clip(values, -limit, limit).astype(held_as)


def setup_inputs(seed: int = 0) -> dict:
    seeds = jax.random.split(jax.random.key(seed), 17)
    return {
        "block_input": gaussian(seeds[0], (TOKENS, D), 1.0, 6.0, ((0, 8),)),
        "norm_gain": jnp.clip(1.0 + 0.1 * jax.random.normal(seeds[1], (D,), jnp.float32), 0.5, 1.5),
        "w_z": gaussian(seeds[2], (D, DI), D ** -0.5, 0.15625, ((0, 4), (1, 4))),
        "w_x": gaussian(seeds[3], (D, DI), D ** -0.5, 0.15625, ((0, 4), (1, 4))),
        "w_bc": gaussian(seeds[4], (D, 2 * STATE), D ** -0.5, 0.15625, ((0, 4),)),
        "w_dt": gaussian(seeds[5], (D, HEADS), D ** -0.5, 0.15625, ((0, 4), (1, 4))),
        "conv_x_weight": gaussian(seeds[6], (CONV, DI), CONV ** -0.5, 3.0, ((1, 4),), jnp.float32),
        "conv_x_bias": gaussian(seeds[7], (DI,), 0.3, 1.5, ((0, 4),), jnp.float32),
        "conv_bc_weight": gaussian(seeds[8], (CONV, 2 * STATE), CONV ** -0.5, 3.0, (), jnp.float32),
        "conv_bc_bias": gaussian(seeds[9], (2 * STATE,), 0.3, 1.5, (), jnp.float32),
        "dt_bias": jnp.clip(-4.0 + 3.0 * jax.random.uniform(seeds[10], (HEADS,), jnp.float32) ** steps_of(seeds[10], (HEADS,), ((0, 4),), -0.2, 0.2), -4.0, -1.0),
        "a_log": jnp.clip(-9.0 + 9.0 * jax.random.uniform(seeds[11], (HEADS,), jnp.float32) ** steps_of(seeds[11], (HEADS,), ((0, 4),), -0.2, 0.2), -9.0, 0.0),
        "d_skip": jnp.clip(0.5 + 1.0 * jax.random.uniform(seeds[12], (HEADS,), jnp.float32) ** steps_of(seeds[12], (HEADS,), ((0, 4),), -0.2, 0.2), 0.5, 1.5),
        "gate_gain": jnp.clip(1.0 + 0.1 * jax.random.normal(seeds[13], (DI,), jnp.float32), 0.5, 1.5),
        "w_out": gaussian(seeds[14], (DI, D), DI ** -0.5, 0.109375, ((0, 4), (1, 4))),
        "out_cotangent": gaussian(seeds[15], (TOKENS, D), 1.0, 6.0, ((0, 8),)),
    }


epsilon = 1e-05
precise = lax.Precision.HIGHEST

def silu_slope(value):
    sigma = jax.nn.sigmoid(value)
    return sigma * (1.0 + value * (1.0 - sigma))

def group_states(x_conv, step_size, decay_rate, b_mat, span):
    length, heads, width = x_conv.shape
    count = length // span
    log_step = (-step_size * decay_rate[None, :]).reshape(count, span, heads)
    cum_log = jnp.cumsum(log_step, axis=1)
    x_step = (x_conv * step_size[:, :, None]).reshape(count, span, heads, width)
    tail = jnp.exp(cum_log[:, -1:, :] - cum_log)
    states = jnp.einsum('cqhp,cqn->chpn', x_step * tail[:, :, :, None], b_mat.reshape(count, span, -1), precision=precise)
    return (cum_log, x_step, states)

def summarize(cum_log, states):
    totals = cum_log[:, -1, :]

    def advance(carry, item):
        total, state = item
        return (jnp.exp(total)[:, None, None] * carry + state, carry)
    final, enter = lax.scan(advance, jnp.zeros(states.shape[1:], jnp.float32), (totals, states))
    return (enter, lax.optimization_barrier(jnp.sum(totals, axis=0)), final)

def entry_scale(cum_log):
    totals = cum_log[:, -1, :]
    return jnp.exp(jnp.cumsum(totals, axis=0) - totals)

def group_output(cum_log, x_step, b_mat, c_mat, enter):
    count, span, heads, width = x_step.shape
    b_view = b_mat.reshape(count, span, -1)
    c_view = c_mat.reshape(count, span, -1)
    scores = jnp.einsum('ctn,csn->cts', c_view, b_view, precision=precise)
    cum_heads = jnp.transpose(cum_log, (0, 2, 1))
    gaps = cum_heads[:, :, :, None] - cum_heads[:, :, None, :]
    lower = jnp.arange(span)[:, None] >= jnp.arange(span)[None, :]
    decay = jnp.where(lower, jnp.exp(jnp.minimum(gaps, 0.0)), 0.0)
    inner = jnp.einsum('chts,cshp->cthp', decay * scores[:, None], x_step, precision=precise)
    outer = jnp.einsum('ctn,chpn->cthp', c_view, enter, precision=precise) * jnp.exp(cum_log)[:, :, :, None]
    return (inner + outer).reshape(count * span, heads, width)

def ssd_local(x_conv, step_size, decay_rate, b_mat, c_mat, s_in):
    span = min(GROUP, x_conv.shape[0])
    cum_log, x_step, states = group_states(x_conv, step_size, decay_rate, b_mat, span)
    enter, log_decay, s_local = summarize(cum_log, states)
    before = entry_scale(cum_log)
    enter = enter + before[:, :, None, None] * s_in[None]
    return (group_output(cum_log, x_step, b_mat, c_mat, enter), log_decay, s_local)

def conv_apply(padded, conv_weight, conv_bias, length):
    total = conv_bias[None, :] + conv_weight[0] * padded[0:length]
    for offset in range(1, CONV):
        total = total + conv_weight[offset] * padded[offset:offset + length]
    return total

def conv_transpose(grad_pre, conv_weight):
    total = jnp.pad(conv_weight[0] * grad_pre, ((0, CONV - 1), (0, 0)))
    for offset in range(1, CONV):
        total = total + jnp.pad(conv_weight[offset] * grad_pre, ((offset, CONV - 1 - offset), (0, 0)))
    return total

def sequence_pass(block_input, cotangent, params):
    norm_gain, w_z, w_x, w_bc, w_dt, conv_weight, conv_bias, dt_bias, a_log, d_skip, gate_gain, w_out = params
    length = block_input.shape[0]
    inner_width = HEADS * HEAD_DIM
    x_float = block_input.astype(jnp.float32)
    inverse = lax.rsqrt(lax.optimization_barrier(jnp.mean(x_float * x_float, axis=1, keepdims=True)) + epsilon)
    normed = (x_float * inverse * norm_gain).astype(jnp.bfloat16)
    z_part = jnp.dot(normed, w_z, preferred_element_type=jnp.float32)
    x_raw = jnp.dot(normed, w_x, preferred_element_type=jnp.float32).astype(jnp.bfloat16)
    bc_raw = jnp.dot(normed, w_bc, preferred_element_type=jnp.float32).astype(jnp.bfloat16)
    dt_raw = jnp.dot(normed, w_dt, preferred_element_type=jnp.float32)
    conv_in = jnp.concatenate([x_raw, bc_raw], axis=1).astype(jnp.float32)
    padded = jnp.concatenate([jnp.zeros((CONV - 1, conv_in.shape[1]), jnp.float32), conv_in], axis=0)
    pre = conv_apply(padded, conv_weight, conv_bias, length)
    act = jax.nn.silu(pre)
    x_conv = act[:, :inner_width].reshape(length, HEADS, HEAD_DIM)
    b_mat = act[:, inner_width:inner_width + STATE]
    c_mat = act[:, inner_width + STATE:]
    step_size = jax.nn.softplus(dt_raw + dt_bias)
    decay_rate = jnp.exp(a_log)
    zero_state = jnp.zeros((HEADS, HEAD_DIM, STATE), jnp.float32)
    (ssd_out, log_decay, s_local), pullback = jax.vjp(ssd_local, x_conv, step_size, decay_rate, b_mat, c_mat, zero_state)
    mixer = (ssd_out + d_skip[None, :, None] * x_conv).reshape(length, inner_width)
    gate_value = jax.nn.silu(z_part)
    gated = mixer * gate_value
    gate_inverse = lax.rsqrt(lax.optimization_barrier(jnp.mean(gated * gated, axis=1, keepdims=True)) + epsilon)
    gated_out = (gated * gate_inverse * gate_gain).astype(jnp.bfloat16)
    out_part = jnp.dot(gated_out, w_out, preferred_element_type=jnp.float32)
    block_output = (x_float + out_part).astype(jnp.bfloat16)
    grad_gated_out = jnp.dot(cotangent, w_out.T, preferred_element_type=jnp.float32)
    grad_w_out = jnp.dot(gated_out.T, cotangent, preferred_element_type=jnp.float32)
    scaled = gate_gain * grad_gated_out
    row_terms = lax.optimization_barrier(jnp.mean(scaled * gated, axis=1, keepdims=True))
    grad_gated = gate_inverse * scaled - gated * gate_inverse * gate_inverse * gate_inverse * row_terms
    grad_gate_gain = lax.optimization_barrier(jnp.sum(grad_gated_out * gated * gate_inverse, axis=0))
    grad_mixer = grad_gated * gate_value
    grad_z = (grad_gated * mixer * silu_slope(z_part)).astype(jnp.bfloat16)
    grad_heads = grad_mixer.reshape(length, HEADS, HEAD_DIM)
    grad_d_skip = lax.optimization_barrier(jnp.sum(grad_heads * x_conv, axis=(0, 2)))
    grad_xc, grad_step, grad_rate, grad_b, grad_c, unused = pullback((grad_heads, jnp.zeros_like(log_decay), jnp.zeros_like(s_local)))
    grad_xc = grad_xc + d_skip[None, :, None] * grad_heads
    grad_act = jnp.concatenate([grad_xc.reshape(length, inner_width), grad_b, grad_c], axis=1)
    grad_pre = grad_act * silu_slope(pre)
    grad_conv_bias = lax.optimization_barrier(jnp.sum(grad_pre, axis=0))
    grad_conv_weight = jnp.stack([lax.optimization_barrier(jnp.sum(grad_pre * padded[offset:offset + length], axis=0)) for offset in range(CONV)])
    grad_conv_in = conv_transpose(grad_pre, conv_weight)[CONV - 1:]
    grad_x_raw = grad_conv_in[:, :inner_width].astype(jnp.bfloat16)
    grad_bc_raw = grad_conv_in[:, inner_width:].astype(jnp.bfloat16)
    slope = jax.nn.sigmoid(dt_raw + dt_bias)
    grad_dt_bias = lax.optimization_barrier(jnp.sum(grad_step * slope, axis=0))
    grad_dt_raw = (grad_step * slope).astype(jnp.bfloat16)
    grad_a_log = grad_rate * decay_rate
    grad_normed = jnp.dot(grad_z, w_z.T, preferred_element_type=jnp.float32) + jnp.dot(grad_x_raw, w_x.T, preferred_element_type=jnp.float32) + jnp.dot(grad_bc_raw, w_bc.T, preferred_element_type=jnp.float32) + jnp.dot(grad_dt_raw, w_dt.T, preferred_element_type=jnp.float32)
    scaled_in = norm_gain * grad_normed
    input_grad = cotangent.astype(jnp.float32) + inverse * scaled_in - x_float * inverse * inverse * inverse * lax.optimization_barrier(jnp.mean(scaled_in * x_float, axis=1, keepdims=True))
    grad_norm_gain = lax.optimization_barrier(jnp.sum(grad_normed * x_float * inverse, axis=0))
    grad_w_z = jnp.dot(normed.T, grad_z, preferred_element_type=jnp.float32)
    grad_w_x = jnp.dot(normed.T, grad_x_raw, preferred_element_type=jnp.float32)
    grad_w_bc = jnp.dot(normed.T, grad_bc_raw, preferred_element_type=jnp.float32)
    grad_w_dt = jnp.dot(normed.T, grad_dt_raw, preferred_element_type=jnp.float32)
    grads = (grad_w_z, grad_w_x, grad_w_bc, grad_w_dt, grad_w_out, grad_norm_gain, grad_conv_weight, grad_conv_bias, grad_dt_bias, grad_a_log, grad_d_skip, grad_gate_gain)
    return (block_output, input_grad, grads)

def reference(block_input, norm_gain, w_z, w_x, w_bc, w_dt, conv_x_weight, conv_x_bias, conv_bc_weight, conv_bc_bias, dt_bias, a_log, d_skip, gate_gain, w_out, out_cotangent):
    conv_weight = jnp.concatenate([conv_x_weight, conv_bc_weight], axis=1)
    conv_bias = jnp.concatenate([conv_x_bias, conv_bc_bias])
    params = (norm_gain, w_z, w_x, w_bc, w_dt, conv_weight, conv_bias, dt_bias, a_log, d_skip, gate_gain, w_out)
    inputs = block_input.reshape(N_SHARD, SEQ_LEN, D)
    cotangents = out_cotangent.reshape(N_SHARD, SEQ_LEN, D)
    inner_width = HEADS * HEAD_DIM
    start = (jnp.zeros((D, inner_width), jnp.float32), jnp.zeros((D, inner_width), jnp.float32), jnp.zeros((D, 2 * STATE), jnp.float32), jnp.zeros((D, HEADS), jnp.float32), jnp.zeros((inner_width, D), jnp.float32), jnp.zeros((D,), jnp.float32), jnp.zeros((CONV, inner_width + 2 * STATE), jnp.float32), jnp.zeros((inner_width + 2 * STATE,), jnp.float32), jnp.zeros((HEADS,), jnp.float32), jnp.zeros((HEADS,), jnp.float32), jnp.zeros((HEADS,), jnp.float32), jnp.zeros((inner_width,), jnp.float32))

    def visit(totals, item):
        output, input_grad, grads = sequence_pass(item[0], item[1], params)
        return (jax.tree.map(lambda left, right: left + right, totals, grads), (output, input_grad))
    totals, (outputs, input_grads) = lax.scan(visit, start, (inputs, cotangents))
    grad_w_z, grad_w_x, grad_w_bc, grad_w_dt, grad_w_out, grad_norm_gain, grad_conv_weight, grad_conv_bias, grad_dt_bias, grad_a_log, grad_d_skip, grad_gate_gain = totals
    return (outputs.reshape(TOKENS, D), input_grads.reshape(TOKENS, D), grad_w_z, grad_w_x, grad_w_bc, grad_w_dt, grad_w_out, grad_norm_gain, grad_conv_weight[:, :inner_width], grad_conv_bias[:inner_width], grad_conv_weight[:, inner_width:], grad_conv_bias[inner_width:], grad_dt_bias, grad_a_log, grad_d_skip, grad_gate_gain)
```

```python
import functools

import jax
import jax.numpy as jnp
from jax import lax
from jax.experimental import pallas as pl
from jax.experimental.pallas import tpu as pltpu
from jax.sharding import PartitionSpec as P

HEADS = 48
HEAD_DIM = 64
STATE = 128
CONV = 4
SPAN = 128
LANES = 128

epsilon = 1e-05
f32 = jnp.float32
bf16 = jnp.bfloat16


def split(v):
    hi = v.astype(bf16)
    return hi, (v - hi.astype(f32)).astype(bf16)


def dot(a, b):
    return lax.dot_general(a, b, (((1,), (0,)), ((), ())), preferred_element_type=f32)


def dot_t(a, b):
    return lax.dot_general(a, b, (((1,), (1,)), ((), ())), preferred_element_type=f32)


def lhs3(parts):
    hi, lo = parts
    return jnp.concatenate([hi, lo, hi], axis=1)


def rhs3(parts):
    hi, lo = parts
    return jnp.concatenate([hi, hi, lo], axis=0)


def rhs3_t(parts):
    hi, lo = parts
    return jnp.concatenate([hi, hi, lo], axis=1)


def spread(values, spread_mat):
    hi, lo = split(values)
    return dot(jnp.concatenate([hi, lo], axis=1), spread_mat)


def gather_heads(values, gather_mat):
    hi, lo = split(values)
    return dot(jnp.concatenate([hi, lo], axis=1), gather_mat)


def tri_sum(tri2, values):
    hi, lo = split(values)
    return dot(tri2, jnp.concatenate([hi, lo], axis=0))


def sigmoid(v):
    return 1.0 / (1.0 + jnp.exp(-v))


def slope_of(v, sigma):
    return sigma * (1.0 + v * (1.0 - sigma))


def front_kernel(x_ref, bc_ref, edge_ref, cw_ref, cb_ref, step_ref, rate_ref, spread_ref, tri_ref,
                 pre_ref, act_ref, cum_ref, state_ref, total_ref, ext, state):
    c = pl.program_id(0)
    rows, inner = x_ref.shape
    wide = cw_ref.shape[1]

    @pl.when(c == 0)
    def _():
        ext[0:8, :] = edge_ref[...]
        state[...] = jnp.zeros_like(state)
        total_ref[...] = jnp.zeros_like(total_ref)

    ext[8 : 8 + rows, 0:inner] = x_ref[...].astype(f32)
    ext[8 : 8 + rows, inner:wide] = bc_ref[...].astype(f32)
    pre = cb_ref[...] + cw_ref[0:1, :] * ext[5 : 5 + rows, :]
    for k in range(1, CONV):
        pre = pre + cw_ref[k : k + 1, :] * ext[5 + k : 5 + k + rows, :]
    ext[0:8, :] = ext[rows : rows + 8, :]
    act = pre * sigmoid(pre)
    pre_ref[...] = pre
    act_ref[...] = act
    step = step_ref[...]
    cum = tri_sum(tri_ref[...], -step * rate_ref[...])
    cum_ref[...] = cum
    total = cum[rows - 1 : rows, :]
    b_t = jnp.transpose(act[:, inner : inner + STATE])
    weight = spread(step * jnp.exp(total - cum), spread_ref[...])
    decay = spread(jnp.broadcast_to(jnp.exp(total), (8, LANES)), spread_ref[...])[0:1, :]
    new = decay * state[...] + dot(lhs3(split(b_t)), rhs3(split(act[:, 0:inner] * weight)))
    state[...] = new
    state_ref[...] = new
    total_ref[...] = total_ref[...] + jnp.broadcast_to(total, (8, LANES))


def forward_kernel(act_ref, step_ref, cum_ref, z_ref, ggo_ref, s_in_ref, d_ref, gain_ref, spread_ref,
                   mixer_ref, enter_ref, exit_ref, sums_ref, state):
    c = pl.program_id(0)
    rows, inner = z_ref.shape

    @pl.when(c == 0)
    def _():
        state[...] = s_in_ref[...]

    heads = inner // HEAD_DIM
    per = LANES // HEAD_DIM
    spread_mat = spread_ref[...]
    x = act_ref[:, 0:inner]
    b_mat = act_ref[:, inner : inner + STATE]
    c_mat = act_ref[:, inner + STATE : inner + 2 * STATE]
    step = step_ref[...]
    cum = cum_ref[...]
    cum_t = jnp.transpose(cum)
    total = cum[rows - 1 : rows, :]
    wide = spread(
        jnp.concatenate([step, step * jnp.exp(total - cum), jnp.exp(cum)], axis=0), spread_mat
    )
    decay = spread(jnp.broadcast_to(jnp.exp(total), (8, LANES)), spread_mat)[0:1, :]
    x_step = x * wide[0:rows]
    c3 = lhs3(split(c_mat))
    scores = dot_t(c3, rhs3_t(split(b_mat)))
    enter = state[...]
    enter_ref[...] = enter
    outer = dot(c3, rhs3(split(enter))) * wide[2 * rows : 3 * rows]
    lower = lax.broadcasted_iota(jnp.int32, (rows, rows), 0) >= lax.broadcasted_iota(
        jnp.int32, (rows, rows), 1
    )
    lane = lax.broadcasted_iota(jnp.int32, (rows, LANES), 1)
    masked = jnp.where(lower, scores, 0.0)
    tiles = []
    for tile in range(heads // per):
        value = rhs3(split(x_step[:, tile * LANES : (tile + 1) * LANES]))
        got = None
        for j in range(per):
            h = tile * per + j
            gap = cum[:, h : h + 1] - cum_t[h : h + 1, :]
            part = dot(lhs3(split(jnp.exp(jnp.minimum(gap, 0.0)) * masked)), value)
            got = part if got is None else jnp.where(lane >= j * HEAD_DIM, part, got)
        tiles.append(got)
    inner_out = jnp.concatenate(tiles, axis=1)
    mixer = inner_out + outer + d_ref[...] * x
    mixer_ref[...] = mixer
    b_t = jnp.transpose(b_mat)
    new = decay * enter + dot(lhs3(split(b_t)), rhs3(split(x * wide[rows : 2 * rows])))
    state[...] = new
    exit_ref[...] = new
    z = z_ref[...]
    gated = mixer * (z * sigmoid(z))
    square = jnp.sum(gated * gated, axis=1, keepdims=True)
    term = jnp.sum(gain_ref[...] * ggo_ref[...] * gated, axis=1, keepdims=True)
    both = jnp.where(lane == 0, square, term)
    sums_ref[...] = jnp.transpose(both)[0:8, :]


def gate_kernel(inner_width, mixer_ref, z_ref, ggo_ref, sums_ref, act_ref, cum_ref, gain_ref, spread_ref,
                out_ref, gm_ref, gz_ref, own_ref, acc_ref, state):
    c = pl.program_id(0)
    rows, inner = z_ref.shape

    @pl.when(c == 0)
    def _():
        state[...] = jnp.zeros_like(state)
        acc_ref[...] = jnp.zeros_like(acc_ref)

    spread_mat = spread_ref[...]
    columns = jnp.transpose(jnp.concatenate([sums_ref[...]] * (LANES // 8), axis=0))
    inverse = lax.rsqrt(columns[:, 0:1] / inner_width + epsilon)
    term = columns[:, 1:2] / inner_width
    mixer = mixer_ref[...]
    z = z_ref[...]
    sigma = sigmoid(z)
    gate = z * sigma
    gated = mixer * gate
    ggo = ggo_ref[...]
    normal = gated * inverse
    out_ref[...] = (normal * gain_ref[...]).astype(bf16)
    grad_gated = inverse * (gain_ref[...] * ggo) - normal * (inverse * inverse * term)
    gm = grad_gated * gate
    gm_ref[...] = gm
    gz_ref[...] = (grad_gated * mixer * slope_of(z, sigma)).astype(bf16)
    x = act_ref[:, 0:inner]
    c_mat = act_ref[:, inner + STATE : inner + 2 * STATE]
    acc_ref[0:1, :] += jnp.sum(ggo * normal, axis=0, keepdims=True)
    acc_ref[1:2, :] += jnp.sum(gm * x, axis=0, keepdims=True)
    cum = cum_ref[...]
    total = cum[rows - 1 : rows, :]
    grown = spread(jnp.exp(cum), spread_mat)
    decay = spread(jnp.broadcast_to(jnp.exp(total), (8, LANES)), spread_mat)[0:1, :]
    new = decay * state[...] + dot(
        lhs3(split(jnp.transpose(c_mat))), rhs3(split(gm * grown))
    )
    state[...] = new
    own_ref[...] = new


def backward_kernel(gm_ref, act_ref, pre_ref, step_ref, cum_ref, mixer_ref, enter_ref, exit_ref, carried_ref,
                    x_raw_ref, cw_ref, d_ref, rate_ref, spread_ref, gather_ref, upper_ref,
                    gx_ref, tail_ref, head_ref, dbc_ref, gstep_ref, conv_ref, rate_out_ref,
                    state, ext):
    c = pl.program_id(0)
    rows, inner = gm_ref.shape

    @pl.when(c == 0)
    def _():
        state[...] = carried_ref[...]
        ext[rows : rows + 8, :] = jnp.zeros((8, inner), f32)
        conv_ref[...] = jnp.zeros_like(conv_ref)
        rate_out_ref[...] = jnp.zeros_like(rate_out_ref)

    heads = inner // HEAD_DIM
    per = LANES // HEAD_DIM
    spread_mat = spread_ref[...]
    gather_mat = gather_ref[...]
    gm = gm_ref[...]
    x = act_ref[:, 0:inner]
    b_mat = act_ref[:, inner : inner + STATE]
    c_mat = act_ref[:, inner + STATE : inner + 2 * STATE]
    step = step_ref[...]
    cum = cum_ref[...]
    cum_t = jnp.transpose(cum)
    total = cum[rows - 1 : rows, :]
    wide = spread(
        jnp.concatenate([step, jnp.exp(total - cum), jnp.exp(cum)], axis=0), spread_mat
    )
    step_wide, tail_wide, grown = wide[0:rows], wide[rows : 2 * rows], wide[2 * rows : 3 * rows]
    decay = spread(jnp.broadcast_to(jnp.exp(total), (8, LANES)), spread_mat)[0:1, :]
    x_step = x * step_wide
    b_parts, c_parts = split(b_mat), split(c_mat)
    b3 = lhs3(b_parts)
    scores_t = dot_t(b3, rhs3_t(c_parts))
    grad_exit = state[...]
    exit_parts = split(grad_exit)
    upper = lax.broadcasted_iota(jnp.int32, (rows, rows), 1) >= lax.broadcasted_iota(
        jnp.int32, (rows, rows), 0
    )
    lane = lax.broadcasted_iota(jnp.int32, (rows, LANES), 1)
    through = dot(b3, rhs3(exit_parts)) * tail_wide
    gm_hi, gm_lo = split(gm)
    xs_hi, xs_lo = split(x_step)
    tiles = []
    grad_scores = jnp.zeros((rows, rows), f32)
    zero = jnp.zeros((rows, LANES), bf16)
    for tile in range(heads // per):
        cut = slice(tile * LANES, (tile + 1) * LANES)
        g_hi, g_lo = gm_hi[:, cut], gm_lo[:, cut]
        g_rows = jnp.concatenate([g_hi, g_hi, g_lo], axis=0)
        g_lanes = jnp.concatenate([g_hi, g_hi, g_lo], axis=1)
        got = None
        for j in range(per):
            h = tile * per + j
            keep = (lane >= j * HEAD_DIM) & (lane < (j + 1) * HEAD_DIM)
            xh = jnp.where(keep, xs_hi[:, cut], zero)
            xl = jnp.where(keep, xs_lo[:, cut], zero)
            gap = cum_t[h : h + 1, :] - cum[:, h : h + 1]
            span = jnp.where(upper, jnp.exp(jnp.minimum(gap, 0.0)), 0.0)
            pairs = dot_t(jnp.concatenate([xh, xl, xh], axis=1), g_lanes)
            grad_scores = grad_scores + span * pairs
            part = dot(lhs3(split(span * scores_t)), g_rows)
            got = part if got is None else jnp.where(lane >= j * HEAD_DIM, part, got)
        tiles.append(got)
    grad_xs = jnp.concatenate(tiles, axis=1) + through
    scores_parts = split(grad_scores)
    weighted = gm * grown
    weighted_parts = split(weighted)
    enter_parts = split(enter_ref[...])
    grad_b = dot(lhs3(scores_parts), rhs3(c_parts)) + dot_t(
        lhs3(split(x_step * tail_wide)), rhs3_t(exit_parts)
    )
    grad_c = dot(lhs3(split(jnp.transpose(grad_scores))), rhs3(b_parts)) + dot_t(
        lhs3(weighted_parts), rhs3_t(enter_parts)
    )
    dbc_ref[:, 0:STATE] = grad_b
    dbc_ref[:, STATE : 2 * STATE] = grad_c
    lost = jnp.sum(grad_exit * exit_ref[...], axis=0, keepdims=True)
    state[...] = decay * grad_exit + dot(
        lhs3(split(jnp.transpose(c_mat))), rhs3(weighted_parts)
    )
    ssd = mixer_ref[...] - d_ref[...] * x
    heads_sum = gather_heads(
        jnp.concatenate([gm * ssd, x * grad_xs, jnp.broadcast_to(lost, (8, inner))], axis=0), gather_mat
    )
    by_step = heads_sum[rows : 2 * rows]
    grad_log = tri_sum(upper_ref[...], heads_sum[0:rows] - step * by_step) + heads_sum[
        2 * rows : 2 * rows + 1
    ]
    gstep_ref[...] = by_step - rate_ref[...] * grad_log
    rate_out_ref[0:1, :] += -jnp.sum(grad_log * step, axis=0, keepdims=True)
    pre = pre_ref[...]
    grad_pre = (grad_xs * step_wide + d_ref[...] * gm) * slope_of(pre, sigmoid(pre))
    ext[0:rows, :] = grad_pre
    raw = x_raw_ref[...].astype(f32)
    conv_ref[CONV : CONV + 1, :] += jnp.sum(grad_pre, axis=0, keepdims=True)
    total_in = None
    for k in range(CONV):
        moved = ext[CONV - 1 - k : CONV - 1 - k + rows, :]
        conv_ref[k : k + 1, :] += jnp.sum(moved * raw, axis=0, keepdims=True)
        piece = cw_ref[k : k + 1, :] * moved
        total_in = piece if total_in is None else total_in + piece
    gx_ref[...] = total_in.astype(bf16)

    @pl.when(c == 0)
    def _():
        tail_ref[...] = total_in[rows - 8 : rows, :]

    head_ref[...] = grad_pre[0:8, :]
    ext[rows : rows + 8, :] = grad_pre[0:8, :]


def shifted(value, axis, by):
    length = lax.axis_size(axis)
    pairs = [(i, i + by) for i in range(length) if 0 <= i + by < length]
    return lax.ppermute(value, axis, pairs)


def rotated(value, axis, by):
    length = lax.axis_size(axis)
    return lax.ppermute(value, axis, [(i, (i + by) % length) for i in range(length)])


def chain(local, decay, axis, by):
    got = None
    for _ in range(lax.axis_size(axis) - 1):
        got = shifted(local if got is None else local + decay * got, axis, by)
    return jnp.zeros_like(local) if got is None else got


def row_block(shape, index):
    return pl.BlockSpec(shape, index)


def shards(
    block_input,
    norm_gain,
    w_z,
    w_x,
    w_bc,
    w_dt,
    conv_x_weight,
    conv_x_bias,
    conv_bc_weight,
    conv_bc_bias,
    dt_bias,
    a_log,
    d_skip,
    gate_gain,
    w_out,
    out_cotangent,
):
    length, width = block_input.shape
    inner = w_z.shape[1]
    heads = w_dt.shape[1]
    wide = inner + 2 * STATE
    inner_width = HEADS * HEAD_DIM
    ranks = lax.axis_size("tensor")
    me = lax.axis_index("tensor")
    quarter = length // ranks
    rows = min(SPAN, length)
    count = length // rows

    w_cat = jnp.concatenate([w_x, jnp.pad(w_dt, ((0, 0), (0, LANES - heads))), w_bc], axis=1)
    full_cat = lax.all_gather(w_cat, "shard", axis=0, tiled=True)
    full_z = lax.all_gather(w_z, "shard", axis=0, tiled=True)
    full_out = lax.all_gather(w_out, "shard", axis=1, tiled=True)

    x_float = block_input.astype(f32)
    inverse = lax.rsqrt(jnp.mean(x_float * x_float, axis=1, keepdims=True) + epsilon)
    normed = (x_float * inverse * norm_gain).astype(bf16)
    proj = jnp.dot(normed, full_cat, preferred_element_type=f32)
    x_raw = proj[:, :inner].astype(bf16)
    dt_raw = proj[:, inner : inner + LANES]
    bc_raw = proj[:, inner + LANES :].astype(bf16)
    z_part = jnp.dot(normed, full_z, preferred_element_type=f32)

    edge = shifted(
        jnp.concatenate([x_raw[length - CONV + 1 :], bc_raw[length - CONV + 1 :]], axis=1), "context", 1
    ).astype(f32)
    edge = jnp.pad(edge, ((8 - CONV + 1, 0), (0, 0)))
    conv_weight = jnp.concatenate([conv_x_weight, conv_bc_weight], axis=1)
    conv_bias = jnp.concatenate([conv_x_bias, conv_bc_bias])[None, :]
    dt_in = dt_raw + jnp.pad(dt_bias, (0, LANES - heads))
    step = jax.nn.softplus(dt_in)
    decay_rate = jnp.exp(a_log)
    rate_row = jnp.pad(decay_rate, (0, LANES - heads))[None, :]
    d_row = jnp.repeat(d_skip, HEAD_DIM)[None, :]
    gain_row = gate_gain[None, :]
    owner = jnp.arange(inner) // HEAD_DIM
    one_hot = (jnp.arange(LANES)[:, None] == owner[None, :]).astype(bf16)
    spread_mat = jnp.concatenate([one_hot, one_hot], axis=0)
    one_hot_t = (owner[:, None] == jnp.arange(LANES)[None, :]).astype(bf16)
    gather_mat = jnp.concatenate([one_hot_t, one_hot_t], axis=0)
    place = jnp.arange(rows)
    lower = (place[:, None] >= place[None, :]).astype(bf16)
    lower2 = jnp.concatenate([lower, lower], axis=1)
    upper = (place[:, None] <= place[None, :]).astype(bf16)
    upper2 = jnp.concatenate([upper, upper], axis=1)

    def whole(shape):
        return pl.BlockSpec(shape, lambda c: (0,) * len(shape))

    def ahead(lanes, high=rows):
        return pl.BlockSpec((high, lanes), lambda c: (c, 0))

    def back(lanes, high=rows):
        return pl.BlockSpec((high, lanes), lambda c: (count - 1 - c, 0))

    def shape(*dims, dtype=f32):
        return jax.ShapeDtypeStruct(dims, dtype)

    params = pltpu.CompilerParams(dimension_semantics=("arbitrary",))

    pre, act, cum, s_local, totals = pl.pallas_call(
        front_kernel,
        grid=(count,),
        in_specs=[
            ahead(inner), ahead(2 * STATE), whole((8, wide)), whole((CONV, wide)), whole((1, wide)),
            ahead(LANES), whole((1, LANES)), whole((2 * LANES, inner)), whole((rows, 2 * rows)),
        ],
        out_specs=[ahead(wide), ahead(wide), ahead(LANES), whole((STATE, inner)), whole((8, LANES))],
        out_shape=[
            shape(length, wide), shape(length, wide), shape(length, LANES), shape(STATE, inner),
            shape(8, LANES),
        ],
        scratch_shapes=[pltpu.VMEM((rows + 8, wide), f32), pltpu.VMEM((STATE, inner), f32)],
        compiler_params=params,
        name="front",
    )(x_raw, bc_raw, edge, conv_weight, conv_bias, step, rate_row, spread_mat, lower2)
    decay = jnp.repeat(jnp.exp(totals[0, :heads]), HEAD_DIM)[None, :]
    s_in = chain(s_local, decay, "context", 1)

    ggo = jnp.einsum("td,kd->tk", out_cotangent, full_out, preferred_element_type=f32)
    mixer, enter, leave, sums = pl.pallas_call(
        forward_kernel,
        grid=(count,),
        in_specs=[
            ahead(wide), ahead(LANES), ahead(LANES), ahead(inner), ahead(inner), whole((STATE, inner)),
            whole((1, inner)), whole((1, inner)), whole((2 * LANES, inner)),
        ],
        out_specs=[
            ahead(inner), ahead(inner, STATE), ahead(inner, STATE), pl.BlockSpec((8, rows), lambda c: (0, c)),
        ],
        out_shape=[
            shape(length, inner), shape(count * STATE, inner), shape(count * STATE, inner), shape(8, length),
        ],
        scratch_shapes=[pltpu.VMEM((STATE, inner), f32)],
        compiler_params=params,
        name="forward",
    )(act, step, cum, z_part, ggo, s_in, d_row, gain_row, spread_mat)
    sums = lax.psum(sums, "tensor")

    gated_out, gm, grad_z, own, gate_acc = pl.pallas_call(
        functools.partial(gate_kernel, inner_width),
        grid=(count,),
        in_specs=[
            back(inner), back(inner), back(inner), pl.BlockSpec((8, rows), lambda c: (0, count - 1 - c)),
            back(wide), back(LANES), whole((1, inner)), whole((2 * LANES, inner)),
        ],
        out_specs=[back(inner), back(inner), back(inner), whole((STATE, inner)), whole((8, inner))],
        out_shape=[
            shape(length, inner, dtype=bf16), shape(length, inner), shape(length, inner, dtype=bf16),
            shape(STATE, inner), shape(8, inner),
        ],
        scratch_shapes=[pltpu.VMEM((STATE, inner), f32)],
        compiler_params=params,
        name="gate",
    )(mixer, z_part, ggo, sums, act, cum, gain_row, spread_mat)
    carried = chain(own, decay, "context", -1)

    def block(value, k):
        return lax.dynamic_slice_in_dim(value, ((me + k) % ranks) * quarter, quarter)

    out_own = jnp.dot(block(gated_out, 0), full_out, preferred_element_type=f32)
    for k in range(1, ranks):
        part = jnp.dot(block(gated_out, k), full_out, preferred_element_type=f32)
        out_own = out_own + rotated(part, "tensor", k)
    block_own = (block(block_input, 0).astype(f32) + out_own).astype(bf16)
    block_output = jnp.zeros((length, width), bf16)
    for k in range(ranks):
        piece = block_own if k == 0 else rotated(block_own, "tensor", k)
        block_output = lax.dynamic_update_slice_in_dim(
            block_output, piece, ((me - k) % ranks) * quarter, 0
        )
    grad_w_out = jnp.einsum("tk,td->kd", gated_out, out_cotangent, preferred_element_type=f32)
    summed_out = lax.psum_scatter(grad_w_out, ("shard", "context"), scatter_dimension=1, tiled=True)
    grad_w_z = jnp.einsum("td,tk->dk", normed, grad_z, preferred_element_type=f32)
    summed_z = lax.psum_scatter(grad_w_z, ("shard", "context"), scatter_dimension=0, tiled=True)

    gx, gx_tail, pre_head, dbc, gstep, conv_acc, rate_acc = pl.pallas_call(
        backward_kernel,
        grid=(count,),
        in_specs=[
            back(inner), back(wide), back(inner), back(LANES), back(LANES), back(inner),
            back(inner, STATE), back(inner, STATE), whole((STATE, inner)), back(inner), whole((CONV, inner)),
            whole((1, inner)), whole((1, LANES)), whole((2 * LANES, inner)), whole((2 * inner, LANES)),
            whole((rows, 2 * rows)),
        ],
        out_specs=[
            back(inner), whole((8, inner)), whole((8, inner)), back(2 * STATE), back(LANES), whole((8, inner)),
            whole((8, LANES)),
        ],
        out_shape=[
            shape(length, inner, dtype=bf16), shape(8, inner), shape(8, inner), shape(length, 2 * STATE),
            shape(length, LANES), shape(8, inner), shape(8, LANES),
        ],
        scratch_shapes=[pltpu.VMEM((STATE, inner), f32), pltpu.VMEM((rows + 8, inner), f32)],
        compiler_params=params,
        name="backward",
    )(gm, act, pre, step, cum, mixer, enter, leave, carried, x_raw, conv_x_weight, d_row, rate_row,
      spread_mat, gather_mat, upper2)

    dbc = lax.psum(dbc, "tensor")
    pre_bc = pre[:, inner:]
    grad_pre_bc = dbc * slope_of(pre_bc, jax.nn.sigmoid(pre_bc))
    next_head = shifted(
        jnp.concatenate([pre_head[: CONV - 1], grad_pre_bc[: CONV - 1]], axis=1), "context", -1
    )
    after = jnp.pad(next_head, ((CONV - 1, CONV - 1), (0, 0)))
    reach = jnp.zeros((CONV - 1, wide), f32)
    for k in range(CONV):
        reach = reach + conv_weight[k] * after[CONV - 1 - k : 2 * (CONV - 1) - k]
    gx_last = (gx_tail + jnp.pad(reach[:, :inner], ((8 - CONV + 1, 0), (0, 0)))).astype(bf16)
    gx = lax.dynamic_update_slice_in_dim(gx, gx_last, length - 8, 0)
    bc_pad = jnp.concatenate([grad_pre_bc, next_head[:, inner:]], axis=0)
    gbc = jnp.zeros((length, 2 * STATE), f32)
    for k in range(CONV):
        gbc = gbc + conv_bc_weight[k] * bc_pad[CONV - 1 - k : CONV - 1 - k + length]
    gbc = gbc.astype(bf16)
    head_pad = jnp.pad(pre_head[: CONV - 1], ((CONV - 1, CONV - 1), (0, 0)))
    entering = edge[8 - CONV + 1 :]
    extra = jnp.stack([
        jnp.sum(entering[:, :inner] * head_pad[CONV - 1 - k : 2 * (CONV - 1) - k], axis=0)
        for k in range(CONV)
    ])
    bc_in = jnp.concatenate([entering[:, inner:], bc_raw.astype(f32)], axis=0)
    grad_conv_bc = jnp.stack([jnp.sum(grad_pre_bc * bc_in[k : k + length], axis=0) for k in range(CONV)])
    grad_conv_bc_bias = jnp.sum(grad_pre_bc, axis=0)

    sigma = jax.nn.sigmoid(dt_in)
    g_dt = gstep * sigma
    grad_dt_bias = jnp.sum(g_dt, axis=0)
    g_dt = g_dt.astype(bf16)
    grad_a_log = rate_acc[0] * rate_row[0]

    g_xdt = jnp.concatenate([gx, g_dt], axis=1)
    full_xdt = full_cat[:, : inner + LANES]

    def partial_of(k):
        return jnp.einsum("tk,dk->td", block(grad_z, k), full_z, preferred_element_type=f32) + jnp.einsum(
            "tk,dk->td", block(g_xdt, k), full_xdt, preferred_element_type=f32
        )

    received = [rotated(partial_of(k).astype(bf16), "tensor", k) for k in range(1, ranks)]
    gn = partial_of(0) + jnp.einsum(
        "tk,dk->td", block(gbc, 0), full_cat[:, inner + LANES :], preferred_element_type=f32
    )
    for piece in received:
        gn = gn + piece.astype(f32)
    x_own, inv_own = block(x_float, 0), block(inverse, 0)
    scaled = norm_gain * gn
    delta = inv_own * scaled - x_own * (inv_own * inv_own * inv_own) * jnp.mean(
        scaled * x_own, axis=1, keepdims=True
    )
    delta = delta.astype(bf16)
    grad_norm_gain = jnp.sum(gn * x_own * inv_own, axis=0)
    input_grad = jnp.zeros((length, width), f32)
    for k in range(ranks):
        piece = delta if k == 0 else rotated(delta, "tensor", k)
        input_grad = lax.dynamic_update_slice_in_dim(
            input_grad,
            block(out_cotangent, -k).astype(f32) + piece.astype(f32),
            ((me - k) % ranks) * quarter,
            0,
        )

    g_cat = jnp.concatenate([g_xdt, gbc], axis=1)
    grad_w_cat = jnp.einsum("td,tk->dk", normed, g_cat, preferred_element_type=f32)
    summed_cat = lax.psum_scatter(grad_w_cat, ("shard", "context"), scatter_dimension=0, tiled=True)

    last = jnp.pad(jnp.concatenate([grad_dt_bias[:LANES], grad_a_log]), (0, inner - 2 * LANES))[None, :]
    packed = jnp.concatenate(
        [
            jnp.concatenate([conv_acc[:CONV] + extra, conv_acc[CONV : CONV + 1], gate_acc[:2], last], axis=0),
            jnp.concatenate(
                [grad_conv_bc, grad_conv_bc_bias[None, :], jnp.zeros((3, 2 * STATE), f32)], axis=0
            ),
        ],
        axis=1,
    )
    packed = lax.psum(packed, ("shard", "context"))
    sum_norm_gain = lax.psum(grad_norm_gain, ("shard", "context", "tensor"))
    return (
        block_output,
        input_grad,
        summed_z,
        summed_cat[:, :inner],
        summed_cat[:, inner + LANES :],
        summed_cat[:, inner : inner + heads],
        summed_out,
        sum_norm_gain,
        packed[:CONV, :inner],
        packed[CONV, :inner],
        packed[:CONV, inner:],
        packed[CONV, inner:],
        packed[7, :heads],
        packed[7, LANES : LANES + heads],
        jnp.sum(packed[6, :inner].reshape(heads, HEAD_DIM), axis=1),
        packed[5, :inner],
    )


def solution(mesh):
    in_specs = (
        P(("shard", "context"), None),
        P(),
        P("shard", "tensor"),
        P("shard", "tensor"),
        P("shard", None),
        P("shard", "tensor"),
        P(None, "tensor"),
        P("tensor"),
        P(),
        P(),
        P("tensor"),
        P("tensor"),
        P("tensor"),
        P("tensor"),
        P("tensor", "shard"),
        P(("shard", "context"), None),
    )
    out_specs = (
        P(("shard", "context"), None),
        P(("shard", "context"), None),
        P(("shard", "context"), "tensor"),
        P(("shard", "context"), "tensor"),
        P(("shard", "context"), None),
        P(("shard", "context"), "tensor"),
        P("tensor", ("shard", "context")),
        P(),
        P(None, "tensor"),
        P("tensor"),
        P(),
        P(),
        P("tensor"),
        P("tensor"),
        P("tensor"),
        P("tensor"),
    )
    return jax.shard_map(shards, mesh=mesh, in_specs=in_specs, out_specs=out_specs, check_vma=False)
```

```python
import functools

import jax
import jax.numpy as jnp
from jax import lax
from jax.experimental import pallas as pl
from jax.experimental.pallas import tpu as pltpu
from jax.sharding import PartitionSpec as P


HEADS = 48
HEAD_DIM = 64
STATE = 128
CONV = 4
SPAN = 128
LANES = 128

epsilon = 1e-05
f32 = jnp.float32
bf16 = jnp.bfloat16


def split(v):
    hi = v.astype(bf16)
    return hi, (v - hi.astype(f32)).astype(bf16)


def dot(a, b):
    return lax.dot_general(a, b, (((1,), (0,)), ((), ())), preferred_element_type=f32)


def dot_t(a, b):
    return lax.dot_general(a, b, (((1,), (1,)), ((), ())), preferred_element_type=f32)


def lhs3(parts):
    hi, lo = parts
    return jnp.concatenate([hi, lo, hi], axis=1)


def rhs3(parts):
    hi, lo = parts
    return jnp.concatenate([hi, hi, lo], axis=0)


def rhs3_t(parts):
    hi, lo = parts
    return jnp.concatenate([hi, hi, lo], axis=1)


def spread(values, spread_mat):
    hi, lo = split(values)
    return dot(jnp.concatenate([hi, lo], axis=1), spread_mat)


def gather_heads(values, gather_mat):
    hi, lo = split(values)
    return dot(jnp.concatenate([hi, lo], axis=1), gather_mat)


def tri_sum(tri2, values):
    hi, lo = split(values)
    return dot(tri2, jnp.concatenate([hi, lo], axis=0))


def sigmoid(v):
    return 1.0 / (1.0 + jnp.exp(-v))


def slope_of(v, sigma):
    return sigma * (1.0 + v * (1.0 - sigma))


def front_kernel(x_ref, bc_ref, edge_ref, cw_ref, cb_ref, step_ref, rate_ref, spread_ref, tri_ref,
                 pre_ref, act_ref, cum_ref, state_ref, total_ref, ext, state):
    c = pl.program_id(0)
    rows, inner = x_ref.shape
    wide = cw_ref.shape[1]

    @pl.when(c == 0)
    def _():
        ext[0:8, :] = edge_ref[...]
        state[...] = jnp.zeros_like(state)
        total_ref[...] = jnp.zeros_like(total_ref)

    ext[8 : 8 + rows, 0:inner] = x_ref[...].astype(f32)
    ext[8 : 8 + rows, inner:wide] = bc_ref[...].astype(f32)
    pre = cb_ref[...] + cw_ref[0:1, :] * ext[5 : 5 + rows, :]
    for k in range(1, CONV):
        pre = pre + cw_ref[k : k + 1, :] * ext[5 + k : 5 + k + rows, :]
    ext[0:8, :] = ext[rows : rows + 8, :]
    act = pre * sigmoid(pre)
    pre_ref[...] = pre
    act_ref[...] = act
    step = step_ref[...]
    cum = tri_sum(tri_ref[...], -step * rate_ref[...])
    cum_ref[...] = cum
    total = cum[rows - 1 : rows, :]
    b_t = jnp.transpose(act[:, inner : inner + STATE])
    weight = spread(step * jnp.exp(total - cum), spread_ref[...])
    decay = spread(jnp.broadcast_to(jnp.exp(total), (8, LANES)), spread_ref[...])[0:1, :]
    new = decay * state[...] + dot(lhs3(split(b_t)), rhs3(split(act[:, 0:inner] * weight)))
    state[...] = new
    state_ref[...] = new
    total_ref[...] = total_ref[...] + jnp.broadcast_to(total, (8, LANES))


def forward_kernel(act_ref, step_ref, cum_ref, z_ref, ggo_ref, s_in_ref, d_ref, gain_ref, spread_ref,
                   mixer_ref, enter_ref, exit_ref, sums_ref, state):
    c = pl.program_id(0)
    rows, inner = z_ref.shape

    @pl.when(c == 0)
    def _():
        state[...] = s_in_ref[...]

    heads = inner // HEAD_DIM
    per = LANES // HEAD_DIM
    spread_mat = spread_ref[...]
    x = act_ref[:, 0:inner]
    b_mat = act_ref[:, inner : inner + STATE]
    c_mat = act_ref[:, inner + STATE : inner + 2 * STATE]
    step = step_ref[...]
    cum = cum_ref[...]
    cum_t = jnp.transpose(cum)
    total = cum[rows - 1 : rows, :]
    wide = spread(
        jnp.concatenate([step, step * jnp.exp(total - cum), jnp.exp(cum)], axis=0), spread_mat
    )
    decay = spread(jnp.broadcast_to(jnp.exp(total), (8, LANES)), spread_mat)[0:1, :]
    x_step = x * wide[0:rows]
    c3 = lhs3(split(c_mat))
    scores = dot_t(c3, rhs3_t(split(b_mat)))
    enter = state[...]
    enter_ref[...] = enter
    outer = dot(c3, rhs3(split(enter))) * wide[2 * rows : 3 * rows]
    lower = lax.broadcasted_iota(jnp.int32, (rows, rows), 0) >= lax.broadcasted_iota(
        jnp.int32, (rows, rows), 1
    )
    lane = lax.broadcasted_iota(jnp.int32, (rows, LANES), 1)
    masked = jnp.where(lower, scores, 0.0)
    tiles = []
    for tile in range(heads // per):
        value = rhs3(split(x_step[:, tile * LANES : (tile + 1) * LANES]))
        got = None
        for j in range(per):
            h = tile * per + j
            gap = cum[:, h : h + 1] - cum_t[h : h + 1, :]
            part = dot(lhs3(split(jnp.exp(jnp.minimum(gap, 0.0)) * masked)), value)
            got = part if got is None else jnp.where(lane >= j * HEAD_DIM, part, got)
        tiles.append(got)
    inner_out = jnp.concatenate(tiles, axis=1)
    mixer = inner_out + outer + d_ref[...] * x
    mixer_ref[...] = mixer
    b_t = jnp.transpose(b_mat)
    new = decay * enter + dot(lhs3(split(b_t)), rhs3(split(x * wide[rows : 2 * rows])))
    state[...] = new
    exit_ref[...] = new
    z = z_ref[...]
    gated = mixer * (z * sigmoid(z))
    square = jnp.sum(gated * gated, axis=1, keepdims=True)
    term = jnp.sum(gain_ref[...] * ggo_ref[...] * gated, axis=1, keepdims=True)
    both = jnp.where(lane == 0, square, term)
    sums_ref[...] = jnp.transpose(both)[0:8, :]


def gate_kernel(inner_width, mixer_ref, z_ref, ggo_ref, sums_ref, act_ref, cum_ref, gain_ref, spread_ref,
                out_ref, gm_ref, gz_ref, own_ref, acc_ref, state):
    c = pl.program_id(0)
    rows, inner = z_ref.shape

    @pl.when(c == 0)
    def _():
        state[...] = jnp.zeros_like(state)
        acc_ref[...] = jnp.zeros_like(acc_ref)

    spread_mat = spread_ref[...]
    columns = jnp.transpose(jnp.concatenate([sums_ref[...]] * (LANES // 8), axis=0))
    inverse = lax.rsqrt(columns[:, 0:1] / inner_width + epsilon)
    term = columns[:, 1:2] / inner_width
    mixer = mixer_ref[...]
    z = z_ref[...]
    sigma = sigmoid(z)
    gate = z * sigma
    gated = mixer * gate
    ggo = ggo_ref[...]
    normal = gated * inverse
    out_ref[...] = (normal * gain_ref[...]).astype(bf16)
    grad_gated = inverse * (gain_ref[...] * ggo) - normal * (inverse * inverse * term)
    gm = grad_gated * gate
    gm_ref[...] = gm
    gz_ref[...] = (grad_gated * mixer * slope_of(z, sigma)).astype(bf16)
    x = act_ref[:, 0:inner]
    c_mat = act_ref[:, inner + STATE : inner + 2 * STATE]
    acc_ref[0:1, :] += jnp.sum(ggo * normal, axis=0, keepdims=True)
    acc_ref[1:2, :] += jnp.sum(gm * x, axis=0, keepdims=True)
    cum = cum_ref[...]
    total = cum[rows - 1 : rows, :]
    grown = spread(jnp.exp(cum), spread_mat)
    decay = spread(jnp.broadcast_to(jnp.exp(total), (8, LANES)), spread_mat)[0:1, :]
    new = decay * state[...] + dot(
        lhs3(split(jnp.transpose(c_mat))), rhs3(split(gm * grown))
    )
    state[...] = new
    own_ref[...] = new


def backward_kernel(gm_ref, act_ref, pre_ref, step_ref, cum_ref, mixer_ref, enter_ref, exit_ref, carried_ref,
                    x_raw_ref, cw_ref, d_ref, rate_ref, spread_ref, gather_ref, upper_ref,
                    gx_ref, tail_ref, head_ref, dbc_ref, gstep_ref, conv_ref, rate_out_ref,
                    state, ext):
    c = pl.program_id(0)
    rows, inner = gm_ref.shape

    @pl.when(c == 0)
    def _():
        state[...] = carried_ref[...]
        ext[rows : rows + 8, :] = jnp.zeros((8, inner), f32)
        conv_ref[...] = jnp.zeros_like(conv_ref)
        rate_out_ref[...] = jnp.zeros_like(rate_out_ref)

    heads = inner // HEAD_DIM
    per = LANES // HEAD_DIM
    spread_mat = spread_ref[...]
    gather_mat = gather_ref[...]
    gm = gm_ref[...]
    x = act_ref[:, 0:inner]
    b_mat = act_ref[:, inner : inner + STATE]
    c_mat = act_ref[:, inner + STATE : inner + 2 * STATE]
    step = step_ref[...]
    cum = cum_ref[...]
    cum_t = jnp.transpose(cum)
    total = cum[rows - 1 : rows, :]
    wide = spread(
        jnp.concatenate([step, jnp.exp(total - cum), jnp.exp(cum)], axis=0), spread_mat
    )
    step_wide, tail_wide, grown = wide[0:rows], wide[rows : 2 * rows], wide[2 * rows : 3 * rows]
    decay = spread(jnp.broadcast_to(jnp.exp(total), (8, LANES)), spread_mat)[0:1, :]
    x_step = x * step_wide
    b_parts, c_parts = split(b_mat), split(c_mat)
    b3 = lhs3(b_parts)
    scores_t = dot_t(b3, rhs3_t(c_parts))
    grad_exit = state[...]
    exit_parts = split(grad_exit)
    upper = lax.broadcasted_iota(jnp.int32, (rows, rows), 1) >= lax.broadcasted_iota(
        jnp.int32, (rows, rows), 0
    )
    lane = lax.broadcasted_iota(jnp.int32, (rows, LANES), 1)
    through = dot(b3, rhs3(exit_parts)) * tail_wide
    gm_hi, gm_lo = split(gm)
    xs_hi, xs_lo = split(x_step)
    tiles = []
    grad_scores = jnp.zeros((rows, rows), f32)
    zero = jnp.zeros((rows, LANES), bf16)
    for tile in range(heads // per):
        cut = slice(tile * LANES, (tile + 1) * LANES)
        g_hi, g_lo = gm_hi[:, cut], gm_lo[:, cut]
        g_rows = jnp.concatenate([g_hi, g_hi, g_lo], axis=0)
        g_lanes = jnp.concatenate([g_hi, g_hi, g_lo], axis=1)
        got = None
        for j in range(per):
            h = tile * per + j
            keep = (lane >= j * HEAD_DIM) & (lane < (j + 1) * HEAD_DIM)
            xh = jnp.where(keep, xs_hi[:, cut], zero)
            xl = jnp.where(keep, xs_lo[:, cut], zero)
            gap = cum_t[h : h + 1, :] - cum[:, h : h + 1]
            span = jnp.where(upper, jnp.exp(jnp.minimum(gap, 0.0)), 0.0)
            pairs = dot_t(jnp.concatenate([xh, xl, xh], axis=1), g_lanes)
            grad_scores = grad_scores + span * pairs
            part = dot(lhs3(split(span * scores_t)), g_rows)
            got = part if got is None else jnp.where(lane >= j * HEAD_DIM, part, got)
        tiles.append(got)
    grad_xs = jnp.concatenate(tiles, axis=1) + through
    scores_parts = split(grad_scores)
    weighted = gm * grown
    weighted_parts = split(weighted)
    enter_parts = split(enter_ref[...])
    grad_b = dot(lhs3(scores_parts), rhs3(c_parts)) + dot_t(
        lhs3(split(x_step * tail_wide)), rhs3_t(exit_parts)
    )
    grad_c = dot(lhs3(split(jnp.transpose(grad_scores))), rhs3(b_parts)) + dot_t(
        lhs3(weighted_parts), rhs3_t(enter_parts)
    )
    dbc_ref[:, 0:STATE] = grad_b
    dbc_ref[:, STATE : 2 * STATE] = grad_c
    lost = jnp.sum(grad_exit * exit_ref[...], axis=0, keepdims=True)
    state[...] = decay * grad_exit + dot(
        lhs3(split(jnp.transpose(c_mat))), rhs3(weighted_parts)
    )
    ssd = mixer_ref[...] - d_ref[...] * x
    heads_sum = gather_heads(
        jnp.concatenate([gm * ssd, x * grad_xs, jnp.broadcast_to(lost, (8, inner))], axis=0), gather_mat
    )
    by_step = heads_sum[rows : 2 * rows]
    grad_log = tri_sum(upper_ref[...], heads_sum[0:rows] - step * by_step) + heads_sum[
        2 * rows : 2 * rows + 1
    ]
    gstep_ref[...] = by_step - rate_ref[...] * grad_log
    rate_out_ref[0:1, :] += -jnp.sum(grad_log * step, axis=0, keepdims=True)
    pre = pre_ref[...]
    grad_pre = (grad_xs * step_wide + d_ref[...] * gm) * slope_of(pre, sigmoid(pre))
    ext[0:rows, :] = grad_pre
    raw = x_raw_ref[...].astype(f32)
    conv_ref[CONV : CONV + 1, :] += jnp.sum(grad_pre, axis=0, keepdims=True)
    total_in = None
    for k in range(CONV):
        moved = ext[CONV - 1 - k : CONV - 1 - k + rows, :]
        conv_ref[k : k + 1, :] += jnp.sum(moved * raw, axis=0, keepdims=True)
        piece = cw_ref[k : k + 1, :] * moved
        total_in = piece if total_in is None else total_in + piece
    gx_ref[...] = total_in.astype(bf16)

    @pl.when(c == 0)
    def _():
        tail_ref[...] = total_in[rows - 8 : rows, :]

    head_ref[...] = grad_pre[0:8, :]
    ext[rows : rows + 8, :] = grad_pre[0:8, :]


def shifted(value, axis, by):
    length = lax.axis_size(axis)
    pairs = [(i, i + by) for i in range(length) if 0 <= i + by < length]
    return lax.ppermute(value, axis, pairs)


def chain(local, decay, axis, by):
    got = None
    for _ in range(lax.axis_size(axis) - 1):
        got = shifted(local if got is None else local + decay * got, axis, by)
    return jnp.zeros_like(local) if got is None else got


class Ring:
    def __init__(self, axis):
        self.axis = axis
        self.size = lax.axis_size(axis)
        self.me = lax.axis_index(axis)
        self.paired = self.size & (self.size - 1) == 0

    def target(self, m):
        return self.me ^ m if self.paired else (self.me + m) % self.size

    def source(self, m):
        return self.me ^ m if self.paired else (self.me - m) % self.size

    def send(self, value, m):
        pairs = [(i, i ^ m if self.paired else (i + m) % self.size) for i in range(self.size)]
        return lax.ppermute(value, self.axis, pairs)

    def gather(self, value):
        if not self.paired:
            return lax.all_gather(value, self.axis, axis=0, tiled=True)
        pieces, step = {0: value}, self.size // 2
        while step:
            pieces.update({m | step: self.send(piece, step) for m, piece in pieces.items()})
            step //= 2
        rows = value.shape[0]
        full = jnp.zeros((rows * self.size,) + value.shape[1:], value.dtype)
        for m, piece in pieces.items():
            full = lax.dynamic_update_slice_in_dim(full, piece, self.source(m) * rows, 0)
        return full

    def sum_pieces(self, piece):
        if self.size != 4:
            got = [self.send(piece(m).astype(bf16), m) for m in range(1, self.size)]
            total = piece(0)
            for value in got:
                total = total + value.astype(f32)
            return total
        far = piece(3).astype(bf16)
        handed = lax.ppermute(far, self.axis, [(0, 1), (3, 2)])
        middle = lax.ppermute(far, self.axis, [(1, 2), (2, 1)])
        near = self.send(piece(1).astype(bf16), 1)
        across = self.send((piece(2) + handed.astype(f32)).astype(bf16), 2)
        total = piece(0)
        for value in (middle, near, across):
            total = total + value.astype(f32)
        return total

    def all_pieces(self, own):
        if self.size != 4:
            return [own] + [self.send(own, m) for m in range(1, self.size)]
        across = self.send(own, 2)
        near = self.send(own, 1)
        middle = lax.ppermute(own, self.axis, [(1, 2), (2, 1)])
        handed = lax.ppermute(across, self.axis, [(1, 0), (2, 3)])
        return [own, near, across, middle + handed]


def body(
    block_input,
    norm_gain,
    w_z,
    w_x,
    w_bc,
    w_dt,
    conv_x_weight,
    conv_x_bias,
    conv_bc_weight,
    conv_bc_bias,
    dt_bias,
    a_log,
    d_skip,
    gate_gain,
    w_out,
    out_cotangent,
):
    length, width = block_input.shape
    inner = w_z.shape[1]
    heads = w_dt.shape[1]
    wide = inner + 2 * STATE
    inner_width = HEADS * HEAD_DIM
    line = Ring("tensor")
    ranks = line.size
    quarter = length // ranks
    rows = min(SPAN, length)
    count = length // rows

    w_cat = jnp.concatenate([w_x, jnp.pad(w_dt, ((0, 0), (0, LANES - heads))), w_bc], axis=1)
    ring = Ring("shard")
    w_out_t = w_out.T
    full_cat = ring.gather(w_cat)
    others = [line.send(w_out_t, m) for m in range(1, ranks)]
    full_z = ring.gather(w_z)
    full_out = ring.gather(w_out_t)
    full_others = ring.gather(jnp.concatenate(others, axis=1))

    x_float = block_input.astype(f32)
    inverse = lax.rsqrt(jnp.mean(x_float * x_float, axis=1, keepdims=True) + epsilon)
    normed = (x_float * inverse * norm_gain).astype(bf16)
    proj = jnp.dot(normed, full_cat, preferred_element_type=f32)
    x_raw = proj[:, :inner].astype(bf16)
    dt_raw = proj[:, inner : inner + LANES]
    bc_raw = proj[:, inner + LANES :].astype(bf16)
    z_part = jnp.dot(normed, full_z, preferred_element_type=f32)

    edge = shifted(
        jnp.concatenate([x_raw[length - CONV + 1 :], bc_raw[length - CONV + 1 :]], axis=1), "context", 1
    ).astype(f32)
    edge = jnp.pad(edge, ((8 - CONV + 1, 0), (0, 0)))
    conv_weight = jnp.concatenate([conv_x_weight, conv_bc_weight], axis=1)
    conv_bias = jnp.concatenate([conv_x_bias, conv_bc_bias])[None, :]
    dt_in = dt_raw + jnp.pad(dt_bias, (0, LANES - heads))
    step = jax.nn.softplus(dt_in)
    decay_rate = jnp.exp(a_log)
    rate_row = jnp.pad(decay_rate, (0, LANES - heads))[None, :]
    d_row = jnp.repeat(d_skip, HEAD_DIM)[None, :]
    gain_row = gate_gain[None, :]
    owner = jnp.arange(inner) // HEAD_DIM
    one_hot = (jnp.arange(LANES)[:, None] == owner[None, :]).astype(bf16)
    spread_mat = jnp.concatenate([one_hot, one_hot], axis=0)
    one_hot_t = (owner[:, None] == jnp.arange(LANES)[None, :]).astype(bf16)
    gather_mat = jnp.concatenate([one_hot_t, one_hot_t], axis=0)
    place = jnp.arange(rows)
    lower = (place[:, None] >= place[None, :]).astype(bf16)
    lower2 = jnp.concatenate([lower, lower], axis=1)
    upper = (place[:, None] <= place[None, :]).astype(bf16)
    upper2 = jnp.concatenate([upper, upper], axis=1)

    def whole(shape):
        return pl.BlockSpec(shape, lambda c: (0,) * len(shape))

    def ahead(lanes, high=rows):
        return pl.BlockSpec((high, lanes), lambda c: (c, 0))

    def back(lanes, high=rows):
        return pl.BlockSpec((high, lanes), lambda c: (count - 1 - c, 0))

    def shape(*dims, dtype=f32):
        return jax.ShapeDtypeStruct(dims, dtype)

    params = pltpu.CompilerParams(dimension_semantics=("arbitrary",))

    pre, act, cum, s_local, totals = pl.pallas_call(
        front_kernel,
        grid=(count,),
        in_specs=[
            ahead(inner), ahead(2 * STATE), whole((8, wide)), whole((CONV, wide)), whole((1, wide)),
            ahead(LANES), whole((1, LANES)), whole((2 * LANES, inner)), whole((rows, 2 * rows)),
        ],
        out_specs=[ahead(wide), ahead(wide), ahead(LANES), whole((STATE, inner)), whole((8, LANES))],
        out_shape=[
            shape(length, wide), shape(length, wide), shape(length, LANES), shape(STATE, inner),
            shape(8, LANES),
        ],
        scratch_shapes=[pltpu.VMEM((rows + 8, wide), f32), pltpu.VMEM((STATE, inner), f32)],
        compiler_params=params,
        name="front",
    )(x_raw, bc_raw, edge, conv_weight, conv_bias, step, rate_row, spread_mat, lower2)
    decay = jnp.repeat(jnp.exp(totals[0, :heads]), HEAD_DIM)[None, :]
    s_in = chain(s_local, decay, "context", 1)

    ggo = jnp.dot(out_cotangent, full_out, preferred_element_type=f32)
    mixer, enter, leave, sums = pl.pallas_call(
        forward_kernel,
        grid=(count,),
        in_specs=[
            ahead(wide), ahead(LANES), ahead(LANES), ahead(inner), ahead(inner), whole((STATE, inner)),
            whole((1, inner)), whole((1, inner)), whole((2 * LANES, inner)),
        ],
        out_specs=[
            ahead(inner), ahead(inner, STATE), ahead(inner, STATE), pl.BlockSpec((8, rows), lambda c: (0, c)),
        ],
        out_shape=[
            shape(length, inner), shape(count * STATE, inner), shape(count * STATE, inner), shape(8, length),
        ],
        scratch_shapes=[pltpu.VMEM((STATE, inner), f32)],
        compiler_params=params,
        name="forward",
    )(act, step, cum, z_part, ggo, s_in, d_row, gain_row, spread_mat)
    sums = lax.psum(sums, "tensor")

    gated_out, gm, grad_z, own, gate_acc = pl.pallas_call(
        functools.partial(gate_kernel, inner_width),
        grid=(count,),
        in_specs=[
            back(inner), back(inner), back(inner), pl.BlockSpec((8, rows), lambda c: (0, count - 1 - c)),
            back(wide), back(LANES), whole((1, inner)), whole((2 * LANES, inner)),
        ],
        out_specs=[back(inner), back(inner), back(inner), whole((STATE, inner)), whole((8, inner))],
        out_shape=[
            shape(length, inner, dtype=bf16), shape(length, inner), shape(length, inner, dtype=bf16),
            shape(STATE, inner), shape(8, inner),
        ],
        scratch_shapes=[pltpu.VMEM((STATE, inner), f32)],
        compiler_params=params,
        name="gate",
    )(mixer, z_part, ggo, sums, act, cum, gain_row, spread_mat)
    carried = chain(own, decay, "context", -1)

    def block(value, rank):
        return lax.dynamic_slice_in_dim(value, rank * quarter, quarter)

    mixed = [line.send(block(gated_out, line.target(m)), m) for m in range(1, ranks)]
    grad_w_out = jnp.einsum("tk,td->kd", gated_out, out_cotangent, preferred_element_type=f32)
    summed_out = lax.psum_scatter(grad_w_out, ("shard", "context"), scatter_dimension=1, tiled=True)
    grad_w_z = jnp.einsum("td,tk->dk", normed, grad_z, preferred_element_type=f32)
    summed_z = lax.psum_scatter(grad_w_z, ("shard", "context"), scatter_dimension=0, tiled=True)

    gx, gx_tail, pre_head, dbc, gstep, conv_acc, rate_acc = pl.pallas_call(
        backward_kernel,
        grid=(count,),
        in_specs=[
            back(inner), back(wide), back(inner), back(LANES), back(LANES), back(inner),
            back(inner, STATE), back(inner, STATE), whole((STATE, inner)), back(inner), whole((CONV, inner)),
            whole((1, inner)), whole((1, LANES)), whole((2 * LANES, inner)), whole((2 * inner, LANES)),
            whole((rows, 2 * rows)),
        ],
        out_specs=[
            back(inner), whole((8, inner)), whole((8, inner)), back(2 * STATE), back(LANES), whole((8, inner)),
            whole((8, LANES)),
        ],
        out_shape=[
            shape(length, inner, dtype=bf16), shape(8, inner), shape(8, inner), shape(length, 2 * STATE),
            shape(length, LANES), shape(8, inner), shape(8, LANES),
        ],
        scratch_shapes=[pltpu.VMEM((STATE, inner), f32), pltpu.VMEM((rows + 8, inner), f32)],
        compiler_params=params,
        name="backward",
    )(gm, act, pre, step, cum, mixer, enter, leave, carried, x_raw, conv_x_weight, d_row, rate_row,
      spread_mat, gather_mat, upper2)

    got = [line.send(block(dbc, line.target(m)), m) for m in range(1, ranks)]
    bc_own = block(dbc, line.me)
    for value in got:
        bc_own = bc_own + value
    pieces = line.all_pieces(bc_own)
    for m in range(ranks):
        dbc = lax.dynamic_update_slice_in_dim(dbc, pieces[m], line.source(m) * quarter, 0)
    pre_bc = pre[:, inner:]
    grad_pre_bc = dbc * slope_of(pre_bc, jax.nn.sigmoid(pre_bc))
    next_head = shifted(pre_head[: CONV - 1], "context", -1)
    next_bc_head = shifted(grad_pre_bc[: CONV - 1], "context", -1)
    after = jnp.pad(next_head, ((CONV - 1, CONV - 1), (0, 0)))
    reach = jnp.zeros((CONV - 1, inner), f32)
    for k in range(CONV):
        reach = reach + conv_x_weight[k] * after[CONV - 1 - k : 2 * (CONV - 1) - k]
    gx_last = (gx_tail + jnp.pad(reach, ((8 - CONV + 1, 0), (0, 0)))).astype(bf16)
    gx = lax.dynamic_update_slice_in_dim(gx, gx_last, length - 8, 0)
    bc_pad = jnp.concatenate([grad_pre_bc, next_bc_head], axis=0)
    gbc = jnp.zeros((length, 2 * STATE), f32)
    for k in range(CONV):
        gbc = gbc + conv_bc_weight[k] * bc_pad[CONV - 1 - k : CONV - 1 - k + length]
    gbc = gbc.astype(bf16)
    head_pad = jnp.pad(pre_head[: CONV - 1], ((CONV - 1, CONV - 1), (0, 0)))
    entering = edge[8 - CONV + 1 :]
    extra = jnp.stack([
        jnp.sum(entering[:, :inner] * head_pad[CONV - 1 - k : 2 * (CONV - 1) - k], axis=0)
        for k in range(CONV)
    ])
    bc_in = jnp.concatenate([entering[:, inner:], bc_raw.astype(f32)], axis=0)
    grad_conv_bc = jnp.stack([jnp.sum(grad_pre_bc * bc_in[k : k + length], axis=0) for k in range(CONV)])
    grad_conv_bc_bias = jnp.sum(grad_pre_bc, axis=0)

    sigma = jax.nn.sigmoid(dt_in)
    g_dt = gstep * sigma
    grad_dt_bias = jnp.sum(g_dt, axis=0)
    g_dt = g_dt.astype(bf16)
    grad_a_log = rate_acc[0] * rate_row[0]

    g_xdt = jnp.concatenate([gx, g_dt], axis=1)
    full_xdt = full_cat[:, : inner + LANES]

    def partial_of(m):
        rank = line.target(m)
        return jnp.einsum("tk,dk->td", block(grad_z, rank), full_z, preferred_element_type=f32) + jnp.einsum(
            "tk,dk->td", block(g_xdt, rank), full_xdt, preferred_element_type=f32
        )

    gn = line.sum_pieces(partial_of)
    gn = gn + jnp.einsum(
        "tk,dk->td", block(gbc, line.me), full_cat[:, inner + LANES :], preferred_element_type=f32
    )

    out_own = jnp.einsum("tk,dk->td", block(gated_out, line.me), full_out, preferred_element_type=f32)
    if ranks > 1:
        out_own = out_own + jnp.einsum(
            "tk,dk->td", jnp.concatenate(mixed, axis=1), full_others, preferred_element_type=f32
        )
    block_own = (block(block_input, line.me).astype(f32) + out_own).astype(bf16)
    pieces = line.all_pieces(block_own)
    block_output = jnp.zeros((length, width), bf16)
    for m in range(ranks):
        block_output = lax.dynamic_update_slice_in_dim(
            block_output, pieces[m], line.source(m) * quarter, 0
        )

    x_own, inv_own = block(x_float, line.me), block(inverse, line.me)
    scaled = norm_gain * gn
    delta = inv_own * scaled - x_own * (inv_own * inv_own * inv_own) * jnp.mean(
        scaled * x_own, axis=1, keepdims=True
    )
    delta = delta.astype(bf16)
    grad_norm_gain = jnp.sum(gn * x_own * inv_own, axis=0)
    pieces = line.all_pieces(delta)
    input_grad = jnp.zeros((length, width), f32)
    for m in range(ranks):
        rank = line.source(m)
        input_grad = lax.dynamic_update_slice_in_dim(
            input_grad,
            block(out_cotangent, rank).astype(f32) + pieces[m].astype(f32),
            rank * quarter,
            0,
        )

    g_cat = jnp.concatenate([g_xdt, gbc], axis=1)
    grad_w_cat = jnp.einsum("td,tk->dk", normed, g_cat, preferred_element_type=f32)
    summed_cat = lax.psum_scatter(grad_w_cat, ("shard", "context"), scatter_dimension=0, tiled=True)

    last = jnp.pad(jnp.concatenate([grad_dt_bias[:LANES], grad_a_log]), (0, inner - 2 * LANES))[None, :]
    packed = jnp.concatenate(
        [
            jnp.concatenate([conv_acc[:CONV] + extra, conv_acc[CONV : CONV + 1], gate_acc[:2], last], axis=0),
            jnp.concatenate(
                [grad_conv_bc, grad_conv_bc_bias[None, :], jnp.zeros((3, 2 * STATE), f32)], axis=0
            ),
        ],
        axis=1,
    )
    wide_lanes = packed.shape[1]
    spare = (-width) % wide_lanes
    gain_rows = jnp.pad(grad_norm_gain, (0, spare)).reshape(-1, wide_lanes)
    packed = lax.psum(jnp.concatenate([packed, gain_rows], axis=0), ("shard", "context"))
    gain_rows = packed[8:]
    parts = [gain_rows] + [line.send(gain_rows, m) for m in range(1, ranks)]
    ordered = jnp.zeros((ranks,) + gain_rows.shape, f32)
    for m in range(ranks):
        ordered = lax.dynamic_update_slice_in_dim(ordered, parts[m][None], line.source(m), 0)
    sum_norm_gain = jnp.sum(ordered, axis=0).reshape(-1)[:width]
    return (
        block_output,
        input_grad,
        summed_z,
        summed_cat[:, :inner],
        summed_cat[:, inner + LANES :],
        summed_cat[:, inner : inner + heads],
        summed_out,
        sum_norm_gain,
        packed[:CONV, :inner],
        packed[CONV, :inner],
        packed[:CONV, inner:],
        packed[CONV, inner:],
        packed[7, :heads],
        packed[7, LANES : LANES + heads],
        jnp.sum(packed[6, :inner].reshape(heads, HEAD_DIM), axis=1),
        packed[5, :inner],
    )


def solution(mesh):
    in_specs = (
        P(("shard", "context"), None),
        P(),
        P("shard", "tensor"),
        P("shard", "tensor"),
        P("shard", None),
        P("shard", "tensor"),
        P(None, "tensor"),
        P("tensor"),
        P(),
        P(),
        P("tensor"),
        P("tensor"),
        P("tensor"),
        P("tensor"),
        P("tensor", "shard"),
        P(("shard", "context"), None),
    )
    out_specs = (
        P(("shard", "context"), None),
        P(("shard", "context"), None),
        P(("shard", "context"), "tensor"),
        P(("shard", "context"), "tensor"),
        P(("shard", "context"), None),
        P(("shard", "context"), "tensor"),
        P("tensor", ("shard", "context")),
        P(),
        P(None, "tensor"),
        P("tensor"),
        P(),
        P(),
        P("tensor"),
        P("tensor"),
        P("tensor"),
        P("tensor"),
    )
    return jax.shard_map(body, mesh=mesh, in_specs=in_specs, out_specs=out_specs, check_vma=False)
```

```python
import functools

import jax
import jax.numpy as jnp
from jax import lax
from jax.experimental import pallas as pl
from jax.experimental.layout import Layout, with_layout_constraint
from jax.experimental.pallas import tpu as pltpu
from jax.sharding import PartitionSpec as P


HEADS = 48
HEAD_DIM = 64
STATE = 128
CONV = 4
SPAN = 128
LANES = 128

epsilon = 1e-05
SHARD = "shard"
CONTEXT = "context"
TENSOR = "tensor"
f32 = jnp.float32
bf16 = jnp.bfloat16


def split(v):
    hi = v.astype(bf16)
    return hi, (v - hi.astype(f32)).astype(bf16)


def dot(a, b):
    return lax.dot_general(a, b, (((1,), (0,)), ((), ())), preferred_element_type=f32)


def dot_t(a, b):
    return lax.dot_general(a, b, (((1,), (1,)), ((), ())), preferred_element_type=f32)


def dot_tn(a, b):
    return lax.dot_general(a, b, (((0,), (0,)), ((), ())), preferred_element_type=f32)


def lhs3(parts):
    hi, lo = parts
    return jnp.concatenate([hi, lo, hi], axis=1)


def rhs3(parts):
    hi, lo = parts
    return jnp.concatenate([hi, hi, lo], axis=0)


def rhs3_t(parts):
    hi, lo = parts
    return jnp.concatenate([hi, hi, lo], axis=1)


def spread(values, spread_mat):
    hi, lo = split(values)
    return dot(jnp.concatenate([hi, lo], axis=1), spread_mat)


def gather_heads(values, gather_mat):
    hi, lo = split(values)
    return dot(jnp.concatenate([hi, lo], axis=1), gather_mat)


def tri_sum(tri2, values):
    hi, lo = split(values)
    return dot(tri2, jnp.concatenate([hi, lo], axis=0))


def sigmoid(v):
    return 1.0 / (1.0 + jnp.exp(-v))


def slope_of(v, sigma):
    return sigma * (1.0 + v * (1.0 - sigma))


def front_kernel(x_ref, bc_ref, edge_ref, cw_ref, cb_ref, step_ref, rate_ref, spread_ref, tri_ref,
                 pre_ref, act_ref, cum_ref, state_ref, total_ref, ext, state):
    c = pl.program_id(0)
    rows, inner = x_ref.shape
    wide = cw_ref.shape[1]

    @pl.when(c == 0)
    def _():
        ext[0:8, :] = edge_ref[...]
        state[...] = jnp.zeros_like(state)
        total_ref[...] = jnp.zeros_like(total_ref)

    ext[8 : 8 + rows, 0:inner] = x_ref[...].astype(f32)
    ext[8 : 8 + rows, inner:wide] = bc_ref[...].astype(f32)
    pre = cb_ref[...] + cw_ref[0:1, :] * ext[5 : 5 + rows, :]
    for k in range(1, CONV):
        pre = pre + cw_ref[k : k + 1, :] * ext[5 + k : 5 + k + rows, :]
    ext[0:8, :] = ext[rows : rows + 8, :]
    act = pre * sigmoid(pre)
    pre_ref[...] = pre
    act_ref[...] = act
    step = step_ref[...]
    cum = tri_sum(tri_ref[...], -step * rate_ref[...])
    cum_ref[...] = cum
    total = cum[rows - 1 : rows, :]
    b_t = jnp.transpose(act[:, inner : inner + STATE])
    weight = spread(step * jnp.exp(total - cum), spread_ref[...])
    decay = spread(jnp.broadcast_to(jnp.exp(total), (8, LANES)), spread_ref[...])[0:1, :]
    new = decay * state[...] + dot(lhs3(split(b_t)), rhs3(split(act[:, 0:inner] * weight)))
    state[...] = new
    state_ref[...] = new
    total_ref[...] = total_ref[...] + jnp.broadcast_to(total, (8, LANES))


def forward_kernel(act_ref, step_ref, cum_ref, z_ref, ggo_ref, s_in_ref, d_ref, gain_ref, spread_ref,
                   mixer_ref, enter_ref, exit_ref, sums_ref, state):
    c = pl.program_id(0)
    rows, inner = z_ref.shape

    @pl.when(c == 0)
    def _():
        state[...] = s_in_ref[...]

    heads = inner // HEAD_DIM
    per = LANES // HEAD_DIM
    spread_mat = spread_ref[...]
    x = act_ref[:, 0:inner]
    b_mat = act_ref[:, inner : inner + STATE]
    c_mat = act_ref[:, inner + STATE : inner + 2 * STATE]
    step = step_ref[...]
    cum = cum_ref[...]
    cum_t = jnp.transpose(cum)
    total = cum[rows - 1 : rows, :]
    wide = spread(
        jnp.concatenate([step, step * jnp.exp(total - cum), jnp.exp(cum)], axis=0), spread_mat
    )
    decay = spread(jnp.broadcast_to(jnp.exp(total), (8, LANES)), spread_mat)[0:1, :]
    x_step = x * wide[0:rows]
    c3 = lhs3(split(c_mat))
    scores = dot_t(c3, rhs3_t(split(b_mat)))
    enter = state[...]
    enter_ref[...] = enter
    outer = dot(c3, rhs3(split(enter))) * wide[2 * rows : 3 * rows]
    lower = lax.broadcasted_iota(jnp.int32, (rows, rows), 0) >= lax.broadcasted_iota(
        jnp.int32, (rows, rows), 1
    )
    lane = lax.broadcasted_iota(jnp.int32, (rows, LANES), 1)
    masked = jnp.where(lower, scores, 0.0)
    tiles = []
    for tile in range(heads // per):
        value = rhs3(split(x_step[:, tile * LANES : (tile + 1) * LANES]))
        got = None
        for j in range(per):
            h = tile * per + j
            gap = cum[:, h : h + 1] - cum_t[h : h + 1, :]
            part = dot(lhs3(split(jnp.exp(jnp.minimum(gap, 0.0)) * masked)), value)
            got = part if got is None else jnp.where(lane >= j * HEAD_DIM, part, got)
        tiles.append(got)
    inner_out = jnp.concatenate(tiles, axis=1)
    mixer = inner_out + outer + d_ref[...] * x
    mixer_ref[...] = mixer
    b_t = jnp.transpose(b_mat)
    new = decay * enter + dot(lhs3(split(b_t)), rhs3(split(x * wide[rows : 2 * rows])))
    state[...] = new
    exit_ref[...] = new
    z = z_ref[...]
    gated = mixer * (z * sigmoid(z))
    square = jnp.sum(gated * gated, axis=1, keepdims=True)
    term = jnp.sum(gain_ref[...] * ggo_ref[...] * gated, axis=1, keepdims=True)
    both = jnp.where(lane == 0, square, term)
    sums_ref[...] = jnp.transpose(both)[0:8, :]


def gate_kernel(inner_width, mixer_ref, z_ref, ggo_ref, sums_ref, act_ref, cum_ref, gain_ref, spread_ref,
                out_ref, gm_ref, gz_ref, own_ref, acc_ref, state):
    c = pl.program_id(0)
    rows, inner = z_ref.shape

    @pl.when(c == 0)
    def _():
        state[...] = jnp.zeros_like(state)
        acc_ref[...] = jnp.zeros_like(acc_ref)

    spread_mat = spread_ref[...]
    columns = jnp.transpose(jnp.concatenate([sums_ref[...]] * (LANES // 8), axis=0))
    inverse = lax.rsqrt(columns[:, 0:1] / inner_width + epsilon)
    term = columns[:, 1:2] / inner_width
    mixer = mixer_ref[...]
    z = z_ref[...]
    sigma = sigmoid(z)
    gate = z * sigma
    gated = mixer * gate
    ggo = ggo_ref[...]
    normal = gated * inverse
    out_ref[...] = (normal * gain_ref[...]).astype(bf16)
    grad_gated = inverse * (gain_ref[...] * ggo) - normal * (inverse * inverse * term)
    gm = grad_gated * gate
    gm_ref[...] = gm
    gz_ref[...] = (grad_gated * mixer * slope_of(z, sigma)).astype(bf16)
    x = act_ref[:, 0:inner]
    c_mat = act_ref[:, inner + STATE : inner + 2 * STATE]
    acc_ref[0:1, :] += jnp.sum(ggo * normal, axis=0, keepdims=True)
    acc_ref[1:2, :] += jnp.sum(gm * x, axis=0, keepdims=True)
    cum = cum_ref[...]
    total = cum[rows - 1 : rows, :]
    grown = spread(jnp.exp(cum), spread_mat)
    decay = spread(jnp.broadcast_to(jnp.exp(total), (8, LANES)), spread_mat)[0:1, :]
    new = decay * state[...] + dot(
        lhs3(split(jnp.transpose(c_mat))), rhs3(split(gm * grown))
    )
    state[...] = new
    own_ref[...] = new


def backward_kernel(gm_ref, act_ref, pre_ref, step_ref, cum_ref, mixer_ref, enter_ref, exit_ref, carried_ref,
                    x_raw_ref, cw_ref, d_ref, rate_ref, spread_ref, gather_ref, upper_ref,
                    gx_ref, tail_ref, head_ref, dbc_ref, gstep_ref, conv_ref, rate_out_ref,
                    state, ext):
    c = pl.program_id(0)
    rows, inner = gm_ref.shape

    @pl.when(c == 0)
    def _():
        state[...] = carried_ref[...]
        ext[rows : rows + 8, :] = jnp.zeros((8, inner), f32)
        conv_ref[...] = jnp.zeros_like(conv_ref)
        rate_out_ref[...] = jnp.zeros_like(rate_out_ref)

    heads = inner // HEAD_DIM
    per = LANES // HEAD_DIM
    spread_mat = spread_ref[...]
    gather_mat = gather_ref[...]
    gm = gm_ref[...]
    x = act_ref[:, 0:inner]
    b_mat = act_ref[:, inner : inner + STATE]
    c_mat = act_ref[:, inner + STATE : inner + 2 * STATE]
    step = step_ref[...]
    cum = cum_ref[...]
    cum_t = jnp.transpose(cum)
    total = cum[rows - 1 : rows, :]
    wide = spread(
        jnp.concatenate([step, jnp.exp(total - cum), jnp.exp(cum)], axis=0), spread_mat
    )
    step_wide, tail_wide, grown = wide[0:rows], wide[rows : 2 * rows], wide[2 * rows : 3 * rows]
    decay = spread(jnp.broadcast_to(jnp.exp(total), (8, LANES)), spread_mat)[0:1, :]
    x_step = x * step_wide
    b_parts, c_parts = split(b_mat), split(c_mat)
    b3 = lhs3(b_parts)
    scores_t = dot_t(b3, rhs3_t(c_parts))
    grad_exit = state[...]
    exit_parts = split(grad_exit)
    upper = lax.broadcasted_iota(jnp.int32, (rows, rows), 1) >= lax.broadcasted_iota(
        jnp.int32, (rows, rows), 0
    )
    lane = lax.broadcasted_iota(jnp.int32, (rows, LANES), 1)
    through = dot(b3, rhs3(exit_parts)) * tail_wide
    gm_hi, gm_lo = split(gm)
    xs_hi, xs_lo = split(x_step)
    tiles = []
    grad_scores = jnp.zeros((rows, rows), f32)
    zero = jnp.zeros((rows, LANES), bf16)
    for tile in range(heads // per):
        cut = slice(tile * LANES, (tile + 1) * LANES)
        g_hi, g_lo = gm_hi[:, cut], gm_lo[:, cut]
        g_rows = jnp.concatenate([g_hi, g_hi, g_lo], axis=0)
        g_lanes = jnp.concatenate([g_hi, g_hi, g_lo], axis=1)
        got = None
        for j in range(per):
            h = tile * per + j
            keep = (lane >= j * HEAD_DIM) & (lane < (j + 1) * HEAD_DIM)
            xh = jnp.where(keep, xs_hi[:, cut], zero)
            xl = jnp.where(keep, xs_lo[:, cut], zero)
            gap = cum_t[h : h + 1, :] - cum[:, h : h + 1]
            span = jnp.where(upper, jnp.exp(jnp.minimum(gap, 0.0)), 0.0)
            pairs = dot_t(jnp.concatenate([xh, xl, xh], axis=1), g_lanes)
            grad_scores = grad_scores + span * pairs
            part = dot(lhs3(split(span * scores_t)), g_rows)
            got = part if got is None else jnp.where(lane >= j * HEAD_DIM, part, got)
        tiles.append(got)
    grad_xs = jnp.concatenate(tiles, axis=1) + through
    scores_parts = split(grad_scores)
    weighted = gm * grown
    weighted_parts = split(weighted)
    enter_parts = split(enter_ref[...])
    grad_b = dot(lhs3(scores_parts), rhs3(c_parts)) + dot_t(
        lhs3(split(x_step * tail_wide)), rhs3_t(exit_parts)
    )
    grad_c = dot(lhs3(split(jnp.transpose(grad_scores))), rhs3(b_parts)) + dot_t(
        lhs3(weighted_parts), rhs3_t(enter_parts)
    )
    dbc_ref[:, 0:STATE] = grad_b
    dbc_ref[:, STATE : 2 * STATE] = grad_c
    lost = jnp.sum(grad_exit * exit_ref[...], axis=0, keepdims=True)
    state[...] = decay * grad_exit + dot(
        lhs3(split(jnp.transpose(c_mat))), rhs3(weighted_parts)
    )
    ssd = mixer_ref[...] - d_ref[...] * x
    heads_sum = gather_heads(
        jnp.concatenate([gm * ssd, x * grad_xs, jnp.broadcast_to(lost, (8, inner))], axis=0), gather_mat
    )
    by_step = heads_sum[rows : 2 * rows]
    grad_log = tri_sum(upper_ref[...], heads_sum[0:rows] - step * by_step) + heads_sum[
        2 * rows : 2 * rows + 1
    ]
    gstep_ref[...] = by_step - rate_ref[...] * grad_log
    rate_out_ref[0:1, :] += -jnp.sum(grad_log * step, axis=0, keepdims=True)
    pre = pre_ref[...]
    grad_pre = (grad_xs * step_wide + d_ref[...] * gm) * slope_of(pre, sigmoid(pre))
    ext[0:rows, :] = grad_pre
    raw = x_raw_ref[...].astype(f32)
    conv_ref[CONV : CONV + 1, :] += jnp.sum(grad_pre, axis=0, keepdims=True)
    total_in = None
    for k in range(CONV):
        moved = ext[CONV - 1 - k : CONV - 1 - k + rows, :]
        conv_ref[k : k + 1, :] += jnp.sum(moved * raw, axis=0, keepdims=True)
        piece = cw_ref[k : k + 1, :] * moved
        total_in = piece if total_in is None else total_in + piece
    gx_ref[...] = total_in.astype(bf16)

    @pl.when(c == 0)
    def _():
        tail_ref[...] = total_in[rows - 8 : rows, :]

    head_ref[...] = grad_pre[0:8, :]
    ext[rows : rows + 8, :] = grad_pre[0:8, :]


def shifted(value, axis, by):
    length = lax.axis_size(axis)
    pairs = [(i, i + by) for i in range(length) if 0 <= i + by < length]
    return lax.ppermute(value, axis, pairs)


def chain(local, decay, axis, by):
    got = None
    for _ in range(lax.axis_size(axis) - 1):
        got = shifted(local if got is None else local + decay * got, axis, by)
    return jnp.zeros_like(local) if got is None else got


class Ring:
    def __init__(self, axis):
        self.axis = axis
        self.size = lax.axis_size(axis)
        self.me = lax.axis_index(axis)
        self.paired = self.size & (self.size - 1) == 0

    def target(self, m):
        return self.me ^ m if self.paired else (self.me + m) % self.size

    def source(self, m):
        return self.me ^ m if self.paired else (self.me - m) % self.size

    def send(self, value, m):
        pairs = [(i, i ^ m if self.paired else (i + m) % self.size) for i in range(self.size)]
        return lax.ppermute(value, self.axis, pairs)

    def far(self, value):
        if self.size == 1 or not self.paired:
            return {0: value}
        return {0: value, self.size // 2: self.send(value, self.size // 2)}

    def near(self, pieces):
        step = self.size // 4
        while step and self.paired:
            pieces = {**pieces, **{m | step: self.send(piece, step) for m, piece in pieces.items()}}
            step //= 2
        return pieces

    def join(self, pieces):
        value = pieces[0]
        if self.paired:
            rows = value.shape[0]
            full = jnp.zeros((rows * self.size,) + value.shape[1:], value.dtype)
            for m, piece in pieces.items():
                full = lax.dynamic_update_slice_in_dim(full, piece, self.source(m) * rows, 0)
        else:
            full = lax.all_gather(value, self.axis, axis=0, tiled=True)
        return with_layout_constraint(full, Layout((0, 1)))

    def reduce_rows(self, value):
        if not self.paired:
            return lax.psum_scatter(value, self.axis, scatter_dimension=0, tiled=True)
        left, step = self.size, 1
        rows = value.shape[0] // self.size
        while step < self.size:
            mine = (self.me // step) % 2
            view = value.reshape((left // 2, 2, rows) + value.shape[1:])
            keep = lax.dynamic_index_in_dim(view, mine, 1, keepdims=False)
            give = lax.dynamic_index_in_dim(view, 1 - mine, 1, keepdims=False)
            got = self.send(give, step)
            left, step = left // 2, step * 2
            value = (keep + got).reshape((left * rows,) + value.shape[1:])
        return value

    def sum_pieces(self, piece):
        if self.size != 4:
            got = [self.send(piece(m).astype(bf16), m) for m in range(1, self.size)]
            total = piece(0)
            for value in got:
                total = total + value.astype(f32)
            return total
        far = piece(3).astype(bf16)
        handed = lax.ppermute(far, self.axis, [(0, 1), (3, 2)])
        middle = lax.ppermute(far, self.axis, [(1, 2), (2, 1)])
        near = self.send(piece(1).astype(bf16), 1)
        across = self.send((piece(2) + handed.astype(f32)).astype(bf16), 2)
        total = piece(0)
        for value in (middle, near, across):
            total = total + value.astype(f32)
        return total

    def all_pieces(self, own):
        if self.size != 4:
            return [own] + [self.send(own, m) for m in range(1, self.size)]
        across = self.send(own, 2)
        near = self.send(own, 1)
        middle = lax.ppermute(own, self.axis, [(1, 2), (2, 1)])
        handed = lax.ppermute(across, self.axis, [(1, 0), (2, 3)])
        return [own, near, across, middle + handed]


def body(
    block_input,
    norm_gain,
    w_z,
    w_x,
    w_bc,
    w_dt,
    conv_x_weight,
    conv_x_bias,
    conv_bc_weight,
    conv_bc_bias,
    dt_bias,
    a_log,
    d_skip,
    gate_gain,
    w_out,
    out_cotangent,
):
    length, width = block_input.shape
    inner = w_z.shape[1]
    heads = w_dt.shape[1]
    wide = inner + 2 * STATE
    inner_width = HEADS * HEAD_DIM
    line = Ring(TENSOR)
    ranks = line.size
    quarter = length // ranks
    rows = min(SPAN, length)
    count = length // rows

    w_cat = jnp.concatenate([w_x, jnp.pad(w_dt, ((0, 0), (0, LANES - heads))), w_bc], axis=1)
    ring, range_ring = Ring(SHARD), Ring(CONTEXT)
    w_out_t = w_out.T
    full_cat = ring.join(ring.near(ring.far(w_cat)))
    others = [line.send(w_out_t, m) for m in range(1, ranks)]
    far_z = ring.far(w_z)
    far_out = ring.far(w_out_t)

    x_float = block_input.astype(f32)
    inverse = lax.rsqrt(jnp.mean(x_float * x_float, axis=1, keepdims=True) + epsilon)
    normed = (x_float * inverse * norm_gain).astype(bf16)
    proj = jnp.dot(normed, full_cat, preferred_element_type=f32)
    x_raw = proj[:, :inner].astype(bf16)
    dt_raw = proj[:, inner : inner + LANES]
    bc_raw = proj[:, inner + LANES :].astype(bf16)

    edge = shifted(
        jnp.concatenate([x_raw[length - CONV + 1 :], bc_raw[length - CONV + 1 :]], axis=1), CONTEXT, 1
    ).astype(f32)
    edge = jnp.pad(edge, ((8 - CONV + 1, 0), (0, 0)))
    conv_weight = jnp.concatenate([conv_x_weight, conv_bc_weight], axis=1)
    conv_bias = jnp.concatenate([conv_x_bias, conv_bc_bias])[None, :]
    dt_in = dt_raw + jnp.pad(dt_bias, (0, LANES - heads))
    step = jax.nn.softplus(dt_in)
    decay_rate = jnp.exp(a_log)
    rate_row = jnp.pad(decay_rate, (0, LANES - heads))[None, :]
    d_row = jnp.repeat(d_skip, HEAD_DIM)[None, :]
    gain_row = gate_gain[None, :]
    owner = jnp.arange(inner) // HEAD_DIM
    one_hot = (jnp.arange(LANES)[:, None] == owner[None, :]).astype(bf16)
    spread_mat = jnp.concatenate([one_hot, one_hot], axis=0)
    one_hot_t = (owner[:, None] == jnp.arange(LANES)[None, :]).astype(bf16)
    gather_mat = jnp.concatenate([one_hot_t, one_hot_t], axis=0)
    place = jnp.arange(rows)
    lower = (place[:, None] >= place[None, :]).astype(bf16)
    lower2 = jnp.concatenate([lower, lower], axis=1)
    upper = (place[:, None] <= place[None, :]).astype(bf16)
    upper2 = jnp.concatenate([upper, upper], axis=1)

    def whole(shape):
        return pl.BlockSpec(shape, lambda c: (0,) * len(shape))

    def ahead(lanes, high=rows):
        return pl.BlockSpec((high, lanes), lambda c: (c, 0))

    def back(lanes, high=rows):
        return pl.BlockSpec((high, lanes), lambda c: (count - 1 - c, 0))

    def shape(*dims, dtype=f32):
        return jax.ShapeDtypeStruct(dims, dtype)

    params = pltpu.CompilerParams(dimension_semantics=("arbitrary",))

    pre, act, cum, s_local, totals = pl.pallas_call(
        front_kernel,
        grid=(count,),
        in_specs=[
            ahead(inner), ahead(2 * STATE), whole((8, wide)), whole((CONV, wide)), whole((1, wide)),
            ahead(LANES), whole((1, LANES)), whole((2 * LANES, inner)), whole((rows, 2 * rows)),
        ],
        out_specs=[ahead(wide), ahead(wide), ahead(LANES), whole((STATE, inner)), whole((8, LANES))],
        out_shape=[
            shape(length, wide), shape(length, wide), shape(length, LANES), shape(STATE, inner),
            shape(8, LANES),
        ],
        scratch_shapes=[pltpu.VMEM((rows + 8, wide), f32), pltpu.VMEM((STATE, inner), f32)],
        compiler_params=params,
        name="front",
    )(x_raw, bc_raw, edge, conv_weight, conv_bias, step, rate_row, spread_mat, lower2)
    decay = jnp.repeat(jnp.exp(totals[0, :heads]), HEAD_DIM)[None, :]
    s_in = chain(s_local, decay, CONTEXT, 1)
    totals, far_z, far_out, others = lax.optimization_barrier((totals, far_z, far_out, others))
    full_z = ring.join(ring.near(far_z))
    full_out = ring.join(ring.near(far_out))
    all_others = ring.near(ring.far(jnp.concatenate(others, axis=1)))
    z_part = dot(normed, full_z)
    ggo = jnp.dot(out_cotangent, full_out, preferred_element_type=f32)
    mixer, enter, leave, sums = pl.pallas_call(
        forward_kernel,
        grid=(count,),
        in_specs=[
            ahead(wide), ahead(LANES), ahead(LANES), ahead(inner), ahead(inner), whole((STATE, inner)),
            whole((1, inner)), whole((1, inner)), whole((2 * LANES, inner)),
        ],
        out_specs=[
            ahead(inner), ahead(inner, STATE), ahead(inner, STATE), pl.BlockSpec((8, rows), lambda c: (0, c)),
        ],
        out_shape=[
            shape(length, inner), shape(count * STATE, inner), shape(count * STATE, inner), shape(8, length),
        ],
        scratch_shapes=[pltpu.VMEM((STATE, inner), f32)],
        compiler_params=params,
        name="forward",
    )(act, step, cum, z_part, ggo, s_in, d_row, gain_row, spread_mat)
    parts = [line.send(sums, m) for m in range(1, ranks)]
    for part in parts:
        sums = sums + part

    gated_out, gm, grad_z, own, gate_acc = pl.pallas_call(
        functools.partial(gate_kernel, inner_width),
        grid=(count,),
        in_specs=[
            back(inner), back(inner), back(inner), pl.BlockSpec((8, rows), lambda c: (0, count - 1 - c)),
            back(wide), back(LANES), whole((1, inner)), whole((2 * LANES, inner)),
        ],
        out_specs=[back(inner), back(inner), back(inner), whole((STATE, inner)), whole((8, inner))],
        out_shape=[
            shape(length, inner, dtype=bf16), shape(length, inner), shape(length, inner, dtype=bf16),
            shape(STATE, inner), shape(8, inner),
        ],
        scratch_shapes=[pltpu.VMEM((STATE, inner), f32)],
        compiler_params=params,
        name="gate",
    )(mixer, z_part, ggo, sums, act, cum, gain_row, spread_mat)
    carried = chain(own, decay, CONTEXT, -1)

    def block(value, rank):
        return lax.dynamic_slice_in_dim(value, rank * quarter, quarter)

    mixed = [line.send(block(gated_out, line.target(m)), m) for m in range(1, ranks)]
    grad_w_out = dot_tn(out_cotangent, gated_out)
    grad_w_z = dot_tn(normed, grad_z)
    summed_out, summed_z = ring.reduce_rows(grad_w_out), ring.reduce_rows(grad_w_z)
    summed_out, summed_z = range_ring.reduce_rows(summed_out).T, range_ring.reduce_rows(summed_z)

    gx, gx_tail, pre_head, dbc, gstep, conv_acc, rate_acc = pl.pallas_call(
        backward_kernel,
        grid=(count,),
        in_specs=[
            back(inner), back(wide), back(inner), back(LANES), back(LANES), back(inner),
            back(inner, STATE), back(inner, STATE), whole((STATE, inner)), back(inner), whole((CONV, inner)),
            whole((1, inner)), whole((1, LANES)), whole((2 * LANES, inner)), whole((2 * inner, LANES)),
            whole((rows, 2 * rows)),
        ],
        out_specs=[
            back(inner), whole((8, inner)), whole((8, inner)), back(2 * STATE), back(LANES), whole((8, inner)),
            whole((8, LANES)),
        ],
        out_shape=[
            shape(length, inner, dtype=bf16), shape(8, inner), shape(8, inner), shape(length, 2 * STATE),
            shape(length, LANES), shape(8, inner), shape(8, LANES),
        ],
        scratch_shapes=[pltpu.VMEM((STATE, inner), f32), pltpu.VMEM((rows + 8, inner), f32)],
        compiler_params=params,
        name="backward",
    )(gm, act, pre, step, cum, mixer, enter, leave, carried, x_raw, conv_x_weight, d_row, rate_row,
      spread_mat, gather_mat, upper2)

    got = [line.send(block(dbc, line.target(m)), m) for m in range(1, ranks)]
    bc_own = block(dbc, line.me)
    for value in got:
        bc_own = bc_own + value
    pieces = [bc_own] + [line.send(bc_own, m) for m in range(1, ranks)]
    for m in range(ranks):
        dbc = lax.dynamic_update_slice_in_dim(dbc, pieces[m], line.source(m) * quarter, 0)
    pre_bc = pre[:, inner:]
    grad_pre_bc = dbc * slope_of(pre_bc, jax.nn.sigmoid(pre_bc))
    next_head = shifted(pre_head[: CONV - 1], CONTEXT, -1)
    next_bc_head = shifted(grad_pre_bc[: CONV - 1], CONTEXT, -1)
    after = jnp.pad(next_head, ((CONV - 1, CONV - 1), (0, 0)))
    reach = jnp.zeros((CONV - 1, inner), f32)
    for k in range(CONV):
        reach = reach + conv_x_weight[k] * after[CONV - 1 - k : 2 * (CONV - 1) - k]
    gx_last = (gx_tail + jnp.pad(reach, ((8 - CONV + 1, 0), (0, 0)))).astype(bf16)
    gx = lax.dynamic_update_slice_in_dim(gx, gx_last, length - 8, 0)
    bc_pad = jnp.concatenate([grad_pre_bc, next_bc_head], axis=0)
    gbc = jnp.zeros((length, 2 * STATE), f32)
    for k in range(CONV):
        gbc = gbc + conv_bc_weight[k] * bc_pad[CONV - 1 - k : CONV - 1 - k + length]
    gbc = gbc.astype(bf16)
    head_pad = jnp.pad(pre_head[: CONV - 1], ((CONV - 1, CONV - 1), (0, 0)))
    entering = edge[8 - CONV + 1 :]
    extra = jnp.stack([
        jnp.sum(entering[:, :inner] * head_pad[CONV - 1 - k : 2 * (CONV - 1) - k], axis=0)
        for k in range(CONV)
    ])
    bc_in = jnp.concatenate([entering[:, inner:], bc_raw.astype(f32)], axis=0)
    grad_conv_bc = jnp.stack([jnp.sum(grad_pre_bc * bc_in[k : k + length], axis=0) for k in range(CONV)])
    grad_conv_bc_bias = jnp.sum(grad_pre_bc, axis=0)

    sigma = jax.nn.sigmoid(dt_in)
    g_dt = gstep * sigma
    grad_dt_bias = jnp.sum(g_dt, axis=0)
    g_dt = g_dt.astype(bf16)
    grad_a_log = rate_acc[0] * rate_row[0]

    g_xdt = jnp.concatenate([gx, g_dt], axis=1)
    full_xdt = full_cat[:, : inner + LANES]

    def partial_of(m):
        rank = line.target(m)
        return dot_t(block(grad_z, rank), full_z) + dot_t(block(g_xdt, rank), full_xdt)

    _, all_others = lax.optimization_barrier((gx_last, all_others))
    gn = line.sum_pieces(partial_of)
    gn = gn + dot_t(block(gbc, line.me), full_cat[:, inner + LANES :])

    out_own = dot_t(block(gated_out, line.me), full_out)
    if ranks > 1:
        out_own = out_own + dot_t(jnp.concatenate(mixed, axis=1), ring.join(all_others))
    block_own = (block(block_input, line.me).astype(f32) + out_own).astype(bf16)
    pieces = line.all_pieces(block_own)
    block_output = jnp.zeros((length, width), bf16)
    for m in range(ranks):
        block_output = lax.dynamic_update_slice_in_dim(
            block_output, pieces[m], line.source(m) * quarter, 0
        )

    x_own, inv_own = block(x_float, line.me), block(inverse, line.me)
    scaled = norm_gain * gn
    delta = inv_own * scaled - x_own * (inv_own * inv_own * inv_own) * jnp.mean(
        scaled * x_own, axis=1, keepdims=True
    )
    delta = delta.astype(bf16)
    grad_norm_gain = jnp.sum(gn * x_own * inv_own, axis=0)
    pieces = line.all_pieces(delta)
    input_grad = jnp.zeros((length, width), f32)
    for m in range(ranks):
        rank = line.source(m)
        input_grad = lax.dynamic_update_slice_in_dim(
            input_grad,
            block(out_cotangent, rank).astype(f32) + pieces[m].astype(f32),
            rank * quarter,
            0,
        )

    g_cat = jnp.concatenate([g_xdt, gbc], axis=1)
    grad_w_cat = dot_tn(normed, g_cat)
    summed_cat = ring.reduce_rows(grad_w_cat)
    summed_cat = range_ring.reduce_rows(summed_cat)

    last = jnp.pad(jnp.concatenate([grad_dt_bias[:LANES], grad_a_log]), (0, inner - 2 * LANES))[None, :]
    packed = jnp.concatenate(
        [
            jnp.concatenate([conv_acc[:CONV] + extra, conv_acc[CONV : CONV + 1], gate_acc[:2], last], axis=0),
            jnp.concatenate(
                [grad_conv_bc, grad_conv_bc_bias[None, :], jnp.zeros((3, 2 * STATE), f32)], axis=0
            ),
        ],
        axis=1,
    )
    wide_lanes = packed.shape[1]
    spare = (-width) % wide_lanes
    gain_rows = jnp.pad(grad_norm_gain, (0, spare)).reshape(-1, wide_lanes)
    packed = lax.psum(jnp.concatenate([packed, gain_rows], axis=0), (SHARD, CONTEXT))
    gain_rows = packed[8:]
    parts = [gain_rows] + [line.send(gain_rows, m) for m in range(1, ranks)]
    ordered = jnp.zeros((ranks,) + gain_rows.shape, f32)
    for m in range(ranks):
        ordered = lax.dynamic_update_slice_in_dim(ordered, parts[m][None], line.source(m), 0)
    sum_norm_gain = jnp.sum(ordered, axis=0).reshape(-1)[:width]
    return (
        block_output,
        input_grad,
        summed_z,
        summed_cat[:, :inner],
        summed_cat[:, inner + LANES :],
        summed_cat[:, inner : inner + heads],
        summed_out,
        sum_norm_gain,
        packed[:CONV, :inner],
        packed[CONV, :inner],
        packed[:CONV, inner:],
        packed[CONV, inner:],
        packed[7, :heads],
        packed[7, LANES : LANES + heads],
        jnp.sum(packed[6, :inner].reshape(heads, HEAD_DIM), axis=1),
        packed[5, :inner],
    )


def solution(mesh):
    in_specs = (
        P((SHARD, CONTEXT), None),
        P(),
        P(SHARD, TENSOR),
        P(SHARD, TENSOR),
        P(SHARD, None),
        P(SHARD, TENSOR),
        P(None, TENSOR),
        P(TENSOR),
        P(),
        P(),
        P(TENSOR),
        P(TENSOR),
        P(TENSOR),
        P(TENSOR),
        P(TENSOR, SHARD),
        P((SHARD, CONTEXT), None),
    )
    out_specs = (
        P((SHARD, CONTEXT), None),
        P((SHARD, CONTEXT), None),
        P((SHARD, CONTEXT), TENSOR),
        P((SHARD, CONTEXT), TENSOR),
        P((SHARD, CONTEXT), None),
        P((SHARD, CONTEXT), TENSOR),
        P(TENSOR, (SHARD, CONTEXT)),
        P(),
        P(None, TENSOR),
        P(TENSOR),
        P(),
        P(),
        P(TENSOR),
        P(TENSOR),
        P(TENSOR),
        P(TENSOR),
    )
    return jax.shard_map(body, mesh=mesh, in_specs=in_specs, out_specs=out_specs, check_vma=False)
```

```python
import functools

import jax
import jax.numpy as jnp
from jax import lax
from jax.experimental import pallas as pl
from jax.experimental.layout import Layout, with_layout_constraint
from jax.experimental.pallas import tpu as pltpu
from jax.sharding import PartitionSpec as P


HEADS = 48
HEAD_DIM = 64
STATE = 128
CONV = 4
SPAN = 128
LANES = 128

epsilon = 1e-05
SHARD = "shard"
CONTEXT = "context"
TENSOR = "tensor"
f32 = jnp.float32
bf16 = jnp.bfloat16


def split(v):
    hi = v.astype(bf16)
    return hi, (v - hi.astype(f32)).astype(bf16)


def dot(a, b):
    return lax.dot_general(a, b, (((1,), (0,)), ((), ())), preferred_element_type=f32)


def dot_t(a, b):
    return lax.dot_general(a, b, (((1,), (1,)), ((), ())), preferred_element_type=f32)


def dot_tn(a, b):
    return lax.dot_general(a, b, (((0,), (0,)), ((), ())), preferred_element_type=f32)


def lhs3(parts):
    hi, lo = parts
    return jnp.concatenate([hi, lo, hi], axis=1)


def rhs3(parts):
    hi, lo = parts
    return jnp.concatenate([hi, hi, lo], axis=0)


def rhs3_t(parts):
    hi, lo = parts
    return jnp.concatenate([hi, hi, lo], axis=1)


def spread(values, spread_mat):
    hi, lo = split(values)
    return dot(jnp.concatenate([hi, lo], axis=1), spread_mat)


def gather_heads(values, gather_mat):
    hi, lo = split(values)
    return dot(jnp.concatenate([hi, lo], axis=1), gather_mat)


def tri_sum(tri2, values):
    hi, lo = split(values)
    return dot(tri2, jnp.concatenate([hi, lo], axis=0))


def sigmoid(v):
    return 1.0 / (1.0 + jnp.exp(-v))


def slope_of(v, sigma):
    return sigma * (1.0 + v * (1.0 - sigma))


def front_kernel(x_ref, bc_ref, edge_ref, cw_ref, cb_ref, step_ref, rate_ref, spread_ref, tri_ref,
                 pre_ref, act_ref, cum_ref, state_ref, total_ref, ext, state):
    c = pl.program_id(0)
    rows, inner = x_ref.shape
    wide = cw_ref.shape[1]

    @pl.when(c == 0)
    def _():
        ext[0:8, :] = edge_ref[...]
        state[...] = jnp.zeros_like(state)
        total_ref[...] = jnp.zeros_like(total_ref)

    ext[8 : 8 + rows, 0:inner] = x_ref[...].astype(f32)
    ext[8 : 8 + rows, inner:wide] = bc_ref[...].astype(f32)
    pre = cb_ref[...] + cw_ref[0:1, :] * ext[5 : 5 + rows, :]
    for k in range(1, CONV):
        pre = pre + cw_ref[k : k + 1, :] * ext[5 + k : 5 + k + rows, :]
    ext[0:8, :] = ext[rows : rows + 8, :]
    act = pre * sigmoid(pre)
    pre_ref[...] = pre
    act_ref[...] = act
    step = step_ref[...]
    cum = tri_sum(tri_ref[...], -step * rate_ref[...])
    cum_ref[...] = cum
    total = cum[rows - 1 : rows, :]
    b_t = jnp.transpose(act[:, inner : inner + STATE])
    weight = spread(step * jnp.exp(total - cum), spread_ref[...])
    decay = spread(jnp.broadcast_to(jnp.exp(total), (8, LANES)), spread_ref[...])[0:1, :]
    new = decay * state[...] + dot(lhs3(split(b_t)), rhs3(split(act[:, 0:inner] * weight)))
    state[...] = new
    state_ref[...] = new
    total_ref[...] = total_ref[...] + jnp.broadcast_to(total, (8, LANES))


def forward_kernel(act_ref, step_ref, cum_ref, z_ref, ggo_ref, s_in_ref, d_ref, gain_ref, spread_ref,
                   mixer_ref, enter_ref, exit_ref, sums_ref, state):
    c = pl.program_id(0)
    rows, inner = z_ref.shape

    @pl.when(c == 0)
    def _():
        state[...] = s_in_ref[...]

    heads = inner // HEAD_DIM
    per = LANES // HEAD_DIM
    spread_mat = spread_ref[...]
    x = act_ref[:, 0:inner]
    b_mat = act_ref[:, inner : inner + STATE]
    c_mat = act_ref[:, inner + STATE : inner + 2 * STATE]
    step = step_ref[...]
    cum = cum_ref[...]
    cum_t = jnp.transpose(cum)
    total = cum[rows - 1 : rows, :]
    wide = spread(
        jnp.concatenate([step, step * jnp.exp(total - cum), jnp.exp(cum)], axis=0), spread_mat
    )
    decay = spread(jnp.broadcast_to(jnp.exp(total), (8, LANES)), spread_mat)[0:1, :]
    x_step = x * wide[0:rows]
    c3 = lhs3(split(c_mat))
    scores = dot_t(c3, rhs3_t(split(b_mat)))
    enter = state[...]
    enter_ref[...] = enter
    outer = dot(c3, rhs3(split(enter))) * wide[2 * rows : 3 * rows]
    lower = lax.broadcasted_iota(jnp.int32, (rows, rows), 0) >= lax.broadcasted_iota(
        jnp.int32, (rows, rows), 1
    )
    lane = lax.broadcasted_iota(jnp.int32, (rows, LANES), 1)
    masked = jnp.where(lower, scores, 0.0)
    tiles = []
    for tile in range(heads // per):
        value = rhs3(split(x_step[:, tile * LANES : (tile + 1) * LANES]))
        got = None
        for j in range(per):
            h = tile * per + j
            gap = cum[:, h : h + 1] - cum_t[h : h + 1, :]
            part = dot(lhs3(split(jnp.exp(jnp.minimum(gap, 0.0)) * masked)), value)
            got = part if got is None else jnp.where(lane >= j * HEAD_DIM, part, got)
        tiles.append(got)
    inner_out = jnp.concatenate(tiles, axis=1)
    mixer = inner_out + outer + d_ref[...] * x
    mixer_ref[...] = mixer
    b_t = jnp.transpose(b_mat)
    new = decay * enter + dot(lhs3(split(b_t)), rhs3(split(x * wide[rows : 2 * rows])))
    state[...] = new
    exit_ref[...] = new
    z = z_ref[...]
    gated = mixer * (z * sigmoid(z))
    square = jnp.sum(gated * gated, axis=1, keepdims=True)
    term = jnp.sum(gain_ref[...] * ggo_ref[...] * gated, axis=1, keepdims=True)
    both = jnp.where(lane == 0, square, term)
    sums_ref[...] = jnp.transpose(both)[0:8, :]


def gate_kernel(inner_width, mixer_ref, z_ref, ggo_ref, sums_ref, act_ref, cum_ref, gain_ref, spread_ref,
                out_ref, gm_ref, gz_ref, own_ref, acc_ref, state):
    c = pl.program_id(0)
    rows, inner = z_ref.shape

    @pl.when(c == 0)
    def _():
        state[...] = jnp.zeros_like(state)
        acc_ref[...] = jnp.zeros_like(acc_ref)

    spread_mat = spread_ref[...]
    columns = jnp.transpose(jnp.concatenate([sums_ref[...]] * (LANES // 8), axis=0))
    inverse = lax.rsqrt(columns[:, 0:1] / inner_width + epsilon)
    term = columns[:, 1:2] / inner_width
    mixer = mixer_ref[...]
    z = z_ref[...]
    sigma = sigmoid(z)
    gate = z * sigma
    gated = mixer * gate
    ggo = ggo_ref[...]
    normal = gated * inverse
    out_ref[...] = (normal * gain_ref[...]).astype(bf16)
    grad_gated = inverse * (gain_ref[...] * ggo) - normal * (inverse * inverse * term)
    gm = grad_gated * gate
    gm_ref[...] = gm
    gz_ref[...] = (grad_gated * mixer * slope_of(z, sigma)).astype(bf16)
    x = act_ref[:, 0:inner]
    c_mat = act_ref[:, inner + STATE : inner + 2 * STATE]
    acc_ref[0:1, :] += jnp.sum(ggo * normal, axis=0, keepdims=True)
    acc_ref[1:2, :] += jnp.sum(gm * x, axis=0, keepdims=True)
    cum = cum_ref[...]
    total = cum[rows - 1 : rows, :]
    grown = spread(jnp.exp(cum), spread_mat)
    decay = spread(jnp.broadcast_to(jnp.exp(total), (8, LANES)), spread_mat)[0:1, :]
    new = decay * state[...] + dot(
        lhs3(split(jnp.transpose(c_mat))), rhs3(split(gm * grown))
    )
    state[...] = new
    own_ref[...] = new


def backward_kernel(gm_ref, act_ref, pre_ref, step_ref, cum_ref, mixer_ref, enter_ref, exit_ref, carried_ref,
                    x_raw_ref, cw_ref, d_ref, rate_ref, spread_ref, gather_ref, upper_ref,
                    gx_ref, tail_ref, head_ref, dbc_ref, gstep_ref, conv_ref, rate_out_ref,
                    state, ext):
    c = pl.program_id(0)
    rows, inner = gm_ref.shape

    @pl.when(c == 0)
    def _():
        state[...] = carried_ref[...]
        ext[rows : rows + 8, :] = jnp.zeros((8, inner), f32)
        conv_ref[...] = jnp.zeros_like(conv_ref)
        rate_out_ref[...] = jnp.zeros_like(rate_out_ref)

    heads = inner // HEAD_DIM
    per = LANES // HEAD_DIM
    spread_mat = spread_ref[...]
    gather_mat = gather_ref[...]
    gm = gm_ref[...]
    x = act_ref[:, 0:inner]
    b_mat = act_ref[:, inner : inner + STATE]
    c_mat = act_ref[:, inner + STATE : inner + 2 * STATE]
    step = step_ref[...]
    cum = cum_ref[...]
    cum_t = jnp.transpose(cum)
    total = cum[rows - 1 : rows, :]
    wide = spread(
        jnp.concatenate([step, jnp.exp(total - cum), jnp.exp(cum)], axis=0), spread_mat
    )
    step_wide, tail_wide, grown = wide[0:rows], wide[rows : 2 * rows], wide[2 * rows : 3 * rows]
    decay = spread(jnp.broadcast_to(jnp.exp(total), (8, LANES)), spread_mat)[0:1, :]
    x_step = x * step_wide
    b_parts, c_parts = split(b_mat), split(c_mat)
    b3 = lhs3(b_parts)
    scores_t = dot_t(b3, rhs3_t(c_parts))
    grad_exit = state[...]
    exit_parts = split(grad_exit)
    upper = lax.broadcasted_iota(jnp.int32, (rows, rows), 1) >= lax.broadcasted_iota(
        jnp.int32, (rows, rows), 0
    )
    lane = lax.broadcasted_iota(jnp.int32, (rows, LANES), 1)
    through = dot(b3, rhs3(exit_parts)) * tail_wide
    gm_hi, gm_lo = split(gm)
    xs_hi, xs_lo = split(x_step)
    tiles = []
    grad_scores = jnp.zeros((rows, rows), f32)
    zero = jnp.zeros((rows, LANES), bf16)
    for tile in range(heads // per):
        cut = slice(tile * LANES, (tile + 1) * LANES)
        g_hi, g_lo = gm_hi[:, cut], gm_lo[:, cut]
        g_rows = jnp.concatenate([g_hi, g_hi, g_lo], axis=0)
        g_lanes = jnp.concatenate([g_hi, g_hi, g_lo], axis=1)
        got = None
        for j in range(per):
            h = tile * per + j
            keep = (lane >= j * HEAD_DIM) & (lane < (j + 1) * HEAD_DIM)
            xh = jnp.where(keep, xs_hi[:, cut], zero)
            xl = jnp.where(keep, xs_lo[:, cut], zero)
            gap = cum_t[h : h + 1, :] - cum[:, h : h + 1]
            span = jnp.where(upper, jnp.exp(jnp.minimum(gap, 0.0)), 0.0)
            pairs = dot_t(jnp.concatenate([xh, xl, xh], axis=1), g_lanes)
            grad_scores = grad_scores + span * pairs
            part = dot(lhs3(split(span * scores_t)), g_rows)
            got = part if got is None else jnp.where(lane >= j * HEAD_DIM, part, got)
        tiles.append(got)
    grad_xs = jnp.concatenate(tiles, axis=1) + through
    scores_parts = split(grad_scores)
    weighted = gm * grown
    weighted_parts = split(weighted)
    enter_parts = split(enter_ref[...])
    grad_b = dot(lhs3(scores_parts), rhs3(c_parts)) + dot_t(
        lhs3(split(x_step * tail_wide)), rhs3_t(exit_parts)
    )
    grad_c = dot(lhs3(split(jnp.transpose(grad_scores))), rhs3(b_parts)) + dot_t(
        lhs3(weighted_parts), rhs3_t(enter_parts)
    )
    dbc_ref[:, 0:STATE] = grad_b
    dbc_ref[:, STATE : 2 * STATE] = grad_c
    lost = jnp.sum(grad_exit * exit_ref[...], axis=0, keepdims=True)
    state[...] = decay * grad_exit + dot(
        lhs3(split(jnp.transpose(c_mat))), rhs3(weighted_parts)
    )
    ssd = mixer_ref[...] - d_ref[...] * x
    heads_sum = gather_heads(
        jnp.concatenate([gm * ssd, x * grad_xs, jnp.broadcast_to(lost, (8, inner))], axis=0), gather_mat
    )
    by_step = heads_sum[rows : 2 * rows]
    grad_log = tri_sum(upper_ref[...], heads_sum[0:rows] - step * by_step) + heads_sum[
        2 * rows : 2 * rows + 1
    ]
    gstep_ref[...] = by_step - rate_ref[...] * grad_log
    rate_out_ref[0:1, :] += -jnp.sum(grad_log * step, axis=0, keepdims=True)
    pre = pre_ref[...]
    grad_pre = (grad_xs * step_wide + d_ref[...] * gm) * slope_of(pre, sigmoid(pre))
    ext[0:rows, :] = grad_pre
    raw = x_raw_ref[...].astype(f32)
    conv_ref[CONV : CONV + 1, :] += jnp.sum(grad_pre, axis=0, keepdims=True)
    total_in = None
    for k in range(CONV):
        moved = ext[CONV - 1 - k : CONV - 1 - k + rows, :]
        conv_ref[k : k + 1, :] += jnp.sum(moved * raw, axis=0, keepdims=True)
        piece = cw_ref[k : k + 1, :] * moved
        total_in = piece if total_in is None else total_in + piece
    gx_ref[...] = total_in.astype(bf16)

    @pl.when(c == 0)
    def _():
        tail_ref[...] = total_in[rows - 8 : rows, :]

    head_ref[...] = grad_pre[0:8, :]
    ext[rows : rows + 8, :] = grad_pre[0:8, :]


def shifted(value, axis, by):
    length = lax.axis_size(axis)
    pairs = [(i, i + by) for i in range(length) if 0 <= i + by < length]
    return lax.ppermute(value, axis, pairs)


def chain(local, decay, axis, by):
    got = None
    for _ in range(lax.axis_size(axis) - 1):
        got = shifted(local if got is None else local + decay * got, axis, by)
    return jnp.zeros_like(local) if got is None else got


class Ring:
    def __init__(self, axis):
        self.axis = axis
        self.size = lax.axis_size(axis)
        self.me = lax.axis_index(axis)
        self.paired = self.size & (self.size - 1) == 0

    def target(self, m):
        return self.me ^ m if self.paired else (self.me + m) % self.size

    def source(self, m):
        return self.me ^ m if self.paired else (self.me - m) % self.size

    def send(self, value, m):
        pairs = [(i, i ^ m if self.paired else (i + m) % self.size) for i in range(self.size)]
        return lax.ppermute(value, self.axis, pairs)

    def far(self, value):
        if self.size == 1 or not self.paired:
            return {0: value}
        return {0: value, self.size // 2: self.send(value, self.size // 2)}

    def near(self, pieces):
        step = self.size // 4
        while step and self.paired:
            pieces = {**pieces, **{m | step: self.send(piece, step) for m, piece in pieces.items()}}
            step //= 2
        return pieces

    def join(self, pieces):
        value = pieces[0]
        if self.paired:
            rows = value.shape[0]
            full = jnp.zeros((rows * self.size,) + value.shape[1:], value.dtype)
            for m, piece in pieces.items():
                full = lax.dynamic_update_slice_in_dim(full, piece, self.source(m) * rows, 0)
        else:
            full = lax.all_gather(value, self.axis, axis=0, tiled=True)
        return with_layout_constraint(full, Layout((0, 1)))

    def reduce_rows(self, value):
        if not self.paired:
            return lax.psum_scatter(value, self.axis, scatter_dimension=0, tiled=True)
        rows, step = value.shape[0] // self.size, 1
        value = with_layout_constraint(value, Layout((0, 1)))
        parts = {m: lax.dynamic_slice_in_dim(value, self.target(m) * rows, rows) for m in range(self.size)}
        while step < self.size:
            parts = {
                m: part + self.send(parts[m | step], step) for m, part in parts.items() if not m & step
            }
            step *= 2
        return parts[0]

    def sum_pieces(self, piece):
        if self.size != 4:
            got = [self.send(piece(m).astype(bf16), m) for m in range(1, self.size)]
            total = piece(0)
            for value in got:
                total = total + value.astype(f32)
            return total
        far = piece(3).astype(bf16)
        handed = lax.ppermute(far, self.axis, [(0, 1), (3, 2)])
        middle = lax.ppermute(far, self.axis, [(1, 2), (2, 1)])
        near = self.send(piece(1).astype(bf16), 1)
        across = self.send((piece(2) + handed.astype(f32)).astype(bf16), 2)
        total = piece(0)
        for value in (middle, near, across):
            total = total + value.astype(f32)
        return total

    def all_pieces(self, own):
        if self.size != 4:
            return [own] + [self.send(own, m) for m in range(1, self.size)]
        across = self.send(own, 2)
        near = self.send(own, 1)
        middle = lax.ppermute(own, self.axis, [(1, 2), (2, 1)])
        handed = lax.ppermute(across, self.axis, [(1, 0), (2, 3)])
        return [own, near, across, middle + handed]


def body(
    block_input,
    norm_gain,
    w_z,
    w_x,
    w_bc,
    w_dt,
    conv_x_weight,
    conv_x_bias,
    conv_bc_weight,
    conv_bc_bias,
    dt_bias,
    a_log,
    d_skip,
    gate_gain,
    w_out,
    out_cotangent,
):
    length, width = block_input.shape
    inner = w_z.shape[1]
    heads = w_dt.shape[1]
    wide = inner + 2 * STATE
    inner_width = HEADS * HEAD_DIM
    line = Ring(TENSOR)
    ranks = line.size
    quarter = length // ranks
    rows = min(SPAN, length)
    count = length // rows

    w_cat = jnp.concatenate([w_x, jnp.pad(w_dt, ((0, 0), (0, LANES - heads))), w_bc], axis=1)
    ring, range_ring = Ring(SHARD), Ring(CONTEXT)
    w_out_t = w_out.T
    full_cat = ring.join(ring.near(ring.far(w_cat)))
    others = [line.send(w_out_t, m) for m in range(1, ranks)]
    far_z = ring.far(w_z)
    far_out = ring.far(w_out_t)

    x_float = block_input.astype(f32)
    inverse = lax.rsqrt(jnp.mean(x_float * x_float, axis=1, keepdims=True) + epsilon)
    normed = (x_float * inverse * norm_gain).astype(bf16)
    proj = jnp.dot(normed, full_cat, preferred_element_type=f32)
    x_raw = proj[:, :inner].astype(bf16)
    dt_raw = proj[:, inner : inner + LANES]
    bc_raw = proj[:, inner + LANES :].astype(bf16)

    edge = shifted(
        jnp.concatenate([x_raw[length - CONV + 1 :], bc_raw[length - CONV + 1 :]], axis=1), CONTEXT, 1
    ).astype(f32)
    edge = jnp.pad(edge, ((8 - CONV + 1, 0), (0, 0)))
    conv_weight = jnp.concatenate([conv_x_weight, conv_bc_weight], axis=1)
    conv_bias = jnp.concatenate([conv_x_bias, conv_bc_bias])[None, :]
    dt_in = dt_raw + jnp.pad(dt_bias, (0, LANES - heads))
    step = jax.nn.softplus(dt_in)
    decay_rate = jnp.exp(a_log)
    rate_row = jnp.pad(decay_rate, (0, LANES - heads))[None, :]
    d_row = jnp.repeat(d_skip, HEAD_DIM)[None, :]
    gain_row = gate_gain[None, :]
    owner = jnp.arange(inner) // HEAD_DIM
    one_hot = (jnp.arange(LANES)[:, None] == owner[None, :]).astype(bf16)
    spread_mat = jnp.concatenate([one_hot, one_hot], axis=0)
    one_hot_t = (owner[:, None] == jnp.arange(LANES)[None, :]).astype(bf16)
    gather_mat = jnp.concatenate([one_hot_t, one_hot_t], axis=0)
    place = jnp.arange(rows)
    lower = (place[:, None] >= place[None, :]).astype(bf16)
    lower2 = jnp.concatenate([lower, lower], axis=1)
    upper = (place[:, None] <= place[None, :]).astype(bf16)
    upper2 = jnp.concatenate([upper, upper], axis=1)

    def whole(shape):
        return pl.BlockSpec(shape, lambda c: (0,) * len(shape))

    def ahead(lanes, high=rows):
        return pl.BlockSpec((high, lanes), lambda c: (c, 0))

    def back(lanes, high=rows):
        return pl.BlockSpec((high, lanes), lambda c: (count - 1 - c, 0))

    def shape(*dims, dtype=f32):
        return jax.ShapeDtypeStruct(dims, dtype)

    params = pltpu.CompilerParams(dimension_semantics=("arbitrary",))

    pre, act, cum, s_local, totals = pl.pallas_call(
        front_kernel,
        grid=(count,),
        in_specs=[
            ahead(inner), ahead(2 * STATE), whole((8, wide)), whole((CONV, wide)), whole((1, wide)),
            ahead(LANES), whole((1, LANES)), whole((2 * LANES, inner)), whole((rows, 2 * rows)),
        ],
        out_specs=[ahead(wide), ahead(wide), ahead(LANES), whole((STATE, inner)), whole((8, LANES))],
        out_shape=[
            shape(length, wide), shape(length, wide), shape(length, LANES), shape(STATE, inner),
            shape(8, LANES),
        ],
        scratch_shapes=[pltpu.VMEM((rows + 8, wide), f32), pltpu.VMEM((STATE, inner), f32)],
        compiler_params=params,
        name="front",
    )(x_raw, bc_raw, edge, conv_weight, conv_bias, step, rate_row, spread_mat, lower2)
    decay = jnp.repeat(jnp.exp(totals[0, :heads]), HEAD_DIM)[None, :]
    s_in = chain(s_local, decay, CONTEXT, 1)
    totals, far_z, far_out, others = lax.optimization_barrier((totals, far_z, far_out, others))
    full_z = ring.join(ring.near(far_z))
    full_out = ring.join(ring.near(far_out))
    all_others = ring.near(ring.far(jnp.concatenate(others, axis=1)))
    z_part = dot(normed, full_z)
    ggo = jnp.dot(out_cotangent, full_out, preferred_element_type=f32)
    mixer, enter, leave, sums = pl.pallas_call(
        forward_kernel,
        grid=(count,),
        in_specs=[
            ahead(wide), ahead(LANES), ahead(LANES), ahead(inner), ahead(inner), whole((STATE, inner)),
            whole((1, inner)), whole((1, inner)), whole((2 * LANES, inner)),
        ],
        out_specs=[
            ahead(inner), ahead(inner, STATE), ahead(inner, STATE), pl.BlockSpec((8, rows), lambda c: (0, c)),
        ],
        out_shape=[
            shape(length, inner), shape(count * STATE, inner), shape(count * STATE, inner), shape(8, length),
        ],
        scratch_shapes=[pltpu.VMEM((STATE, inner), f32)],
        compiler_params=params,
        name="forward",
    )(act, step, cum, z_part, ggo, s_in, d_row, gain_row, spread_mat)
    parts = [line.send(sums, m) for m in range(1, ranks)]
    for part in parts:
        sums = sums + part

    gated_out, gm, grad_z, own, gate_acc = pl.pallas_call(
        functools.partial(gate_kernel, inner_width),
        grid=(count,),
        in_specs=[
            back(inner), back(inner), back(inner), pl.BlockSpec((8, rows), lambda c: (0, count - 1 - c)),
            back(wide), back(LANES), whole((1, inner)), whole((2 * LANES, inner)),
        ],
        out_specs=[back(inner), back(inner), back(inner), whole((STATE, inner)), whole((8, inner))],
        out_shape=[
            shape(length, inner, dtype=bf16), shape(length, inner), shape(length, inner, dtype=bf16),
            shape(STATE, inner), shape(8, inner),
        ],
        scratch_shapes=[pltpu.VMEM((STATE, inner), f32)],
        compiler_params=params,
        name="gate",
    )(mixer, z_part, ggo, sums, act, cum, gain_row, spread_mat)
    carried = chain(own, decay, CONTEXT, -1)

    def block(value, rank):
        return lax.dynamic_slice_in_dim(value, rank * quarter, quarter)

    mixed = [line.send(block(gated_out, line.target(m)), m) for m in range(1, ranks)]
    grad_w_out = dot_tn(out_cotangent, gated_out)
    grad_w_z = dot_tn(normed, grad_z)
    summed_out, summed_z = ring.reduce_rows(grad_w_out), ring.reduce_rows(grad_w_z)
    summed_out, summed_z = range_ring.reduce_rows(summed_out).T, range_ring.reduce_rows(summed_z)

    gx, gx_tail, pre_head, dbc, gstep, conv_acc, rate_acc = pl.pallas_call(
        backward_kernel,
        grid=(count,),
        in_specs=[
            back(inner), back(wide), back(inner), back(LANES), back(LANES), back(inner),
            back(inner, STATE), back(inner, STATE), whole((STATE, inner)), back(inner), whole((CONV, inner)),
            whole((1, inner)), whole((1, LANES)), whole((2 * LANES, inner)), whole((2 * inner, LANES)),
            whole((rows, 2 * rows)),
        ],
        out_specs=[
            back(inner), whole((8, inner)), whole((8, inner)), back(2 * STATE), back(LANES), whole((8, inner)),
            whole((8, LANES)),
        ],
        out_shape=[
            shape(length, inner, dtype=bf16), shape(8, inner), shape(8, inner), shape(length, 2 * STATE),
            shape(length, LANES), shape(8, inner), shape(8, LANES),
        ],
        scratch_shapes=[pltpu.VMEM((STATE, inner), f32), pltpu.VMEM((rows + 8, inner), f32)],
        compiler_params=params,
        name="backward",
    )(gm, act, pre, step, cum, mixer, enter, leave, carried, x_raw, conv_x_weight, d_row, rate_row,
      spread_mat, gather_mat, upper2)

    got = [line.send(block(dbc, line.target(m)), m) for m in range(1, ranks)]
    bc_own = block(dbc, line.me)
    for value in got:
        bc_own = bc_own + value
    pieces = [bc_own] + [line.send(bc_own, m) for m in range(1, ranks)]
    for m in range(ranks):
        dbc = lax.dynamic_update_slice_in_dim(dbc, pieces[m], line.source(m) * quarter, 0)
    pre_bc = pre[:, inner:]
    grad_pre_bc = dbc * slope_of(pre_bc, jax.nn.sigmoid(pre_bc))
    next_head = shifted(pre_head[: CONV - 1], CONTEXT, -1)
    next_bc_head = shifted(grad_pre_bc[: CONV - 1], CONTEXT, -1)
    after = jnp.pad(next_head, ((CONV - 1, CONV - 1), (0, 0)))
    reach = jnp.zeros((CONV - 1, inner), f32)
    for k in range(CONV):
        reach = reach + conv_x_weight[k] * after[CONV - 1 - k : 2 * (CONV - 1) - k]
    gx_last = (gx_tail + jnp.pad(reach, ((8 - CONV + 1, 0), (0, 0)))).astype(bf16)
    gx = lax.dynamic_update_slice_in_dim(gx, gx_last, length - 8, 0)
    bc_pad = jnp.concatenate([grad_pre_bc, next_bc_head], axis=0)
    gbc = jnp.zeros((length, 2 * STATE), f32)
    for k in range(CONV):
        gbc = gbc + conv_bc_weight[k] * bc_pad[CONV - 1 - k : CONV - 1 - k + length]
    gbc = gbc.astype(bf16)
    head_pad = jnp.pad(pre_head[: CONV - 1], ((CONV - 1, CONV - 1), (0, 0)))
    entering = edge[8 - CONV + 1 :]
    extra = jnp.stack([
        jnp.sum(entering[:, :inner] * head_pad[CONV - 1 - k : 2 * (CONV - 1) - k], axis=0)
        for k in range(CONV)
    ])
    bc_in = jnp.concatenate([entering[:, inner:], bc_raw.astype(f32)], axis=0)
    grad_conv_bc = jnp.stack([jnp.sum(grad_pre_bc * bc_in[k : k + length], axis=0) for k in range(CONV)])
    grad_conv_bc_bias = jnp.sum(grad_pre_bc, axis=0)

    sigma = jax.nn.sigmoid(dt_in)
    g_dt = gstep * sigma
    grad_dt_bias = jnp.sum(g_dt, axis=0)
    g_dt = g_dt.astype(bf16)
    grad_a_log = rate_acc[0] * rate_row[0]

    gx, late_z = lax.optimization_barrier((gx, grad_z))
    g_xdt = jnp.concatenate([gx, g_dt], axis=1)
    grad_w_xdt = dot_tn(normed, g_xdt)
    summed_xdt = ring.reduce_rows(grad_w_xdt)
    summed_xdt = range_ring.reduce_rows(summed_xdt)
    full_xdt = full_cat[:, : inner + LANES]

    def partial_of(m):
        rank = line.target(m)
        return dot_t(block(late_z, rank), full_z) + dot_t(block(g_xdt, rank), full_xdt)

    _, all_others = lax.optimization_barrier((gx_last, all_others))
    gn = line.sum_pieces(partial_of)
    gn = gn + dot_t(block(gbc, line.me), full_cat[:, inner + LANES :])

    out_own = dot_t(block(gated_out, line.me), full_out)
    if ranks > 1:
        out_own = out_own + dot_t(jnp.concatenate(mixed, axis=1), ring.join(all_others))
    block_own = (block(block_input, line.me).astype(f32) + out_own).astype(bf16)
    pieces = line.all_pieces(block_own)
    block_output = jnp.zeros((length, width), bf16)
    for m in range(ranks):
        block_output = lax.dynamic_update_slice_in_dim(
            block_output, pieces[m], line.source(m) * quarter, 0
        )

    x_own, inv_own = block(x_float, line.me), block(inverse, line.me)
    scaled = norm_gain * gn
    delta = inv_own * scaled - x_own * (inv_own * inv_own * inv_own) * jnp.mean(
        scaled * x_own, axis=1, keepdims=True
    )
    delta = delta.astype(bf16)
    grad_norm_gain = jnp.sum(gn * x_own * inv_own, axis=0)
    pieces = line.all_pieces(delta)
    back_pieces = pieces

    summed_bc = ring.reduce_rows(dot_tn(normed, gbc))
    summed_bc = range_ring.reduce_rows(summed_bc)

    last = jnp.pad(jnp.concatenate([grad_dt_bias[:LANES], grad_a_log]), (0, inner - 2 * LANES))[None, :]
    packed = jnp.concatenate(
        [
            jnp.concatenate([conv_acc[:CONV] + extra, conv_acc[CONV : CONV + 1], gate_acc[:2], last], axis=0),
            jnp.concatenate(
                [grad_conv_bc, grad_conv_bc_bias[None, :], jnp.zeros((3, 2 * STATE), f32)], axis=0
            ),
        ],
        axis=1,
    )
    wide_lanes = packed.shape[1]
    spare = (-width) % wide_lanes
    gain_rows = jnp.pad(grad_norm_gain, (0, spare)).reshape(-1, wide_lanes)
    packed = lax.psum(jnp.concatenate([packed, gain_rows], axis=0), (SHARD, CONTEXT))
    gain_rows = packed[8:]
    parts = [gain_rows] + [line.send(gain_rows, m) for m in range(1, ranks)]
    ordered = jnp.zeros((ranks,) + gain_rows.shape, f32)
    for m in range(ranks):
        ordered = lax.dynamic_update_slice_in_dim(ordered, parts[m][None], line.source(m), 0)
    sum_norm_gain = jnp.sum(ordered, axis=0).reshape(-1)[:width]
    if ranks > 1:
        packed, back_pieces[1] = lax.optimization_barrier((packed, back_pieces[1]))
    input_grad = jnp.zeros((length, width), f32)
    for m in range(ranks):
        rank = line.source(m)
        input_grad = lax.dynamic_update_slice_in_dim(
            input_grad,
            block(out_cotangent, rank).astype(f32) + back_pieces[m].astype(f32),
            rank * quarter,
            0,
        )
    return (
        block_output,
        input_grad,
        summed_z,
        summed_xdt[:, :inner],
        summed_bc,
        summed_xdt[:, inner : inner + heads],
        summed_out,
        sum_norm_gain,
        packed[:CONV, :inner],
        packed[CONV, :inner],
        packed[:CONV, inner:],
        packed[CONV, inner:],
        packed[7, :heads],
        packed[7, LANES : LANES + heads],
        jnp.sum(packed[6, :inner].reshape(heads, HEAD_DIM), axis=1),
        packed[5, :inner],
    )


def solution(mesh):
    in_specs = (
        P((SHARD, CONTEXT), None),
        P(),
        P(SHARD, TENSOR),
        P(SHARD, TENSOR),
        P(SHARD, None),
        P(SHARD, TENSOR),
        P(None, TENSOR),
        P(TENSOR),
        P(),
        P(),
        P(TENSOR),
        P(TENSOR),
        P(TENSOR),
        P(TENSOR),
        P(TENSOR, SHARD),
        P((SHARD, CONTEXT), None),
    )
    out_specs = (
        P((SHARD, CONTEXT), None),
        P((SHARD, CONTEXT), None),
        P((SHARD, CONTEXT), TENSOR),
        P((SHARD, CONTEXT), TENSOR),
        P((SHARD, CONTEXT), None),
        P((SHARD, CONTEXT), TENSOR),
        P(TENSOR, (SHARD, CONTEXT)),
        P(),
        P(None, TENSOR),
        P(TENSOR),
        P(),
        P(),
        P(TENSOR),
        P(TENSOR),
        P(TENSOR),
        P(TENSOR),
    )
    return jax.shard_map(body, mesh=mesh, in_specs=in_specs, out_specs=out_specs, check_vma=False)
```

```python
import functools

import jax
import jax.numpy as jnp
from jax import lax
from jax.experimental import pallas as pl
from jax.experimental.layout import Layout, with_layout_constraint
from jax.experimental.pallas import tpu as pltpu
from jax.sharding import PartitionSpec as P


HEADS = 48
HEAD_DIM = 64
STATE = 128
CONV = 4
SPAN = 128
LANES = 128

epsilon = 1e-05
SHARD = "shard"
CONTEXT = "context"
TENSOR = "tensor"
f32 = jnp.float32
bf16 = jnp.bfloat16


def split(v):
    hi = v.astype(bf16)
    return hi, (v - hi.astype(f32)).astype(bf16)


def dot(a, b):
    return lax.dot_general(a, b, (((1,), (0,)), ((), ())), preferred_element_type=f32)


def dot_t(a, b):
    return lax.dot_general(a, b, (((1,), (1,)), ((), ())), preferred_element_type=f32)


def dot_tn(a, b):
    return lax.dot_general(a, b, (((0,), (0,)), ((), ())), preferred_element_type=f32)


def lhs3(parts):
    hi, lo = parts
    return jnp.concatenate([hi, lo, hi], axis=1)


def rhs3(parts):
    hi, lo = parts
    return jnp.concatenate([hi, hi, lo], axis=0)


def rhs3_t(parts):
    hi, lo = parts
    return jnp.concatenate([hi, hi, lo], axis=1)


def spread(values, spread_mat):
    hi, lo = split(values)
    return dot(jnp.concatenate([hi, lo], axis=1), spread_mat)


def gather_heads(values, gather_mat):
    hi, lo = split(values)
    return dot(jnp.concatenate([hi, lo], axis=1), gather_mat)


def tri_sum(tri2, values):
    hi, lo = split(values)
    return dot(tri2, jnp.concatenate([hi, lo], axis=0))


def sigmoid(v):
    return 1.0 / (1.0 + jnp.exp(-v))


def slope_of(v, sigma):
    return sigma * (1.0 + v * (1.0 - sigma))


def front_kernel(x_ref, bc_ref, edge_ref, cw_ref, cb_ref, step_ref, rate_ref, spread_ref, tri_ref,
                 pre_ref, act_ref, cum_ref, state_ref, total_ref, ext, state):
    c = pl.program_id(0)
    rows, inner = x_ref.shape
    wide = cw_ref.shape[1]

    @pl.when(c == 0)
    def _():
        ext[0:8, :] = edge_ref[...]
        state[...] = jnp.zeros_like(state)
        total_ref[...] = jnp.zeros_like(total_ref)

    ext[8 : 8 + rows, 0:inner] = x_ref[...].astype(f32)
    ext[8 : 8 + rows, inner:wide] = bc_ref[...].astype(f32)
    pre = cb_ref[...] + cw_ref[0:1, :] * ext[5 : 5 + rows, :]
    for k in range(1, CONV):
        pre = pre + cw_ref[k : k + 1, :] * ext[5 + k : 5 + k + rows, :]
    ext[0:8, :] = ext[rows : rows + 8, :]
    act = pre * sigmoid(pre)
    pre_ref[...] = pre
    act_ref[...] = act
    step = step_ref[...]
    cum = tri_sum(tri_ref[...], -step * rate_ref[...])
    cum_ref[...] = cum
    total = cum[rows - 1 : rows, :]
    b_t = jnp.transpose(act[:, inner : inner + STATE])
    weight = spread(step * jnp.exp(total - cum), spread_ref[...])
    decay = spread(jnp.broadcast_to(jnp.exp(total), (8, LANES)), spread_ref[...])[0:1, :]
    new = decay * state[...] + dot(lhs3(split(b_t)), rhs3(split(act[:, 0:inner] * weight)))
    state[...] = new
    state_ref[...] = new
    total_ref[...] = total_ref[...] + jnp.broadcast_to(total, (8, LANES))


def forward_kernel(act_ref, step_ref, cum_ref, z_ref, ggo_ref, s_in_ref, d_ref, gain_ref, spread_ref,
                   mixer_ref, enter_ref, exit_ref, sums_ref, state):
    c = pl.program_id(0)
    rows, inner = z_ref.shape

    @pl.when(c == 0)
    def _():
        state[...] = s_in_ref[...]

    heads = inner // HEAD_DIM
    per = LANES // HEAD_DIM
    spread_mat = spread_ref[...]
    x = act_ref[:, 0:inner]
    b_mat = act_ref[:, inner : inner + STATE]
    c_mat = act_ref[:, inner + STATE : inner + 2 * STATE]
    step = step_ref[...]
    cum = cum_ref[...]
    cum_t = jnp.transpose(cum)
    total = cum[rows - 1 : rows, :]
    wide = spread(
        jnp.concatenate([step, step * jnp.exp(total - cum), jnp.exp(cum)], axis=0), spread_mat
    )
    decay = spread(jnp.broadcast_to(jnp.exp(total), (8, LANES)), spread_mat)[0:1, :]
    x_step = x * wide[0:rows]
    c3 = lhs3(split(c_mat))
    scores = dot_t(c3, rhs3_t(split(b_mat)))
    enter = state[...]
    enter_ref[...] = enter
    outer = dot(c3, rhs3(split(enter))) * wide[2 * rows : 3 * rows]
    lower = lax.broadcasted_iota(jnp.int32, (rows, rows), 0) >= lax.broadcasted_iota(
        jnp.int32, (rows, rows), 1
    )
    lane = lax.broadcasted_iota(jnp.int32, (rows, LANES), 1)
    masked = jnp.where(lower, scores, 0.0)
    tiles = []
    for tile in range(heads // per):
        value = rhs3(split(x_step[:, tile * LANES : (tile + 1) * LANES]))
        got = None
        for j in range(per):
            h = tile * per + j
            gap = cum[:, h : h + 1] - cum_t[h : h + 1, :]
            part = dot(lhs3(split(jnp.exp(jnp.minimum(gap, 0.0)) * masked)), value)
            got = part if got is None else jnp.where(lane >= j * HEAD_DIM, part, got)
        tiles.append(got)
    inner_out = jnp.concatenate(tiles, axis=1)
    mixer = inner_out + outer + d_ref[...] * x
    mixer_ref[...] = mixer
    b_t = jnp.transpose(b_mat)
    new = decay * enter + dot(lhs3(split(b_t)), rhs3(split(x * wide[rows : 2 * rows])))
    state[...] = new
    exit_ref[...] = new
    z = z_ref[...]
    gated = mixer * (z * sigmoid(z))
    square = jnp.sum(gated * gated, axis=1, keepdims=True)
    term = jnp.sum(gain_ref[...] * ggo_ref[...] * gated, axis=1, keepdims=True)
    both = jnp.where(lane == 0, square, term)
    sums_ref[...] = jnp.transpose(both)[0:8, :]


def gate_kernel(inner_width, mixer_ref, z_ref, ggo_ref, sums_ref, act_ref, cum_ref, gain_ref, spread_ref,
                out_ref, gm_ref, gz_ref, own_ref, acc_ref, state):
    c = pl.program_id(0)
    rows, inner = z_ref.shape

    @pl.when(c == 0)
    def _():
        state[...] = jnp.zeros_like(state)
        acc_ref[...] = jnp.zeros_like(acc_ref)

    spread_mat = spread_ref[...]
    columns = jnp.transpose(jnp.concatenate([sums_ref[...]] * (LANES // 8), axis=0))
    inverse = lax.rsqrt(columns[:, 0:1] / inner_width + epsilon)
    term = columns[:, 1:2] / inner_width
    mixer = mixer_ref[...]
    z = z_ref[...]
    sigma = sigmoid(z)
    gate = z * sigma
    gated = mixer * gate
    ggo = ggo_ref[...]
    normal = gated * inverse
    out_ref[...] = (normal * gain_ref[...]).astype(bf16)
    grad_gated = inverse * (gain_ref[...] * ggo) - normal * (inverse * inverse * term)
    gm = grad_gated * gate
    gm_ref[...] = gm
    gz_ref[...] = (grad_gated * mixer * slope_of(z, sigma)).astype(bf16)
    x = act_ref[:, 0:inner]
    c_mat = act_ref[:, inner + STATE : inner + 2 * STATE]
    acc_ref[0:1, :] += jnp.sum(ggo * normal, axis=0, keepdims=True)
    acc_ref[1:2, :] += jnp.sum(gm * x, axis=0, keepdims=True)
    cum = cum_ref[...]
    total = cum[rows - 1 : rows, :]
    grown = spread(jnp.exp(cum), spread_mat)
    decay = spread(jnp.broadcast_to(jnp.exp(total), (8, LANES)), spread_mat)[0:1, :]
    new = decay * state[...] + dot(
        lhs3(split(jnp.transpose(c_mat))), rhs3(split(gm * grown))
    )
    state[...] = new
    own_ref[...] = new


def backward_kernel(gm_ref, act_ref, pre_ref, step_ref, cum_ref, mixer_ref, enter_ref, exit_ref, carried_ref,
                    x_raw_ref, cw_ref, d_ref, rate_ref, spread_ref, gather_ref, upper_ref,
                    gx_ref, tail_ref, head_ref, dbc_ref, gstep_ref, conv_ref, rate_out_ref,
                    state, ext):
    c = pl.program_id(0)
    rows, inner = gm_ref.shape

    @pl.when(c == 0)
    def _():
        state[...] = carried_ref[...]
        ext[rows : rows + 8, :] = jnp.zeros((8, inner), f32)
        conv_ref[...] = jnp.zeros_like(conv_ref)
        rate_out_ref[...] = jnp.zeros_like(rate_out_ref)

    heads = inner // HEAD_DIM
    per = LANES // HEAD_DIM
    spread_mat = spread_ref[...]
    gather_mat = gather_ref[...]
    gm = gm_ref[...]
    x = act_ref[:, 0:inner]
    b_mat = act_ref[:, inner : inner + STATE]
    c_mat = act_ref[:, inner + STATE : inner + 2 * STATE]
    step = step_ref[...]
    cum = cum_ref[...]
    cum_t = jnp.transpose(cum)
    total = cum[rows - 1 : rows, :]
    wide = spread(
        jnp.concatenate([step, jnp.exp(total - cum), jnp.exp(cum)], axis=0), spread_mat
    )
    step_wide, tail_wide, grown = wide[0:rows], wide[rows : 2 * rows], wide[2 * rows : 3 * rows]
    decay = spread(jnp.broadcast_to(jnp.exp(total), (8, LANES)), spread_mat)[0:1, :]
    x_step = x * step_wide
    b_parts, c_parts = split(b_mat), split(c_mat)
    b3 = lhs3(b_parts)
    scores_t = dot_t(b3, rhs3_t(c_parts))
    grad_exit = state[...]
    exit_parts = split(grad_exit)
    upper = lax.broadcasted_iota(jnp.int32, (rows, rows), 1) >= lax.broadcasted_iota(
        jnp.int32, (rows, rows), 0
    )
    lane = lax.broadcasted_iota(jnp.int32, (rows, LANES), 1)
    through = dot(b3, rhs3(exit_parts)) * tail_wide
    gm_hi, gm_lo = split(gm)
    xs_hi, xs_lo = split(x_step)
    tiles = []
    grad_scores = jnp.zeros((rows, rows), f32)
    zero = jnp.zeros((rows, LANES), bf16)
    for tile in range(heads // per):
        cut = slice(tile * LANES, (tile + 1) * LANES)
        g_hi, g_lo = gm_hi[:, cut], gm_lo[:, cut]
        g_rows = jnp.concatenate([g_hi, g_hi, g_lo], axis=0)
        g_lanes = jnp.concatenate([g_hi, g_hi, g_lo], axis=1)
        got = None
        for j in range(per):
            h = tile * per + j
            keep = (lane >= j * HEAD_DIM) & (lane < (j + 1) * HEAD_DIM)
            xh = jnp.where(keep, xs_hi[:, cut], zero)
            xl = jnp.where(keep, xs_lo[:, cut], zero)
            gap = cum_t[h : h + 1, :] - cum[:, h : h + 1]
            span = jnp.where(upper, jnp.exp(jnp.minimum(gap, 0.0)), 0.0)
            pairs = dot_t(jnp.concatenate([xh, xl, xh], axis=1), g_lanes)
            grad_scores = grad_scores + span * pairs
            part = dot(lhs3(split(span * scores_t)), g_rows)
            got = part if got is None else jnp.where(lane >= j * HEAD_DIM, part, got)
        tiles.append(got)
    grad_xs = jnp.concatenate(tiles, axis=1) + through
    scores_parts = split(grad_scores)
    weighted = gm * grown
    weighted_parts = split(weighted)
    enter_parts = split(enter_ref[...])
    grad_b = dot(lhs3(scores_parts), rhs3(c_parts)) + dot_t(
        lhs3(split(x_step * tail_wide)), rhs3_t(exit_parts)
    )
    grad_c = dot(lhs3(split(jnp.transpose(grad_scores))), rhs3(b_parts)) + dot_t(
        lhs3(weighted_parts), rhs3_t(enter_parts)
    )
    dbc_ref[:, 0:STATE] = grad_b
    dbc_ref[:, STATE : 2 * STATE] = grad_c
    lost = jnp.sum(grad_exit * exit_ref[...], axis=0, keepdims=True)
    state[...] = decay * grad_exit + dot(
        lhs3(split(jnp.transpose(c_mat))), rhs3(weighted_parts)
    )
    ssd = mixer_ref[...] - d_ref[...] * x
    heads_sum = gather_heads(
        jnp.concatenate([gm * ssd, x * grad_xs, jnp.broadcast_to(lost, (8, inner))], axis=0), gather_mat
    )
    by_step = heads_sum[rows : 2 * rows]
    grad_log = tri_sum(upper_ref[...], heads_sum[0:rows] - step * by_step) + heads_sum[
        2 * rows : 2 * rows + 1
    ]
    gstep_ref[...] = by_step - rate_ref[...] * grad_log
    rate_out_ref[0:1, :] += -jnp.sum(grad_log * step, axis=0, keepdims=True)
    pre = pre_ref[...]
    grad_pre = (grad_xs * step_wide + d_ref[...] * gm) * slope_of(pre, sigmoid(pre))
    ext[0:rows, :] = grad_pre
    raw = x_raw_ref[...].astype(f32)
    conv_ref[CONV : CONV + 1, :] += jnp.sum(grad_pre, axis=0, keepdims=True)
    total_in = None
    for k in range(CONV):
        moved = ext[CONV - 1 - k : CONV - 1 - k + rows, :]
        conv_ref[k : k + 1, :] += jnp.sum(moved * raw, axis=0, keepdims=True)
        piece = cw_ref[k : k + 1, :] * moved
        total_in = piece if total_in is None else total_in + piece
    gx_ref[...] = total_in.astype(bf16)

    @pl.when(c == 0)
    def _():
        tail_ref[...] = total_in[rows - 8 : rows, :]

    head_ref[...] = grad_pre[0:8, :]
    ext[rows : rows + 8, :] = grad_pre[0:8, :]


def shifted(value, axis, by):
    length = lax.axis_size(axis)
    pairs = [(i, i + by) for i in range(length) if 0 <= i + by < length]
    return lax.ppermute(value, axis, pairs)


def chain(local, decay, axis, by):
    got = None
    for _ in range(lax.axis_size(axis) - 1):
        got = shifted(local if got is None else local + decay * got, axis, by)
    return jnp.zeros_like(local) if got is None else got


class Ring:
    def __init__(self, axis):
        self.axis = axis
        self.size = lax.axis_size(axis)
        self.me = lax.axis_index(axis)
        self.paired = self.size & (self.size - 1) == 0

    def target(self, m):
        return self.me ^ m if self.paired else (self.me + m) % self.size

    def source(self, m):
        return self.me ^ m if self.paired else (self.me - m) % self.size

    def send(self, value, m):
        pairs = [(i, i ^ m if self.paired else (i + m) % self.size) for i in range(self.size)]
        return lax.ppermute(value, self.axis, pairs)

    def far(self, value):
        if self.size == 1 or not self.paired:
            return {0: value}
        return {0: value, self.size // 2: self.send(value, self.size // 2)}

    def near(self, pieces):
        step = self.size // 4
        while step and self.paired:
            pieces = {**pieces, **{m | step: self.send(piece, step) for m, piece in pieces.items()}}
            step //= 2
        return pieces

    def join(self, pieces):
        value = pieces[0]
        if self.paired:
            rows = value.shape[0]
            full = jnp.zeros((rows * self.size,) + value.shape[1:], value.dtype)
            for m, piece in pieces.items():
                full = lax.dynamic_update_slice_in_dim(full, piece, self.source(m) * rows, 0)
        else:
            full = lax.all_gather(value, self.axis, axis=0, tiled=True)
        return with_layout_constraint(full, Layout((0, 1)))

    def reduce_rows(self, value):
        if not self.paired:
            return lax.psum_scatter(value, self.axis, scatter_dimension=0, tiled=True)
        rows, step = value.shape[0] // self.size, 1
        value = with_layout_constraint(value, Layout((0, 1)))
        parts = {m: lax.dynamic_slice_in_dim(value, self.target(m) * rows, rows) for m in range(self.size)}
        while step < self.size:
            parts = {
                m: part + self.send(parts[m | step], step) for m, part in parts.items() if not m & step
            }
            step *= 2
        return parts[0]

    def sum_pieces(self, piece):
        if self.size != 4:
            got = [self.send(piece(m).astype(bf16), m) for m in range(1, self.size)]
            total = piece(0)
            for value in got:
                total = total + value.astype(f32)
            return total
        far = piece(3).astype(bf16)
        handed = lax.ppermute(far, self.axis, [(0, 1), (3, 2)])
        middle = lax.ppermute(far, self.axis, [(1, 2), (2, 1)])
        near = self.send(piece(1).astype(bf16), 1)
        across = self.send((piece(2) + handed.astype(f32)).astype(bf16), 2)
        total = piece(0)
        for value in (middle, near, across):
            total = total + value.astype(f32)
        return total

    def all_pieces(self, own):
        if self.size != 4:
            return [own] + [self.send(own, m) for m in range(1, self.size)]
        right, left = [(i, i + 1) for i in range(3)], [(i + 1, i) for i in range(3)]
        before = lax.ppermute(own, self.axis, right)
        after = lax.ppermute(own, self.axis, left)
        across = lax.ppermute(before, self.axis, right[1:]) + lax.ppermute(after, self.axis, left[:2])
        ends = lax.ppermute(across, self.axis, [(2, 3), (1, 0)])
        near = jnp.where(self.me % 2 == 1, before, after)
        far = jnp.where(self.me == 1, after, jnp.where(self.me == 2, before, ends))
        return [own, near, across, far]

    def total(self, value):
        if not self.paired:
            return lax.psum(value, self.axis)
        step = 1
        while step < self.size:
            value = value + self.send(value, step)
            step *= 2
        return value


def body(
    block_input,
    norm_gain,
    w_z,
    w_x,
    w_bc,
    w_dt,
    conv_x_weight,
    conv_x_bias,
    conv_bc_weight,
    conv_bc_bias,
    dt_bias,
    a_log,
    d_skip,
    gate_gain,
    w_out,
    out_cotangent,
):
    length, width = block_input.shape
    inner = w_z.shape[1]
    heads = w_dt.shape[1]
    wide = inner + 2 * STATE
    inner_width = HEADS * HEAD_DIM
    line = Ring(TENSOR)
    ranks = line.size
    quarter = length // ranks
    rows = min(SPAN, length)
    count = length // rows

    w_cat = jnp.concatenate([w_x, jnp.pad(w_dt, ((0, 0), (0, LANES - heads))), w_bc], axis=1)
    ring, range_ring = Ring(SHARD), Ring(CONTEXT)
    w_out_t = w_out.T
    full_cat = ring.join(ring.near(ring.far(w_cat)))
    others = [line.send(w_out_t, m) for m in range(1, ranks)]
    far_z = ring.far(w_z)
    far_out = ring.far(w_out_t)

    x_float = block_input.astype(f32)
    inverse = lax.rsqrt(jnp.mean(x_float * x_float, axis=1, keepdims=True) + epsilon)
    normed = (x_float * inverse * norm_gain).astype(bf16)
    proj = jnp.dot(normed, full_cat, preferred_element_type=f32)
    x_raw = proj[:, :inner].astype(bf16)
    dt_raw = proj[:, inner : inner + LANES]
    bc_raw = proj[:, inner + LANES :].astype(bf16)

    edge = shifted(
        jnp.concatenate([x_raw[length - CONV + 1 :], bc_raw[length - CONV + 1 :]], axis=1), CONTEXT, 1
    ).astype(f32)
    edge = jnp.pad(edge, ((8 - CONV + 1, 0), (0, 0)))
    conv_weight = jnp.concatenate([conv_x_weight, conv_bc_weight], axis=1)
    conv_bias = jnp.concatenate([conv_x_bias, conv_bc_bias])[None, :]
    dt_in = dt_raw + jnp.pad(dt_bias, (0, LANES - heads))
    step = jax.nn.softplus(dt_in)
    decay_rate = jnp.exp(a_log)
    rate_row = jnp.pad(decay_rate, (0, LANES - heads))[None, :]
    d_row = jnp.repeat(d_skip, HEAD_DIM)[None, :]
    gain_row = gate_gain[None, :]
    owner = jnp.arange(inner) // HEAD_DIM
    one_hot = (jnp.arange(LANES)[:, None] == owner[None, :]).astype(bf16)
    spread_mat = jnp.concatenate([one_hot, one_hot], axis=0)
    one_hot_t = (owner[:, None] == jnp.arange(LANES)[None, :]).astype(bf16)
    gather_mat = jnp.concatenate([one_hot_t, one_hot_t], axis=0)
    place = jnp.arange(rows)
    lower = (place[:, None] >= place[None, :]).astype(bf16)
    lower2 = jnp.concatenate([lower, lower], axis=1)
    upper = (place[:, None] <= place[None, :]).astype(bf16)
    upper2 = jnp.concatenate([upper, upper], axis=1)

    def whole(shape):
        return pl.BlockSpec(shape, lambda c: (0,) * len(shape))

    def ahead(lanes, high=rows):
        return pl.BlockSpec((high, lanes), lambda c: (c, 0))

    def back(lanes, high=rows):
        return pl.BlockSpec((high, lanes), lambda c: (count - 1 - c, 0))

    def shape(*dims, dtype=f32):
        return jax.ShapeDtypeStruct(dims, dtype)

    params = pltpu.CompilerParams(dimension_semantics=("arbitrary",))

    pre, act, cum, s_local, totals = pl.pallas_call(
        front_kernel,
        grid=(count,),
        in_specs=[
            ahead(inner), ahead(2 * STATE), whole((8, wide)), whole((CONV, wide)), whole((1, wide)),
            ahead(LANES), whole((1, LANES)), whole((2 * LANES, inner)), whole((rows, 2 * rows)),
        ],
        out_specs=[ahead(wide), ahead(wide), ahead(LANES), whole((STATE, inner)), whole((8, LANES))],
        out_shape=[
            shape(length, wide), shape(length, wide), shape(length, LANES), shape(STATE, inner),
            shape(8, LANES),
        ],
        scratch_shapes=[pltpu.VMEM((rows + 8, wide), f32), pltpu.VMEM((STATE, inner), f32)],
        compiler_params=params,
        name="front",
    )(x_raw, bc_raw, edge, conv_weight, conv_bias, step, rate_row, spread_mat, lower2)
    decay = jnp.repeat(jnp.exp(totals[0, :heads]), HEAD_DIM)[None, :]
    s_in = chain(s_local, decay, CONTEXT, 1)
    totals, far_z, far_out = lax.optimization_barrier((totals, far_z, far_out))
    full_z = ring.join(ring.near(far_z))
    full_out = ring.join(ring.near(far_out))
    z_part = dot(normed, full_z)
    ggo = jnp.dot(out_cotangent, full_out, preferred_element_type=f32)
    mixer, enter, leave, sums = pl.pallas_call(
        forward_kernel,
        grid=(count,),
        in_specs=[
            ahead(wide), ahead(LANES), ahead(LANES), ahead(inner), ahead(inner), whole((STATE, inner)),
            whole((1, inner)), whole((1, inner)), whole((2 * LANES, inner)),
        ],
        out_specs=[
            ahead(inner), ahead(inner, STATE), ahead(inner, STATE), pl.BlockSpec((8, rows), lambda c: (0, c)),
        ],
        out_shape=[
            shape(length, inner), shape(count * STATE, inner), shape(count * STATE, inner), shape(8, length),
        ],
        scratch_shapes=[pltpu.VMEM((STATE, inner), f32)],
        compiler_params=params,
        name="forward",
    )(act, step, cum, z_part, ggo, s_in, d_row, gain_row, spread_mat)
    mixer, others = lax.optimization_barrier((mixer, others))
    all_others = ring.near(ring.far(jnp.concatenate(others, axis=1)))
    parts = [line.send(sums, m) for m in range(1, ranks)]
    for part in parts:
        sums = sums + part

    gated_out, gm, grad_z, own, gate_acc = pl.pallas_call(
        functools.partial(gate_kernel, inner_width),
        grid=(count,),
        in_specs=[
            back(inner), back(inner), back(inner), pl.BlockSpec((8, rows), lambda c: (0, count - 1 - c)),
            back(wide), back(LANES), whole((1, inner)), whole((2 * LANES, inner)),
        ],
        out_specs=[back(inner), back(inner), back(inner), whole((STATE, inner)), whole((8, inner))],
        out_shape=[
            shape(length, inner, dtype=bf16), shape(length, inner), shape(length, inner, dtype=bf16),
            shape(STATE, inner), shape(8, inner),
        ],
        scratch_shapes=[pltpu.VMEM((STATE, inner), f32)],
        compiler_params=params,
        name="gate",
    )(mixer, z_part, ggo, sums, act, cum, gain_row, spread_mat)
    carried = chain(own, decay, CONTEXT, -1)

    def block(value, rank):
        return lax.dynamic_slice_in_dim(value, rank * quarter, quarter)

    mixed = [line.send(block(gated_out, line.target(m)), m) for m in range(1, ranks)]
    grad_w_out = dot_tn(out_cotangent, gated_out)
    gx, gx_tail, pre_head, dbc, gstep, conv_acc, rate_acc = pl.pallas_call(
        backward_kernel,
        grid=(count,),
        in_specs=[
            back(inner), back(wide), back(inner), back(LANES), back(LANES), back(inner),
            back(inner, STATE), back(inner, STATE), whole((STATE, inner)), back(inner), whole((CONV, inner)),
            whole((1, inner)), whole((1, LANES)), whole((2 * LANES, inner)), whole((2 * inner, LANES)),
            whole((rows, 2 * rows)),
        ],
        out_specs=[
            back(inner), whole((8, inner)), whole((8, inner)), back(2 * STATE), back(LANES), whole((8, inner)),
            whole((8, LANES)),
        ],
        out_shape=[
            shape(length, inner, dtype=bf16), shape(8, inner), shape(8, inner), shape(length, 2 * STATE),
            shape(length, LANES), shape(8, inner), shape(8, LANES),
        ],
        scratch_shapes=[pltpu.VMEM((STATE, inner), f32), pltpu.VMEM((rows + 8, inner), f32)],
        compiler_params=params,
        name="backward",
    )(gm, act, pre, step, cum, mixer, enter, leave, carried, x_raw, conv_x_weight, d_row, rate_row,
      spread_mat, gather_mat, upper2)

    got = [line.send(block(dbc, line.target(m)), m) for m in range(1, ranks)]
    bc_own = block(dbc, line.me)
    for value in got:
        bc_own = bc_own + value
    pieces = line.all_pieces(bc_own)
    for m in range(ranks):
        dbc = lax.dynamic_update_slice_in_dim(dbc, pieces[m], line.source(m) * quarter, 0)
    pre_bc = pre[:, inner:]
    grad_pre_bc = dbc * slope_of(pre_bc, jax.nn.sigmoid(pre_bc))
    next_head = shifted(pre_head[: CONV - 1], CONTEXT, -1)
    next_bc_head = shifted(grad_pre_bc[: CONV - 1], CONTEXT, -1)
    after = jnp.pad(next_head, ((CONV - 1, CONV - 1), (0, 0)))
    reach = jnp.zeros((CONV - 1, inner), f32)
    for k in range(CONV):
        reach = reach + conv_x_weight[k] * after[CONV - 1 - k : 2 * (CONV - 1) - k]
    gx_last = (gx_tail + jnp.pad(reach, ((8 - CONV + 1, 0), (0, 0)))).astype(bf16)
    gx = lax.dynamic_update_slice_in_dim(gx, gx_last, length - 8, 0)
    bc_pad = jnp.concatenate([grad_pre_bc, next_bc_head], axis=0)
    gbc = jnp.zeros((length, 2 * STATE), f32)
    for k in range(CONV):
        gbc = gbc + conv_bc_weight[k] * bc_pad[CONV - 1 - k : CONV - 1 - k + length]
    gbc = gbc.astype(bf16)
    head_pad = jnp.pad(pre_head[: CONV - 1], ((CONV - 1, CONV - 1), (0, 0)))
    entering = edge[8 - CONV + 1 :]
    extra = jnp.stack([
        jnp.sum(entering[:, :inner] * head_pad[CONV - 1 - k : 2 * (CONV - 1) - k], axis=0)
        for k in range(CONV)
    ])
    bc_in = jnp.concatenate([entering[:, inner:], bc_raw.astype(f32)], axis=0)
    grad_conv_bc = jnp.stack([jnp.sum(grad_pre_bc * bc_in[k : k + length], axis=0) for k in range(CONV)])
    grad_conv_bc_bias = jnp.sum(grad_pre_bc, axis=0)

    sigma = jax.nn.sigmoid(dt_in)
    g_dt = gstep * sigma
    grad_dt_bias = jnp.sum(g_dt, axis=0)
    g_dt = g_dt.astype(bf16)
    grad_a_log = rate_acc[0] * rate_row[0]

    gx, late_z = lax.optimization_barrier((gx, grad_z))
    grad_w_z = dot_tn(normed, late_z)
    summed_out, summed_z = ring.reduce_rows(grad_w_out), ring.reduce_rows(grad_w_z)
    summed_out, summed_z = range_ring.reduce_rows(summed_out).T, range_ring.reduce_rows(summed_z)
    g_xdt = jnp.concatenate([gx, g_dt], axis=1)
    grad_w_xdt = dot_tn(normed, g_xdt)
    summed_xdt = ring.reduce_rows(grad_w_xdt)
    summed_xdt = range_ring.reduce_rows(summed_xdt)
    full_xdt = full_cat[:, : inner + LANES]

    def partial_of(m):
        rank = line.target(m)
        return dot_t(block(late_z, rank), full_z) + dot_t(block(g_xdt, rank), full_xdt)

    _, all_others = lax.optimization_barrier((gx_last, all_others))
    gn = line.sum_pieces(partial_of)
    gn = gn + dot_t(block(gbc, line.me), full_cat[:, inner + LANES :])

    out_own = dot_t(block(gated_out, line.me), full_out)
    if ranks > 1:
        out_own = out_own + dot_t(jnp.concatenate(mixed, axis=1), ring.join(all_others))
    block_own = (block(block_input, line.me).astype(f32) + out_own).astype(bf16)
    pieces = line.all_pieces(block_own)
    block_output = jnp.zeros((length, width), bf16)
    for m in range(ranks):
        block_output = lax.dynamic_update_slice_in_dim(
            block_output, pieces[m], line.source(m) * quarter, 0
        )

    x_own, inv_own = block(block_input, line.me).astype(f32), block(inverse, line.me)
    scaled = norm_gain * gn
    delta = inv_own * scaled - x_own * (inv_own * inv_own * inv_own) * jnp.mean(
        scaled * x_own, axis=1, keepdims=True
    )
    delta = lax.optimization_barrier(delta.astype(bf16))
    grad_norm_gain = jnp.sum(gn * x_own * inv_own, axis=0)
    pieces = line.all_pieces(delta)
    back_pieces = pieces

    summed_bc = ring.reduce_rows(dot_tn(normed, gbc))
    summed_bc = range_ring.reduce_rows(summed_bc)

    last = jnp.pad(jnp.concatenate([grad_dt_bias[:LANES], grad_a_log]), (0, inner - 2 * LANES))[None, :]
    packed = jnp.concatenate(
        [
            jnp.concatenate([conv_acc[:CONV] + extra, conv_acc[CONV : CONV + 1], gate_acc[:2], last], axis=0),
            jnp.concatenate(
                [grad_conv_bc, grad_conv_bc_bias[None, :], jnp.zeros((3, 2 * STATE), f32)], axis=0
            ),
        ],
        axis=1,
    )
    wide_lanes = packed.shape[1]
    spare = (-width) % wide_lanes
    gain_rows = jnp.pad(grad_norm_gain, (0, spare)).reshape(-1, wide_lanes)
    packed = ring.total(jnp.concatenate([packed, gain_rows], axis=0))
    packed = range_ring.total(packed)
    gain_rows = packed[8:]
    parts = [gain_rows] + [line.send(gain_rows, m) for m in range(1, ranks)]
    ordered = jnp.zeros((ranks,) + gain_rows.shape, f32)
    for m in range(ranks):
        ordered = lax.dynamic_update_slice_in_dim(ordered, parts[m][None], line.source(m), 0)
    sum_norm_gain = jnp.sum(ordered, axis=0).reshape(-1)[:width]
    input_grad = jnp.zeros((length, width), f32)
    for m in range(ranks):
        rank = line.source(m)
        input_grad = lax.dynamic_update_slice_in_dim(
            input_grad,
            block(out_cotangent, rank).astype(f32) + back_pieces[m].astype(f32),
            rank * quarter,
            0,
        )
    return (
        block_output,
        input_grad,
        summed_z,
        summed_xdt[:, :inner],
        summed_bc,
        summed_xdt[:, inner : inner + heads],
        summed_out,
        sum_norm_gain,
        packed[:CONV, :inner],
        packed[CONV, :inner],
        packed[:CONV, inner:],
        packed[CONV, inner:],
        packed[7, :heads],
        packed[7, LANES : LANES + heads],
        jnp.sum(packed[6, :inner].reshape(heads, HEAD_DIM), axis=1),
        packed[5, :inner],
    )


def solution(mesh):
    in_specs = (
        P((SHARD, CONTEXT), None),
        P(),
        P(SHARD, TENSOR),
        P(SHARD, TENSOR),
        P(SHARD, None),
        P(SHARD, TENSOR),
        P(None, TENSOR),
        P(TENSOR),
        P(),
        P(),
        P(TENSOR),
        P(TENSOR),
        P(TENSOR),
        P(TENSOR),
        P(TENSOR, SHARD),
        P((SHARD, CONTEXT), None),
    )
    out_specs = (
        P((SHARD, CONTEXT), None),
        P((SHARD, CONTEXT), None),
        P((SHARD, CONTEXT), TENSOR),
        P((SHARD, CONTEXT), TENSOR),
        P((SHARD, CONTEXT), None),
        P((SHARD, CONTEXT), TENSOR),
        P(TENSOR, (SHARD, CONTEXT)),
        P(),
        P(None, TENSOR),
        P(TENSOR),
        P(),
        P(),
        P(TENSOR),
        P(TENSOR),
        P(TENSOR),
        P(TENSOR),
    )
    return jax.shard_map(body, mesh=mesh, in_specs=in_specs, out_specs=out_specs, check_vma=False)
```

```python
import functools

import jax
import jax.numpy as jnp
from jax import lax
from jax.experimental import pallas as pl
from jax.experimental.layout import Layout, with_layout_constraint
from jax.experimental.pallas import tpu as pltpu
from jax.sharding import PartitionSpec as P


HEADS = 48
HEAD_DIM = 64
STATE = 128
CONV = 4
SPAN = 128
LANES = 128

epsilon = 1e-05
SHARD = "shard"
CONTEXT = "context"
TENSOR = "tensor"
f32 = jnp.float32
bf16 = jnp.bfloat16


def split(v):
    hi = v.astype(bf16)
    return hi, (v - hi.astype(f32)).astype(bf16)


def dot(a, b):
    return lax.dot_general(a, b, (((1,), (0,)), ((), ())), preferred_element_type=f32)


def dot_t(a, b):
    return lax.dot_general(a, b, (((1,), (1,)), ((), ())), preferred_element_type=f32)


def dot_tn(a, b):
    return lax.dot_general(a, b, (((0,), (0,)), ((), ())), preferred_element_type=f32)


def lhs3(parts):
    hi, lo = parts
    return jnp.concatenate([hi, lo, hi], axis=1)


def rhs3(parts):
    hi, lo = parts
    return jnp.concatenate([hi, hi, lo], axis=0)


def rhs3_t(parts):
    hi, lo = parts
    return jnp.concatenate([hi, hi, lo], axis=1)


def spread(values, spread_mat):
    hi, lo = split(values)
    return dot(jnp.concatenate([hi, lo], axis=1), spread_mat)


def gather_heads(values, gather_mat):
    hi, lo = split(values)
    return dot(jnp.concatenate([hi, lo], axis=1), gather_mat)


def tri_sum(tri2, values):
    hi, lo = split(values)
    return dot(tri2, jnp.concatenate([hi, lo], axis=0))


def sigmoid(v):
    return 1.0 / (1.0 + jnp.exp(-v))


def slope_of(v, sigma):
    return sigma * (1.0 + v * (1.0 - sigma))


def front_kernel(x_ref, bc_ref, edge_ref, cw_ref, cb_ref, step_ref, rate_ref, spread_ref, tri_ref,
                 pre_ref, act_ref, cum_ref, state_ref, total_ref, ext, state):
    c = pl.program_id(0)
    rows, inner = x_ref.shape
    wide = cw_ref.shape[1]

    @pl.when(c == 0)
    def _():
        ext[0:8, :] = edge_ref[...]
        state[...] = jnp.zeros_like(state)
        total_ref[...] = jnp.zeros_like(total_ref)

    ext[8 : 8 + rows, 0:inner] = x_ref[...].astype(f32)
    ext[8 : 8 + rows, inner:wide] = bc_ref[...].astype(f32)
    pre = cb_ref[...] + cw_ref[0:1, :] * ext[5 : 5 + rows, :]
    for k in range(1, CONV):
        pre = pre + cw_ref[k : k + 1, :] * ext[5 + k : 5 + k + rows, :]
    ext[0:8, :] = ext[rows : rows + 8, :]
    act = pre * sigmoid(pre)
    pre_ref[...] = pre
    act_ref[...] = act
    step = step_ref[...]
    cum = tri_sum(tri_ref[...], -step * rate_ref[...])
    cum_ref[...] = cum
    total = cum[rows - 1 : rows, :]
    b_t = jnp.transpose(act[:, inner : inner + STATE])
    weight = spread(step * jnp.exp(total - cum), spread_ref[...])
    decay = spread(jnp.broadcast_to(jnp.exp(total), (8, LANES)), spread_ref[...])[0:1, :]
    new = decay * state[...] + dot(lhs3(split(b_t)), rhs3(split(act[:, 0:inner] * weight)))
    state[...] = new
    state_ref[...] = new
    total_ref[...] = total_ref[...] + jnp.broadcast_to(total, (8, LANES))


def forward_kernel(act_ref, step_ref, cum_ref, z_ref, ggo_ref, s_in_ref, d_ref, gain_ref, spread_ref,
                   mixer_ref, enter_ref, exit_ref, sums_ref, state):
    c = pl.program_id(0)
    rows, inner = z_ref.shape

    @pl.when(c == 0)
    def _():
        state[...] = s_in_ref[...]

    heads = inner // HEAD_DIM
    per = LANES // HEAD_DIM
    spread_mat = spread_ref[...]
    x = act_ref[:, 0:inner]
    b_mat = act_ref[:, inner : inner + STATE]
    c_mat = act_ref[:, inner + STATE : inner + 2 * STATE]
    step = step_ref[...]
    cum = cum_ref[...]
    cum_t = jnp.transpose(cum)
    total = cum[rows - 1 : rows, :]
    wide = spread(
        jnp.concatenate([step, step * jnp.exp(total - cum), jnp.exp(cum)], axis=0), spread_mat
    )
    decay = spread(jnp.broadcast_to(jnp.exp(total), (8, LANES)), spread_mat)[0:1, :]
    x_step = x * wide[0:rows]
    c3 = lhs3(split(c_mat))
    scores = dot_t(c3, rhs3_t(split(b_mat)))
    enter = state[...]
    enter_ref[...] = enter
    outer = dot(c3, rhs3(split(enter))) * wide[2 * rows : 3 * rows]
    lower = lax.broadcasted_iota(jnp.int32, (rows, rows), 0) >= lax.broadcasted_iota(
        jnp.int32, (rows, rows), 1
    )
    lane = lax.broadcasted_iota(jnp.int32, (rows, LANES), 1)
    masked = jnp.where(lower, scores, 0.0)
    tiles = []
    for tile in range(heads // per):
        value = rhs3(split(x_step[:, tile * LANES : (tile + 1) * LANES]))
        got = None
        for j in range(per):
            h = tile * per + j
            gap = cum[:, h : h + 1] - cum_t[h : h + 1, :]
            part = dot(lhs3(split(jnp.exp(jnp.minimum(gap, 0.0)) * masked)), value)
            got = part if got is None else jnp.where(lane >= j * HEAD_DIM, part, got)
        tiles.append(got)
    inner_out = jnp.concatenate(tiles, axis=1)
    mixer = inner_out + outer + d_ref[...] * x
    mixer_ref[...] = mixer
    b_t = jnp.transpose(b_mat)
    new = decay * enter + dot(lhs3(split(b_t)), rhs3(split(x * wide[rows : 2 * rows])))
    state[...] = new
    exit_ref[...] = new
    z = z_ref[...]
    gated = mixer * (z * sigmoid(z))
    square = jnp.sum(gated * gated, axis=1, keepdims=True)
    term = jnp.sum(gain_ref[...] * ggo_ref[...] * gated, axis=1, keepdims=True)
    both = jnp.where(lane == 0, square, term)
    sums_ref[...] = jnp.transpose(both)[0:8, :]


def gate_kernel(inner_width, mixer_ref, z_ref, ggo_ref, sums_ref, act_ref, cum_ref, gain_ref, spread_ref,
                out_ref, gm_ref, gz_ref, own_ref, acc_ref, state):
    c = pl.program_id(0)
    rows, inner = z_ref.shape

    @pl.when(c == 0)
    def _():
        state[...] = jnp.zeros_like(state)
        acc_ref[...] = jnp.zeros_like(acc_ref)

    spread_mat = spread_ref[...]
    columns = jnp.transpose(jnp.concatenate([sums_ref[...]] * (LANES // 8), axis=0))
    inverse = lax.rsqrt(columns[:, 0:1] / inner_width + epsilon)
    term = columns[:, 1:2] / inner_width
    mixer = mixer_ref[...]
    z = z_ref[...]
    sigma = sigmoid(z)
    gate = z * sigma
    gated = mixer * gate
    ggo = ggo_ref[...]
    normal = gated * inverse
    out_ref[...] = (normal * gain_ref[...]).astype(bf16)
    grad_gated = inverse * (gain_ref[...] * ggo) - normal * (inverse * inverse * term)
    gm = grad_gated * gate
    gm_ref[...] = gm
    gz_ref[...] = (grad_gated * mixer * slope_of(z, sigma)).astype(bf16)
    x = act_ref[:, 0:inner]
    c_mat = act_ref[:, inner + STATE : inner + 2 * STATE]
    acc_ref[0:1, :] += jnp.sum(ggo * normal, axis=0, keepdims=True)
    acc_ref[1:2, :] += jnp.sum(gm * x, axis=0, keepdims=True)
    cum = cum_ref[...]
    total = cum[rows - 1 : rows, :]
    grown = spread(jnp.exp(cum), spread_mat)
    decay = spread(jnp.broadcast_to(jnp.exp(total), (8, LANES)), spread_mat)[0:1, :]
    new = decay * state[...] + dot(
        lhs3(split(jnp.transpose(c_mat))), rhs3(split(gm * grown))
    )
    state[...] = new
    own_ref[...] = new


def backward_kernel(gm_ref, act_ref, pre_ref, step_ref, cum_ref, mixer_ref, enter_ref, exit_ref, carried_ref,
                    x_raw_ref, cw_ref, d_ref, rate_ref, spread_ref, gather_ref, upper_ref,
                    gx_ref, tail_ref, head_ref, dbc_ref, gstep_ref, conv_ref, rate_out_ref,
                    state, ext):
    c = pl.program_id(0)
    rows, inner = gm_ref.shape

    @pl.when(c == 0)
    def _():
        state[...] = carried_ref[...]
        ext[rows : rows + 8, :] = jnp.zeros((8, inner), f32)
        conv_ref[...] = jnp.zeros_like(conv_ref)
        rate_out_ref[...] = jnp.zeros_like(rate_out_ref)

    heads = inner // HEAD_DIM
    per = LANES // HEAD_DIM
    spread_mat = spread_ref[...]
    gather_mat = gather_ref[...]
    gm = gm_ref[...]
    x = act_ref[:, 0:inner]
    b_mat = act_ref[:, inner : inner + STATE]
    c_mat = act_ref[:, inner + STATE : inner + 2 * STATE]
    step = step_ref[...]
    cum = cum_ref[...]
    cum_t = jnp.transpose(cum)
    total = cum[rows - 1 : rows, :]
    wide = spread(
        jnp.concatenate([step, jnp.exp(total - cum), jnp.exp(cum)], axis=0), spread_mat
    )
    step_wide, tail_wide, grown = wide[0:rows], wide[rows : 2 * rows], wide[2 * rows : 3 * rows]
    decay = spread(jnp.broadcast_to(jnp.exp(total), (8, LANES)), spread_mat)[0:1, :]
    x_step = x * step_wide
    b_parts, c_parts = split(b_mat), split(c_mat)
    b3 = lhs3(b_parts)
    scores_t = dot_t(b3, rhs3_t(c_parts))
    grad_exit = state[...]
    exit_parts = split(grad_exit)
    upper = lax.broadcasted_iota(jnp.int32, (rows, rows), 1) >= lax.broadcasted_iota(
        jnp.int32, (rows, rows), 0
    )
    lane = lax.broadcasted_iota(jnp.int32, (rows, LANES), 1)
    through = dot(b3, rhs3(exit_parts)) * tail_wide
    gm_hi, gm_lo = split(gm)
    xs_hi, xs_lo = split(x_step)
    tiles = []
    grad_scores = jnp.zeros((rows, rows), f32)
    zero = jnp.zeros((rows, LANES), bf16)
    for tile in range(heads // per):
        cut = slice(tile * LANES, (tile + 1) * LANES)
        g_hi, g_lo = gm_hi[:, cut], gm_lo[:, cut]
        g_rows = jnp.concatenate([g_hi, g_hi, g_lo], axis=0)
        g_lanes = jnp.concatenate([g_hi, g_hi, g_lo], axis=1)
        got = None
        for j in range(per):
            h = tile * per + j
            keep = (lane >= j * HEAD_DIM) & (lane < (j + 1) * HEAD_DIM)
            xh = jnp.where(keep, xs_hi[:, cut], zero)
            xl = jnp.where(keep, xs_lo[:, cut], zero)
            gap = cum_t[h : h + 1, :] - cum[:, h : h + 1]
            span = jnp.where(upper, jnp.exp(jnp.minimum(gap, 0.0)), 0.0)
            pairs = dot_t(jnp.concatenate([xh, xl, xh], axis=1), g_lanes)
            grad_scores = grad_scores + span * pairs
            part = dot(lhs3(split(span * scores_t)), g_rows)
            got = part if got is None else jnp.where(lane >= j * HEAD_DIM, part, got)
        tiles.append(got)
    grad_xs = jnp.concatenate(tiles, axis=1) + through
    scores_parts = split(grad_scores)
    weighted = gm * grown
    weighted_parts = split(weighted)
    enter_parts = split(enter_ref[...])
    grad_b = dot(lhs3(scores_parts), rhs3(c_parts)) + dot_t(
        lhs3(split(x_step * tail_wide)), rhs3_t(exit_parts)
    )
    grad_c = dot(lhs3(split(jnp.transpose(grad_scores))), rhs3(b_parts)) + dot_t(
        lhs3(weighted_parts), rhs3_t(enter_parts)
    )
    dbc_ref[:, 0:STATE] = grad_b
    dbc_ref[:, STATE : 2 * STATE] = grad_c
    lost = jnp.sum(grad_exit * exit_ref[...], axis=0, keepdims=True)
    state[...] = decay * grad_exit + dot(
        lhs3(split(jnp.transpose(c_mat))), rhs3(weighted_parts)
    )
    ssd = mixer_ref[...] - d_ref[...] * x
    heads_sum = gather_heads(
        jnp.concatenate([gm * ssd, x * grad_xs, jnp.broadcast_to(lost, (8, inner))], axis=0), gather_mat
    )
    by_step = heads_sum[rows : 2 * rows]
    grad_log = tri_sum(upper_ref[...], heads_sum[0:rows] - step * by_step) + heads_sum[
        2 * rows : 2 * rows + 1
    ]
    gstep_ref[...] = by_step - rate_ref[...] * grad_log
    rate_out_ref[0:1, :] += -jnp.sum(grad_log * step, axis=0, keepdims=True)
    pre = pre_ref[...]
    grad_pre = (grad_xs * step_wide + d_ref[...] * gm) * slope_of(pre, sigmoid(pre))
    ext[0:rows, :] = grad_pre
    raw = x_raw_ref[...].astype(f32)
    conv_ref[CONV : CONV + 1, :] += jnp.sum(grad_pre, axis=0, keepdims=True)
    total_in = None
    for k in range(CONV):
        moved = ext[CONV - 1 - k : CONV - 1 - k + rows, :]
        conv_ref[k : k + 1, :] += jnp.sum(moved * raw, axis=0, keepdims=True)
        piece = cw_ref[k : k + 1, :] * moved
        total_in = piece if total_in is None else total_in + piece
    gx_ref[...] = total_in.astype(bf16)

    @pl.when(c == 0)
    def _():
        tail_ref[...] = total_in[rows - 8 : rows, :]

    head_ref[...] = grad_pre[0:8, :]
    ext[rows : rows + 8, :] = grad_pre[0:8, :]


def shifted(value, axis, by):
    length = lax.axis_size(axis)
    pairs = [(i, i + by) for i in range(length) if 0 <= i + by < length]
    return lax.ppermute(value, axis, pairs)


def chain(local, decay, axis, by):
    got = None
    for _ in range(lax.axis_size(axis) - 1):
        got = shifted(local if got is None else local + decay * got, axis, by)
    return jnp.zeros_like(local) if got is None else got


class Ring:
    def __init__(self, axis):
        self.axis = axis
        self.size = lax.axis_size(axis)
        self.me = lax.axis_index(axis)
        self.paired = self.size & (self.size - 1) == 0

    def target(self, m):
        return self.me ^ m if self.paired else (self.me + m) % self.size

    def source(self, m):
        return self.me ^ m if self.paired else (self.me - m) % self.size

    def send(self, value, m):
        pairs = [(i, i ^ m if self.paired else (i + m) % self.size) for i in range(self.size)]
        return lax.ppermute(value, self.axis, pairs)

    def far(self, value):
        if self.size == 1 or not self.paired:
            return {0: value}
        return {0: value, self.size // 2: self.send(value, self.size // 2)}

    def near(self, pieces):
        step = self.size // 4
        while step and self.paired:
            pieces = {**pieces, **{m | step: self.send(piece, step) for m, piece in pieces.items()}}
            step //= 2
        return pieces

    def join(self, pieces):
        value = pieces[0]
        if self.paired:
            rows = value.shape[0]
            full = jnp.zeros((rows * self.size,) + value.shape[1:], value.dtype)
            for m, piece in pieces.items():
                full = lax.dynamic_update_slice_in_dim(full, piece, self.source(m) * rows, 0)
        else:
            full = lax.all_gather(value, self.axis, axis=0, tiled=True)
        return with_layout_constraint(full, Layout((0, 1)))

    def reduce_rows(self, value):
        if not self.paired:
            return lax.psum_scatter(value, self.axis, scatter_dimension=0, tiled=True)
        rows, step = value.shape[0] // self.size, 1
        value = with_layout_constraint(value, Layout((0, 1)))
        parts = {m: lax.dynamic_slice_in_dim(value, self.target(m) * rows, rows) for m in range(self.size)}
        while step < self.size:
            parts = {
                m: part + self.send(parts[m | step], step) for m, part in parts.items() if not m & step
            }
            step *= 2
        return parts[0]

    def sum_pieces(self, piece):
        if self.size != 4:
            got = [self.send(piece(m).astype(bf16), m) for m in range(1, self.size)]
            total = piece(0)
            for value in got:
                total = total + value.astype(f32)
            return total
        far = piece(3).astype(bf16)
        handed = lax.ppermute(far, self.axis, [(0, 1), (3, 2)])
        middle = lax.ppermute(far, self.axis, [(1, 2), (2, 1)])
        near = self.send(piece(1).astype(bf16), 1)
        across = self.send((piece(2) + handed.astype(f32)).astype(bf16), 2)
        total = piece(0)
        for value in (middle, near, across):
            total = total + value.astype(f32)
        return total

    def all_pieces(self, own, parts=1):
        rows = own.shape[0] // parts
        cuts = [own[p * rows : (p + 1) * rows] for p in range(parts)]
        if self.size != 4:
            return [
                (m, p * rows, self.send(cut, m) if m else cut) for m in range(self.size) for p, cut in enumerate(cuts)
            ]
        direct = []
        for cut in cuts:
            middle = lax.ppermute(cut, self.axis, [(1, 2), (2, 1)])
            cross = lax.ppermute(cut, self.axis, [(0, 2), (3, 1)])
            direct.append((self.send(cut, 1), middle, cross))
        found = [(0, p * rows, cut) for p, cut in enumerate(cuts)]
        for p, (near, middle, cross) in enumerate(direct):
            first = lax.ppermute(middle, self.axis, [(1, 0), (2, 3)])
            second = lax.ppermute(cross, self.axis, [(1, 0), (2, 3)])
            found += [(1, p * rows, near), (2, p * rows, cross + first), (3, p * rows, middle + second)]
        return found

    def total(self, value):
        if not self.paired:
            return lax.psum(value, self.axis)
        step = 1
        while step < self.size:
            value = value + self.send(value, step)
            step *= 2
        return value


def body(
    block_input,
    norm_gain,
    w_z,
    w_x,
    w_bc,
    w_dt,
    conv_x_weight,
    conv_x_bias,
    conv_bc_weight,
    conv_bc_bias,
    dt_bias,
    a_log,
    d_skip,
    gate_gain,
    w_out,
    out_cotangent,
):
    length, width = block_input.shape
    inner = w_z.shape[1]
    heads = w_dt.shape[1]
    wide = inner + 2 * STATE
    inner_width = HEADS * HEAD_DIM
    line = Ring(TENSOR)
    ranks = line.size
    quarter = length // ranks
    rows = min(SPAN, length)
    count = length // rows

    w_cat = jnp.concatenate([w_x, jnp.pad(w_dt, ((0, 0), (0, LANES - heads))), w_bc], axis=1)
    ring, range_ring = Ring(SHARD), Ring(CONTEXT)
    w_out_t = w_out.T
    full_cat = ring.join(ring.near(ring.far(w_cat)))
    others = [line.send(w_out_t, m) for m in range(1, ranks)]
    far_z = ring.far(w_z)
    far_out = ring.far(w_out_t)

    x_float = block_input.astype(f32)
    inverse = lax.rsqrt(jnp.mean(x_float * x_float, axis=1, keepdims=True) + epsilon)
    normed = (x_float * inverse * norm_gain).astype(bf16)
    proj = jnp.dot(normed, full_cat, preferred_element_type=f32)
    x_raw = proj[:, :inner].astype(bf16)
    dt_raw = proj[:, inner : inner + LANES]
    bc_raw = proj[:, inner + LANES :].astype(bf16)

    edge = shifted(
        jnp.concatenate([x_raw[length - CONV + 1 :], bc_raw[length - CONV + 1 :]], axis=1), CONTEXT, 1
    ).astype(f32)
    edge = jnp.pad(edge, ((8 - CONV + 1, 0), (0, 0)))
    conv_weight = jnp.concatenate([conv_x_weight, conv_bc_weight], axis=1)
    conv_bias = jnp.concatenate([conv_x_bias, conv_bc_bias])[None, :]
    dt_in = dt_raw + jnp.pad(dt_bias, (0, LANES - heads))
    step = jax.nn.softplus(dt_in)
    decay_rate = jnp.exp(a_log)
    rate_row = jnp.pad(decay_rate, (0, LANES - heads))[None, :]
    d_row = jnp.repeat(d_skip, HEAD_DIM)[None, :]
    gain_row = gate_gain[None, :]
    owner = jnp.arange(inner) // HEAD_DIM
    one_hot = (jnp.arange(LANES)[:, None] == owner[None, :]).astype(bf16)
    spread_mat = jnp.concatenate([one_hot, one_hot], axis=0)
    one_hot_t = (owner[:, None] == jnp.arange(LANES)[None, :]).astype(bf16)
    gather_mat = jnp.concatenate([one_hot_t, one_hot_t], axis=0)
    place = jnp.arange(rows)
    lower = (place[:, None] >= place[None, :]).astype(bf16)
    lower2 = jnp.concatenate([lower, lower], axis=1)
    upper = (place[:, None] <= place[None, :]).astype(bf16)
    upper2 = jnp.concatenate([upper, upper], axis=1)

    def whole(shape):
        return pl.BlockSpec(shape, lambda c: (0,) * len(shape))

    def ahead(lanes, high=rows):
        return pl.BlockSpec((high, lanes), lambda c: (c, 0))

    def back(lanes, high=rows):
        return pl.BlockSpec((high, lanes), lambda c: (count - 1 - c, 0))

    def shape(*dims, dtype=f32):
        return jax.ShapeDtypeStruct(dims, dtype)

    params = pltpu.CompilerParams(dimension_semantics=("arbitrary",))

    pre, act, cum, s_local, totals = pl.pallas_call(
        front_kernel,
        grid=(count,),
        in_specs=[
            ahead(inner), ahead(2 * STATE), whole((8, wide)), whole((CONV, wide)), whole((1, wide)),
            ahead(LANES), whole((1, LANES)), whole((2 * LANES, inner)), whole((rows, 2 * rows)),
        ],
        out_specs=[ahead(wide), ahead(wide), ahead(LANES), whole((STATE, inner)), whole((8, LANES))],
        out_shape=[
            shape(length, wide), shape(length, wide), shape(length, LANES), shape(STATE, inner),
            shape(8, LANES),
        ],
        scratch_shapes=[pltpu.VMEM((rows + 8, wide), f32), pltpu.VMEM((STATE, inner), f32)],
        compiler_params=params,
        name="front",
    )(x_raw, bc_raw, edge, conv_weight, conv_bias, step, rate_row, spread_mat, lower2)
    decay = jnp.repeat(jnp.exp(totals[0, :heads]), HEAD_DIM)[None, :]
    s_in = chain(s_local, decay, CONTEXT, 1)
    totals, far_z, far_out = lax.optimization_barrier((totals, far_z, far_out))
    full_z = ring.join(ring.near(far_z))
    full_out = ring.join(ring.near(far_out))
    z_part = dot(normed, full_z)
    ggo = jnp.dot(out_cotangent, full_out, preferred_element_type=f32)
    mixer, enter, leave, sums = pl.pallas_call(
        forward_kernel,
        grid=(count,),
        in_specs=[
            ahead(wide), ahead(LANES), ahead(LANES), ahead(inner), ahead(inner), whole((STATE, inner)),
            whole((1, inner)), whole((1, inner)), whole((2 * LANES, inner)),
        ],
        out_specs=[
            ahead(inner), ahead(inner, STATE), ahead(inner, STATE), pl.BlockSpec((8, rows), lambda c: (0, c)),
        ],
        out_shape=[
            shape(length, inner), shape(count * STATE, inner), shape(count * STATE, inner), shape(8, length),
        ],
        scratch_shapes=[pltpu.VMEM((STATE, inner), f32)],
        compiler_params=params,
        name="forward",
    )(act, step, cum, z_part, ggo, s_in, d_row, gain_row, spread_mat)
    mixer, others = lax.optimization_barrier((mixer, others))
    all_others = ring.near(ring.far(jnp.concatenate(others, axis=1)))
    parts = [line.send(sums, m) for m in range(1, ranks)]
    for part in parts:
        sums = sums + part

    gated_out, gm, grad_z, own, gate_acc = pl.pallas_call(
        functools.partial(gate_kernel, inner_width),
        grid=(count,),
        in_specs=[
            back(inner), back(inner), back(inner), pl.BlockSpec((8, rows), lambda c: (0, count - 1 - c)),
            back(wide), back(LANES), whole((1, inner)), whole((2 * LANES, inner)),
        ],
        out_specs=[back(inner), back(inner), back(inner), whole((STATE, inner)), whole((8, inner))],
        out_shape=[
            shape(length, inner, dtype=bf16), shape(length, inner), shape(length, inner, dtype=bf16),
            shape(STATE, inner), shape(8, inner),
        ],
        scratch_shapes=[pltpu.VMEM((STATE, inner), f32)],
        compiler_params=params,
        name="gate",
    )(mixer, z_part, ggo, sums, act, cum, gain_row, spread_mat)
    carried = chain(own, decay, CONTEXT, -1)

    def block(value, rank):
        return lax.dynamic_slice_in_dim(value, rank * quarter, quarter)

    mixed = [line.send(block(gated_out, line.target(m)), m) for m in range(1, ranks)]
    grad_w_out = dot_tn(out_cotangent, gated_out)
    gx, gx_tail, pre_head, dbc, gstep, conv_acc, rate_acc = pl.pallas_call(
        backward_kernel,
        grid=(count,),
        in_specs=[
            back(inner), back(wide), back(inner), back(LANES), back(LANES), back(inner),
            back(inner, STATE), back(inner, STATE), whole((STATE, inner)), back(inner), whole((CONV, inner)),
            whole((1, inner)), whole((1, LANES)), whole((2 * LANES, inner)), whole((2 * inner, LANES)),
            whole((rows, 2 * rows)),
        ],
        out_specs=[
            back(inner), whole((8, inner)), whole((8, inner)), back(2 * STATE), back(LANES), whole((8, inner)),
            whole((8, LANES)),
        ],
        out_shape=[
            shape(length, inner, dtype=bf16), shape(8, inner), shape(8, inner), shape(length, 2 * STATE),
            shape(length, LANES), shape(8, inner), shape(8, LANES),
        ],
        scratch_shapes=[pltpu.VMEM((STATE, inner), f32), pltpu.VMEM((rows + 8, inner), f32)],
        compiler_params=params,
        name="backward",
    )(gm, act, pre, step, cum, mixer, enter, leave, carried, x_raw, conv_x_weight, d_row, rate_row,
      spread_mat, gather_mat, upper2)

    got = [line.send(block(dbc, line.target(m)), m) for m in range(1, ranks)]
    bc_own = block(dbc, line.me)
    for value in got:
        bc_own = bc_own + value
    pieces = [bc_own] + [line.send(bc_own, m) for m in range(1, ranks)]
    for m in range(ranks):
        dbc = lax.dynamic_update_slice_in_dim(dbc, pieces[m], line.source(m) * quarter, 0)
    pre_bc = pre[:, inner:]
    grad_pre_bc = dbc * slope_of(pre_bc, jax.nn.sigmoid(pre_bc))
    next_head = shifted(pre_head[: CONV - 1], CONTEXT, -1)
    next_bc_head = shifted(grad_pre_bc[: CONV - 1], CONTEXT, -1)
    after = jnp.pad(next_head, ((CONV - 1, CONV - 1), (0, 0)))
    reach = jnp.zeros((CONV - 1, inner), f32)
    for k in range(CONV):
        reach = reach + conv_x_weight[k] * after[CONV - 1 - k : 2 * (CONV - 1) - k]
    gx_last = (gx_tail + jnp.pad(reach, ((8 - CONV + 1, 0), (0, 0)))).astype(bf16)
    gx = lax.dynamic_update_slice_in_dim(gx, gx_last, length - 8, 0)
    bc_pad = jnp.concatenate([grad_pre_bc, next_bc_head], axis=0)
    gbc = jnp.zeros((length, 2 * STATE), f32)
    for k in range(CONV):
        gbc = gbc + conv_bc_weight[k] * bc_pad[CONV - 1 - k : CONV - 1 - k + length]
    gbc = gbc.astype(bf16)
    head_pad = jnp.pad(pre_head[: CONV - 1], ((CONV - 1, CONV - 1), (0, 0)))
    entering = edge[8 - CONV + 1 :]
    extra = jnp.stack([
        jnp.sum(entering[:, :inner] * head_pad[CONV - 1 - k : 2 * (CONV - 1) - k], axis=0)
        for k in range(CONV)
    ])
    bc_in = jnp.concatenate([entering[:, inner:], bc_raw.astype(f32)], axis=0)
    grad_conv_bc = jnp.stack([jnp.sum(grad_pre_bc * bc_in[k : k + length], axis=0) for k in range(CONV)])
    grad_conv_bc_bias = jnp.sum(grad_pre_bc, axis=0)

    sigma = jax.nn.sigmoid(dt_in)
    g_dt = gstep * sigma
    grad_dt_bias = jnp.sum(g_dt, axis=0)
    g_dt = g_dt.astype(bf16)
    grad_a_log = rate_acc[0] * rate_row[0]

    gx, late_z = lax.optimization_barrier((gx, grad_z))
    grad_w_z = dot_tn(normed, late_z)
    summed_out, summed_z = ring.reduce_rows(grad_w_out), ring.reduce_rows(grad_w_z)
    summed_out, summed_z = range_ring.reduce_rows(summed_out).T, range_ring.reduce_rows(summed_z)
    g_xdt = jnp.concatenate([gx, g_dt], axis=1)
    grad_w_xdt = dot_tn(normed, g_xdt)
    summed_xdt = ring.reduce_rows(grad_w_xdt)
    summed_xdt = range_ring.reduce_rows(summed_xdt)
    full_xdt = full_cat[:, : inner + LANES]

    def partial_of(m):
        rank = line.target(m)
        return dot_t(block(late_z, rank), full_z) + dot_t(block(g_xdt, rank), full_xdt)

    _, all_others = lax.optimization_barrier((gx_last, all_others))
    gn = line.sum_pieces(partial_of)
    gn = gn + dot_t(block(gbc, line.me), full_cat[:, inner + LANES :])

    out_own = dot_t(block(gated_out, line.me), full_out)
    if ranks > 1:
        out_own = out_own + dot_t(jnp.concatenate(mixed, axis=1), ring.join(all_others))
    block_own = (block(block_input, line.me).astype(f32) + out_own).astype(bf16)
    pieces = line.all_pieces(block_own)
    block_output = jnp.zeros((length, width), bf16)
    for m, first, piece in pieces:
        block_output = lax.dynamic_update_slice_in_dim(
            block_output, piece, line.source(m) * quarter + first, 0
        )

    x_own, inv_own = block(block_input, line.me).astype(f32), block(inverse, line.me)
    scaled = norm_gain * gn
    delta = inv_own * scaled - x_own * (inv_own * inv_own * inv_own) * jnp.mean(
        scaled * x_own, axis=1, keepdims=True
    )
    delta = lax.optimization_barrier(delta.astype(bf16))
    grad_norm_gain = jnp.sum(gn * x_own * inv_own, axis=0)
    pieces = line.all_pieces(delta, 2)
    back_pieces = pieces

    summed_bc = ring.reduce_rows(dot_tn(normed, gbc))
    summed_bc = range_ring.reduce_rows(summed_bc)

    last = jnp.pad(jnp.concatenate([grad_dt_bias[:LANES], grad_a_log]), (0, inner - 2 * LANES))[None, :]
    packed = jnp.concatenate(
        [
            jnp.concatenate([conv_acc[:CONV] + extra, conv_acc[CONV : CONV + 1], gate_acc[:2], last], axis=0),
            jnp.concatenate(
                [grad_conv_bc, grad_conv_bc_bias[None, :], jnp.zeros((3, 2 * STATE), f32)], axis=0
            ),
        ],
        axis=1,
    )
    wide_lanes = packed.shape[1]
    spare = (-width) % wide_lanes
    gain_rows = jnp.pad(grad_norm_gain, (0, spare)).reshape(-1, wide_lanes)
    packed = range_ring.total(jnp.concatenate([packed, gain_rows], axis=0))
    packed = ring.total(packed)
    gain_rows = packed[8:]
    parts = [gain_rows] + [line.send(gain_rows, m) for m in range(1, ranks)]
    ordered = jnp.zeros((ranks,) + gain_rows.shape, f32)
    for m in range(ranks):
        ordered = lax.dynamic_update_slice_in_dim(ordered, parts[m][None], line.source(m), 0)
    sum_norm_gain = jnp.sum(ordered, axis=0).reshape(-1)[:width]
    input_grad = jnp.zeros((length, width), f32)
    for m, first, piece in back_pieces:
        first = line.source(m) * quarter + first
        kept = lax.dynamic_slice_in_dim(out_cotangent, first, piece.shape[0])
        input_grad = lax.dynamic_update_slice_in_dim(
            input_grad, kept.astype(f32) + piece.astype(f32), first, 0
        )
    return (
        block_output,
        input_grad,
        summed_z,
        summed_xdt[:, :inner],
        summed_bc,
        summed_xdt[:, inner : inner + heads],
        summed_out,
        sum_norm_gain,
        packed[:CONV, :inner],
        packed[CONV, :inner],
        packed[:CONV, inner:],
        packed[CONV, inner:],
        packed[7, :heads],
        packed[7, LANES : LANES + heads],
        jnp.sum(packed[6, :inner].reshape(heads, HEAD_DIM), axis=1),
        packed[5, :inner],
    )


def solution(mesh):
    in_specs = (
        P((SHARD, CONTEXT), None),
        P(),
        P(SHARD, TENSOR),
        P(SHARD, TENSOR),
        P(SHARD, None),
        P(SHARD, TENSOR),
        P(None, TENSOR),
        P(TENSOR),
        P(),
        P(),
        P(TENSOR),
        P(TENSOR),
        P(TENSOR),
        P(TENSOR),
        P(TENSOR, SHARD),
        P((SHARD, CONTEXT), None),
    )
    out_specs = (
        P((SHARD, CONTEXT), None),
        P((SHARD, CONTEXT), None),
        P((SHARD, CONTEXT), TENSOR),
        P((SHARD, CONTEXT), TENSOR),
        P((SHARD, CONTEXT), None),
        P((SHARD, CONTEXT), TENSOR),
        P(TENSOR, (SHARD, CONTEXT)),
        P(),
        P(None, TENSOR),
        P(TENSOR),
        P(),
        P(),
        P(TENSOR),
        P(TENSOR),
        P(TENSOR),
        P(TENSOR),
    )
    return jax.shard_map(body, mesh=mesh, in_specs=in_specs, out_specs=out_specs, check_vma=False)
```

```python
import functools

import jax
import jax.numpy as jnp
from jax import lax
from jax.experimental import pallas as pl
from jax.experimental.layout import Layout, with_layout_constraint
from jax.experimental.pallas import tpu as pltpu
from jax.sharding import PartitionSpec as P


HEADS = 48
HEAD_DIM = 64
STATE = 128
CONV = 4
SPAN = 128
LANES = 128

epsilon = 1e-05
SHARD = "shard"
CONTEXT = "context"
TENSOR = "tensor"
f32 = jnp.float32
bf16 = jnp.bfloat16


def split(v):
    hi = v.astype(bf16)
    return hi, (v - hi.astype(f32)).astype(bf16)


def dot(a, b):
    return lax.dot_general(a, b, (((1,), (0,)), ((), ())), preferred_element_type=f32)


def dot_t(a, b):
    return lax.dot_general(a, b, (((1,), (1,)), ((), ())), preferred_element_type=f32)


def dot_tn(a, b):
    return lax.dot_general(a, b, (((0,), (0,)), ((), ())), preferred_element_type=f32)


def lhs3(parts):
    hi, lo = parts
    return jnp.concatenate([hi, lo, hi], axis=1)


def rhs3(parts):
    hi, lo = parts
    return jnp.concatenate([hi, hi, lo], axis=0)


def rhs3_t(parts):
    hi, lo = parts
    return jnp.concatenate([hi, hi, lo], axis=1)


def spread(values, spread_mat):
    hi, lo = split(values)
    return dot(jnp.concatenate([hi, lo], axis=1), spread_mat)


def gather_heads(values, gather_mat):
    hi, lo = split(values)
    return dot(jnp.concatenate([hi, lo], axis=1), gather_mat)


def tri_sum(tri2, values):
    hi, lo = split(values)
    return dot(tri2, jnp.concatenate([hi, lo], axis=0))


def sigmoid(v):
    return 1.0 / (1.0 + jnp.exp(-v))


def slope_of(v, sigma):
    return sigma * (1.0 + v * (1.0 - sigma))


def front_kernel(x_ref, bc_ref, edge_ref, cw_ref, cb_ref, step_ref, rate_ref, spread_ref, tri_ref,
                 pre_ref, act_ref, cum_ref, state_ref, total_ref, ext, state):
    c = pl.program_id(0)
    rows, inner = x_ref.shape
    wide = cw_ref.shape[1]

    @pl.when(c == 0)
    def _():
        ext[0:8, :] = edge_ref[...]
        state[...] = jnp.zeros_like(state)
        total_ref[...] = jnp.zeros_like(total_ref)

    ext[8 : 8 + rows, 0:inner] = x_ref[...].astype(f32)
    ext[8 : 8 + rows, inner:wide] = bc_ref[...].astype(f32)
    pre = cb_ref[...] + cw_ref[0:1, :] * ext[5 : 5 + rows, :]
    for k in range(1, CONV):
        pre = pre + cw_ref[k : k + 1, :] * ext[5 + k : 5 + k + rows, :]
    ext[0:8, :] = ext[rows : rows + 8, :]
    act = pre * sigmoid(pre)
    pre_ref[...] = pre
    act_ref[...] = act
    step = step_ref[...]
    cum = tri_sum(tri_ref[...], -step * rate_ref[...])
    cum_ref[...] = cum
    total = cum[rows - 1 : rows, :]
    b_t = jnp.transpose(act[:, inner : inner + STATE])
    weight = spread(step * jnp.exp(total - cum), spread_ref[...])
    decay = spread(jnp.broadcast_to(jnp.exp(total), (8, LANES)), spread_ref[...])[0:1, :]
    new = decay * state[...] + dot(lhs3(split(b_t)), rhs3(split(act[:, 0:inner] * weight)))
    state[...] = new
    state_ref[...] = new
    total_ref[...] = total_ref[...] + jnp.broadcast_to(total, (8, LANES))


def forward_kernel(act_ref, step_ref, cum_ref, z_ref, ggo_ref, s_in_ref, d_ref, gain_ref, spread_ref,
                   mixer_ref, enter_ref, exit_ref, sums_ref, state):
    c = pl.program_id(0)
    rows, inner = z_ref.shape

    @pl.when(c == 0)
    def _():
        state[...] = s_in_ref[...]

    heads = inner // HEAD_DIM
    per = LANES // HEAD_DIM
    spread_mat = spread_ref[...]
    x = act_ref[:, 0:inner]
    b_mat = act_ref[:, inner : inner + STATE]
    c_mat = act_ref[:, inner + STATE : inner + 2 * STATE]
    step = step_ref[...]
    cum = cum_ref[...]
    cum_t = jnp.transpose(cum)
    total = cum[rows - 1 : rows, :]
    wide = spread(
        jnp.concatenate([step, step * jnp.exp(total - cum), jnp.exp(cum)], axis=0), spread_mat
    )
    decay = spread(jnp.broadcast_to(jnp.exp(total), (8, LANES)), spread_mat)[0:1, :]
    x_step = x * wide[0:rows]
    c3 = lhs3(split(c_mat))
    scores = dot_t(c3, rhs3_t(split(b_mat)))
    enter = state[...]
    enter_ref[...] = enter
    outer = dot(c3, rhs3(split(enter))) * wide[2 * rows : 3 * rows]
    lower = lax.broadcasted_iota(jnp.int32, (rows, rows), 0) >= lax.broadcasted_iota(
        jnp.int32, (rows, rows), 1
    )
    lane = lax.broadcasted_iota(jnp.int32, (rows, LANES), 1)
    masked = jnp.where(lower, scores, 0.0)
    tiles = []
    for tile in range(heads // per):
        value = rhs3(split(x_step[:, tile * LANES : (tile + 1) * LANES]))
        got = None
        for j in range(per):
            h = tile * per + j
            gap = cum[:, h : h + 1] - cum_t[h : h + 1, :]
            part = dot(lhs3(split(jnp.exp(jnp.minimum(gap, 0.0)) * masked)), value)
            got = part if got is None else jnp.where(lane >= j * HEAD_DIM, part, got)
        tiles.append(got)
    inner_out = jnp.concatenate(tiles, axis=1)
    mixer = inner_out + outer + d_ref[...] * x
    mixer_ref[...] = mixer
    b_t = jnp.transpose(b_mat)
    new = decay * enter + dot(lhs3(split(b_t)), rhs3(split(x * wide[rows : 2 * rows])))
    state[...] = new
    exit_ref[...] = new
    z = z_ref[...]
    gated = mixer * (z * sigmoid(z))
    square = jnp.sum(gated * gated, axis=1, keepdims=True)
    term = jnp.sum(gain_ref[...] * ggo_ref[...] * gated, axis=1, keepdims=True)
    both = jnp.where(lane == 0, square, term)
    sums_ref[...] = jnp.transpose(both)[0:8, :]


def gate_kernel(inner_width, mixer_ref, z_ref, ggo_ref, sums_ref, act_ref, cum_ref, gain_ref, spread_ref,
                out_ref, gm_ref, gz_ref, own_ref, acc_ref, state):
    c = pl.program_id(0)
    rows, inner = z_ref.shape

    @pl.when(c == 0)
    def _():
        state[...] = jnp.zeros_like(state)
        acc_ref[...] = jnp.zeros_like(acc_ref)

    spread_mat = spread_ref[...]
    columns = jnp.transpose(jnp.concatenate([sums_ref[...]] * (LANES // 8), axis=0))
    inverse = lax.rsqrt(columns[:, 0:1] / inner_width + epsilon)
    term = columns[:, 1:2] / inner_width
    mixer = mixer_ref[...]
    z = z_ref[...]
    sigma = sigmoid(z)
    gate = z * sigma
    gated = mixer * gate
    ggo = ggo_ref[...]
    normal = gated * inverse
    out_ref[...] = (normal * gain_ref[...]).astype(bf16)
    grad_gated = inverse * (gain_ref[...] * ggo) - normal * (inverse * inverse * term)
    gm = grad_gated * gate
    gm_ref[...] = gm
    gz_ref[...] = (grad_gated * mixer * slope_of(z, sigma)).astype(bf16)
    x = act_ref[:, 0:inner]
    c_mat = act_ref[:, inner + STATE : inner + 2 * STATE]
    acc_ref[0:1, :] += jnp.sum(ggo * normal, axis=0, keepdims=True)
    acc_ref[1:2, :] += jnp.sum(gm * x, axis=0, keepdims=True)
    cum = cum_ref[...]
    total = cum[rows - 1 : rows, :]
    grown = spread(jnp.exp(cum), spread_mat)
    decay = spread(jnp.broadcast_to(jnp.exp(total), (8, LANES)), spread_mat)[0:1, :]
    new = decay * state[...] + dot(
        lhs3(split(jnp.transpose(c_mat))), rhs3(split(gm * grown))
    )
    state[...] = new
    own_ref[...] = new


def backward_kernel(gm_ref, act_ref, pre_ref, step_ref, cum_ref, mixer_ref, enter_ref, exit_ref, carried_ref,
                    x_raw_ref, cw_ref, d_ref, rate_ref, spread_ref, gather_ref, upper_ref,
                    gx_ref, tail_ref, head_ref, dbc_ref, gstep_ref, conv_ref, rate_out_ref,
                    state, ext):
    c = pl.program_id(0)
    rows, inner = gm_ref.shape

    @pl.when(c == 0)
    def _():
        state[...] = carried_ref[...]
        ext[rows : rows + 8, :] = jnp.zeros((8, inner), f32)
        conv_ref[...] = jnp.zeros_like(conv_ref)
        rate_out_ref[...] = jnp.zeros_like(rate_out_ref)

    heads = inner // HEAD_DIM
    per = LANES // HEAD_DIM
    spread_mat = spread_ref[...]
    gather_mat = gather_ref[...]
    gm = gm_ref[...]
    x = act_ref[:, 0:inner]
    b_mat = act_ref[:, inner : inner + STATE]
    c_mat = act_ref[:, inner + STATE : inner + 2 * STATE]
    step = step_ref[...]
    cum = cum_ref[...]
    cum_t = jnp.transpose(cum)
    total = cum[rows - 1 : rows, :]
    wide = spread(
        jnp.concatenate([step, jnp.exp(total - cum), jnp.exp(cum)], axis=0), spread_mat
    )
    step_wide, tail_wide, grown = wide[0:rows], wide[rows : 2 * rows], wide[2 * rows : 3 * rows]
    decay = spread(jnp.broadcast_to(jnp.exp(total), (8, LANES)), spread_mat)[0:1, :]
    x_step = x * step_wide
    b_parts, c_parts = split(b_mat), split(c_mat)
    b3 = lhs3(b_parts)
    scores_t = dot_t(b3, rhs3_t(c_parts))
    grad_exit = state[...]
    exit_parts = split(grad_exit)
    upper = lax.broadcasted_iota(jnp.int32, (rows, rows), 1) >= lax.broadcasted_iota(
        jnp.int32, (rows, rows), 0
    )
    lane = lax.broadcasted_iota(jnp.int32, (rows, LANES), 1)
    through = dot(b3, rhs3(exit_parts)) * tail_wide
    gm_hi, gm_lo = split(gm)
    xs_hi, xs_lo = split(x_step)
    tiles = []
    grad_scores = jnp.zeros((rows, rows), f32)
    zero = jnp.zeros((rows, LANES), bf16)
    for tile in range(heads // per):
        cut = slice(tile * LANES, (tile + 1) * LANES)
        g_hi, g_lo = gm_hi[:, cut], gm_lo[:, cut]
        g_rows = jnp.concatenate([g_hi, g_hi, g_lo], axis=0)
        g_lanes = jnp.concatenate([g_hi, g_hi, g_lo], axis=1)
        got = None
        for j in range(per):
            h = tile * per + j
            keep = (lane >= j * HEAD_DIM) & (lane < (j + 1) * HEAD_DIM)
            xh = jnp.where(keep, xs_hi[:, cut], zero)
            xl = jnp.where(keep, xs_lo[:, cut], zero)
            gap = cum_t[h : h + 1, :] - cum[:, h : h + 1]
            span = jnp.where(upper, jnp.exp(jnp.minimum(gap, 0.0)), 0.0)
            pairs = dot_t(jnp.concatenate([xh, xl, xh], axis=1), g_lanes)
            grad_scores = grad_scores + span * pairs
            part = dot(lhs3(split(span * scores_t)), g_rows)
            got = part if got is None else jnp.where(lane >= j * HEAD_DIM, part, got)
        tiles.append(got)
    grad_xs = jnp.concatenate(tiles, axis=1) + through
    scores_parts = split(grad_scores)
    weighted = gm * grown
    weighted_parts = split(weighted)
    enter_parts = split(enter_ref[...])
    grad_b = dot(lhs3(scores_parts), rhs3(c_parts)) + dot_t(
        lhs3(split(x_step * tail_wide)), rhs3_t(exit_parts)
    )
    grad_c = dot(lhs3(split(jnp.transpose(grad_scores))), rhs3(b_parts)) + dot_t(
        lhs3(weighted_parts), rhs3_t(enter_parts)
    )
    dbc_ref[:, 0:STATE] = grad_b
    dbc_ref[:, STATE : 2 * STATE] = grad_c
    lost = jnp.sum(grad_exit * exit_ref[...], axis=0, keepdims=True)
    state[...] = decay * grad_exit + dot(
        lhs3(split(jnp.transpose(c_mat))), rhs3(weighted_parts)
    )
    ssd = mixer_ref[...] - d_ref[...] * x
    heads_sum = gather_heads(
        jnp.concatenate([gm * ssd, x * grad_xs, jnp.broadcast_to(lost, (8, inner))], axis=0), gather_mat
    )
    by_step = heads_sum[rows : 2 * rows]
    grad_log = tri_sum(upper_ref[...], heads_sum[0:rows] - step * by_step) + heads_sum[
        2 * rows : 2 * rows + 1
    ]
    gstep_ref[...] = by_step - rate_ref[...] * grad_log
    rate_out_ref[0:1, :] += -jnp.sum(grad_log * step, axis=0, keepdims=True)
    pre = pre_ref[...]
    grad_pre = (grad_xs * step_wide + d_ref[...] * gm) * slope_of(pre, sigmoid(pre))
    ext[0:rows, :] = grad_pre
    raw = x_raw_ref[...].astype(f32)
    conv_ref[CONV : CONV + 1, :] += jnp.sum(grad_pre, axis=0, keepdims=True)
    total_in = None
    for k in range(CONV):
        moved = ext[CONV - 1 - k : CONV - 1 - k + rows, :]
        conv_ref[k : k + 1, :] += jnp.sum(moved * raw, axis=0, keepdims=True)
        piece = cw_ref[k : k + 1, :] * moved
        total_in = piece if total_in is None else total_in + piece
    gx_ref[...] = total_in.astype(bf16)

    @pl.when(c == 0)
    def _():
        tail_ref[...] = total_in[rows - 8 : rows, :]

    head_ref[...] = grad_pre[0:8, :]
    ext[rows : rows + 8, :] = grad_pre[0:8, :]


def shifted(value, axis, by):
    length = lax.axis_size(axis)
    pairs = [(i, i + by) for i in range(length) if 0 <= i + by < length]
    return lax.ppermute(value, axis, pairs)


def chain(local, decay, axis, by):
    got = None
    for _ in range(lax.axis_size(axis) - 1):
        got = shifted(local if got is None else local + decay * got, axis, by)
    return jnp.zeros_like(local) if got is None else got


class Ring:
    def __init__(self, axis):
        self.axis = axis
        self.size = lax.axis_size(axis)
        self.me = lax.axis_index(axis)
        self.paired = self.size & (self.size - 1) == 0

    def target(self, m):
        return self.me ^ m if self.paired else (self.me + m) % self.size

    def source(self, m):
        return self.me ^ m if self.paired else (self.me - m) % self.size

    def send(self, value, m):
        pairs = [(i, i ^ m if self.paired else (i + m) % self.size) for i in range(self.size)]
        return lax.ppermute(value, self.axis, pairs)

    def far(self, value):
        if self.size == 1 or not self.paired:
            return {0: value}
        return {0: value, self.size // 2: self.send(value, self.size // 2)}

    def near(self, pieces):
        step = self.size // 4
        while step and self.paired:
            pieces = {**pieces, **{m | step: self.send(piece, step) for m, piece in pieces.items()}}
            step //= 2
        return pieces

    def join(self, pieces):
        value = pieces[0]
        if self.paired:
            rows = value.shape[0]
            full = jnp.zeros((rows * self.size,) + value.shape[1:], value.dtype)
            for m, piece in pieces.items():
                full = lax.dynamic_update_slice_in_dim(full, piece, self.source(m) * rows, 0)
        else:
            full = lax.all_gather(value, self.axis, axis=0, tiled=True)
        return with_layout_constraint(full, Layout((0, 1)))

    def reduce_rows(self, value):
        if not self.paired:
            return lax.psum_scatter(value, self.axis, scatter_dimension=0, tiled=True)
        rows, step = value.shape[0] // self.size, 1
        value = with_layout_constraint(value, Layout((0, 1)))
        parts = {m: lax.dynamic_slice_in_dim(value, self.target(m) * rows, rows) for m in range(self.size)}
        while step < self.size:
            parts = {
                m: part + self.send(parts[m | step], step) for m, part in parts.items() if not m & step
            }
            step *= 2
        return parts[0]

    def sum_pieces(self, piece):
        if self.size != 4:
            got = [self.send(piece(m).astype(bf16), m) for m in range(1, self.size)]
            total = piece(0)
            for value in got:
                total = total + value.astype(f32)
            return total
        far = piece(3).astype(bf16)
        handed = lax.ppermute(far, self.axis, [(0, 1), (3, 2)])
        middle = lax.ppermute(far, self.axis, [(1, 2), (2, 1)])
        near = self.send(piece(1).astype(bf16), 1)
        across = self.send((piece(2) + handed.astype(f32)).astype(bf16), 2)
        total = piece(0)
        for value in (middle, near, across):
            total = total + value.astype(f32)
        return total

    def all_pieces(self, own, parts=1):
        rows = own.shape[0] // parts
        cuts = [own[p * rows : (p + 1) * rows] for p in range(parts)]
        if self.size != 4:
            return [
                (m, p * rows, self.send(cut, m) if m else cut) for m in range(self.size) for p, cut in enumerate(cuts)
            ]
        direct = []
        for cut in cuts:
            middle = lax.ppermute(cut, self.axis, [(1, 2), (2, 1)])
            cross = lax.ppermute(cut, self.axis, [(0, 2), (3, 1)])
            direct.append((self.send(cut, 1), middle, cross))
        found = [(0, p * rows, cut) for p, cut in enumerate(cuts)]
        for p, (near, middle, cross) in enumerate(direct):
            first = lax.ppermute(middle, self.axis, [(1, 0), (2, 3)])
            second = lax.ppermute(cross, self.axis, [(1, 0), (2, 3)])
            found += [(1, p * rows, near), (2, p * rows, cross + first), (3, p * rows, middle + second)]
        return found

    def total(self, value):
        if not self.paired:
            return lax.psum(value, self.axis)
        step = 1
        while step < self.size:
            value = value + self.send(value, step)
            step *= 2
        return value


def body(
    block_input,
    norm_gain,
    w_z,
    w_x,
    w_bc,
    w_dt,
    conv_x_weight,
    conv_x_bias,
    conv_bc_weight,
    conv_bc_bias,
    dt_bias,
    a_log,
    d_skip,
    gate_gain,
    w_out,
    out_cotangent,
):
    length, width = block_input.shape
    inner = w_z.shape[1]
    heads = w_dt.shape[1]
    wide = inner + 2 * STATE
    inner_width = HEADS * HEAD_DIM
    line = Ring(TENSOR)
    ranks = line.size
    quarter = length // ranks
    rows = min(SPAN, length)
    count = length // rows

    w_cat = jnp.concatenate([w_x, jnp.pad(w_dt, ((0, 0), (0, LANES - heads))), w_bc], axis=1)
    ring, range_ring = Ring(SHARD), Ring(CONTEXT)
    w_out_t = w_out.T
    full_cat = ring.join(ring.near(ring.far(w_cat)))
    others = [line.send(w_out_t, m) for m in range(1, ranks)]
    far_z = ring.far(w_z)
    far_out = ring.far(w_out_t)

    x_float = block_input.astype(f32)
    inverse = lax.rsqrt(jnp.mean(x_float * x_float, axis=1, keepdims=True) + epsilon)
    normed = (x_float * inverse * norm_gain).astype(bf16)
    proj = jnp.dot(normed, full_cat, preferred_element_type=f32)
    x_raw = proj[:, :inner].astype(bf16)
    dt_raw = proj[:, inner : inner + LANES]
    bc_raw = proj[:, inner + LANES :].astype(bf16)

    edge = shifted(
        jnp.concatenate([x_raw[length - CONV + 1 :], bc_raw[length - CONV + 1 :]], axis=1), CONTEXT, 1
    ).astype(f32)
    edge = jnp.pad(edge, ((8 - CONV + 1, 0), (0, 0)))
    conv_weight = jnp.concatenate([conv_x_weight, conv_bc_weight], axis=1)
    conv_bias = jnp.concatenate([conv_x_bias, conv_bc_bias])[None, :]
    dt_in = dt_raw + jnp.pad(dt_bias, (0, LANES - heads))
    step = jax.nn.softplus(dt_in)
    decay_rate = jnp.exp(a_log)
    rate_row = jnp.pad(decay_rate, (0, LANES - heads))[None, :]
    d_row = jnp.repeat(d_skip, HEAD_DIM)[None, :]
    gain_row = gate_gain[None, :]
    owner = jnp.arange(inner) // HEAD_DIM
    one_hot = (jnp.arange(LANES)[:, None] == owner[None, :]).astype(bf16)
    spread_mat = jnp.concatenate([one_hot, one_hot], axis=0)
    one_hot_t = (owner[:, None] == jnp.arange(LANES)[None, :]).astype(bf16)
    gather_mat = jnp.concatenate([one_hot_t, one_hot_t], axis=0)
    place = jnp.arange(rows)
    lower = (place[:, None] >= place[None, :]).astype(bf16)
    lower2 = jnp.concatenate([lower, lower], axis=1)
    upper = (place[:, None] <= place[None, :]).astype(bf16)
    upper2 = jnp.concatenate([upper, upper], axis=1)

    def whole(shape):
        return pl.BlockSpec(shape, lambda c: (0,) * len(shape))

    def ahead(lanes, high=rows):
        return pl.BlockSpec((high, lanes), lambda c: (c, 0))

    def back(lanes, high=rows):
        return pl.BlockSpec((high, lanes), lambda c: (count - 1 - c, 0))

    def shape(*dims, dtype=f32):
        return jax.ShapeDtypeStruct(dims, dtype)

    params = pltpu.CompilerParams(dimension_semantics=("arbitrary",))

    pre, act, cum, s_local, totals = pl.pallas_call(
        front_kernel,
        grid=(count,),
        in_specs=[
            ahead(inner), ahead(2 * STATE), whole((8, wide)), whole((CONV, wide)), whole((1, wide)),
            ahead(LANES), whole((1, LANES)), whole((2 * LANES, inner)), whole((rows, 2 * rows)),
        ],
        out_specs=[ahead(wide), ahead(wide), ahead(LANES), whole((STATE, inner)), whole((8, LANES))],
        out_shape=[
            shape(length, wide), shape(length, wide), shape(length, LANES), shape(STATE, inner),
            shape(8, LANES),
        ],
        scratch_shapes=[pltpu.VMEM((rows + 8, wide), f32), pltpu.VMEM((STATE, inner), f32)],
        compiler_params=params,
        name="front",
    )(x_raw, bc_raw, edge, conv_weight, conv_bias, step, rate_row, spread_mat, lower2)
    decay = jnp.repeat(jnp.exp(totals[0, :heads]), HEAD_DIM)[None, :]
    s_in = chain(s_local, decay, CONTEXT, 1)
    totals, far_z, far_out = lax.optimization_barrier((totals, far_z, far_out))
    full_z = ring.join(ring.near(far_z))
    full_out = ring.join(ring.near(far_out))
    z_part = dot(normed, full_z)
    ggo = jnp.dot(out_cotangent, full_out, preferred_element_type=f32)
    mixer, enter, leave, sums = pl.pallas_call(
        forward_kernel,
        grid=(count,),
        in_specs=[
            ahead(wide), ahead(LANES), ahead(LANES), ahead(inner), ahead(inner), whole((STATE, inner)),
            whole((1, inner)), whole((1, inner)), whole((2 * LANES, inner)),
        ],
        out_specs=[
            ahead(inner), ahead(inner, STATE), ahead(inner, STATE), pl.BlockSpec((8, rows), lambda c: (0, c)),
        ],
        out_shape=[
            shape(length, inner), shape(count * STATE, inner), shape(count * STATE, inner), shape(8, length),
        ],
        scratch_shapes=[pltpu.VMEM((STATE, inner), f32)],
        compiler_params=params,
        name="forward",
    )(act, step, cum, z_part, ggo, s_in, d_row, gain_row, spread_mat)
    mixer, others = lax.optimization_barrier((mixer, others))
    all_others = ring.near(ring.far(jnp.concatenate(others, axis=1)))
    parts = [line.send(sums, m) for m in range(1, ranks)]
    for part in parts:
        sums = sums + part

    gated_out, gm, grad_z, own, gate_acc = pl.pallas_call(
        functools.partial(gate_kernel, inner_width),
        grid=(count,),
        in_specs=[
            back(inner), back(inner), back(inner), pl.BlockSpec((8, rows), lambda c: (0, count - 1 - c)),
            back(wide), back(LANES), whole((1, inner)), whole((2 * LANES, inner)),
        ],
        out_specs=[back(inner), back(inner), back(inner), whole((STATE, inner)), whole((8, inner))],
        out_shape=[
            shape(length, inner, dtype=bf16), shape(length, inner), shape(length, inner, dtype=bf16),
            shape(STATE, inner), shape(8, inner),
        ],
        scratch_shapes=[pltpu.VMEM((STATE, inner), f32)],
        compiler_params=params,
        name="gate",
    )(mixer, z_part, ggo, sums, act, cum, gain_row, spread_mat)
    carried = chain(own, decay, CONTEXT, -1)

    def block(value, rank):
        return lax.dynamic_slice_in_dim(value, rank * quarter, quarter)

    mixed = [line.send(block(gated_out, line.target(m)), m) for m in range(1, ranks)]
    grad_w_out = dot_tn(out_cotangent, gated_out)
    gx, gx_tail, pre_head, dbc, gstep, conv_acc, rate_acc = pl.pallas_call(
        backward_kernel,
        grid=(count,),
        in_specs=[
            back(inner), back(wide), back(inner), back(LANES), back(LANES), back(inner),
            back(inner, STATE), back(inner, STATE), whole((STATE, inner)), back(inner), whole((CONV, inner)),
            whole((1, inner)), whole((1, LANES)), whole((2 * LANES, inner)), whole((2 * inner, LANES)),
            whole((rows, 2 * rows)),
        ],
        out_specs=[
            back(inner), whole((8, inner)), whole((8, inner)), back(2 * STATE), back(LANES), whole((8, inner)),
            whole((8, LANES)),
        ],
        out_shape=[
            shape(length, inner, dtype=bf16), shape(8, inner), shape(8, inner), shape(length, 2 * STATE),
            shape(length, LANES), shape(8, inner), shape(8, LANES),
        ],
        scratch_shapes=[pltpu.VMEM((STATE, inner), f32), pltpu.VMEM((rows + 8, inner), f32)],
        compiler_params=params,
        name="backward",
    )(gm, act, pre, step, cum, mixer, enter, leave, carried, x_raw, conv_x_weight, d_row, rate_row,
      spread_mat, gather_mat, upper2)

    got = [line.send(block(dbc, line.target(m)), m) for m in range(1, ranks)]
    bc_own = block(dbc, line.me)
    for value in got:
        bc_own = bc_own + value
    pieces = [bc_own] + [line.send(bc_own, m) for m in range(1, ranks)]
    for m in range(ranks):
        dbc = lax.dynamic_update_slice_in_dim(dbc, pieces[m], line.source(m) * quarter, 0)
    pre_bc = pre[:, inner:]
    grad_pre_bc = dbc * slope_of(pre_bc, jax.nn.sigmoid(pre_bc))
    next_head = shifted(pre_head[: CONV - 1], CONTEXT, -1)
    next_bc_head = shifted(grad_pre_bc[: CONV - 1], CONTEXT, -1)
    after = jnp.pad(next_head, ((CONV - 1, CONV - 1), (0, 0)))
    reach = jnp.zeros((CONV - 1, inner), f32)
    for k in range(CONV):
        reach = reach + conv_x_weight[k] * after[CONV - 1 - k : 2 * (CONV - 1) - k]
    gx_last = (gx_tail + jnp.pad(reach, ((8 - CONV + 1, 0), (0, 0)))).astype(bf16)
    gx = lax.dynamic_update_slice_in_dim(gx, gx_last, length - 8, 0)
    bc_pad = jnp.concatenate([grad_pre_bc, next_bc_head], axis=0)
    gbc = jnp.zeros((length, 2 * STATE), f32)
    for k in range(CONV):
        gbc = gbc + conv_bc_weight[k] * bc_pad[CONV - 1 - k : CONV - 1 - k + length]
    gbc = gbc.astype(bf16)
    head_pad = jnp.pad(pre_head[: CONV - 1], ((CONV - 1, CONV - 1), (0, 0)))
    entering = edge[8 - CONV + 1 :]
    extra = jnp.stack([
        jnp.sum(entering[:, :inner] * head_pad[CONV - 1 - k : 2 * (CONV - 1) - k], axis=0)
        for k in range(CONV)
    ])
    bc_in = jnp.concatenate([entering[:, inner:], bc_raw.astype(f32)], axis=0)
    grad_conv_bc = jnp.stack([jnp.sum(grad_pre_bc * bc_in[k : k + length], axis=0) for k in range(CONV)])
    grad_conv_bc_bias = jnp.sum(grad_pre_bc, axis=0)

    sigma = jax.nn.sigmoid(dt_in)
    g_dt = gstep * sigma
    grad_dt_bias = jnp.sum(g_dt, axis=0)
    g_dt = g_dt.astype(bf16)
    grad_a_log = rate_acc[0] * rate_row[0]

    gx, late_z = lax.optimization_barrier((gx, grad_z))
    grad_w_z = dot_tn(normed, late_z)
    summed_out, summed_z = ring.reduce_rows(grad_w_out), ring.reduce_rows(grad_w_z)
    summed_out, summed_z = range_ring.reduce_rows(summed_out).T, range_ring.reduce_rows(summed_z)
    g_xdt = jnp.concatenate([gx, g_dt], axis=1)
    grad_w_xdt = dot_tn(normed, g_xdt)
    summed_xdt = ring.reduce_rows(grad_w_xdt)
    summed_xdt = range_ring.reduce_rows(summed_xdt)
    full_xdt = full_cat[:, : inner + LANES]

    def partial_of(m):
        rank = line.target(m)
        return dot_t(block(late_z, rank), full_z) + dot_t(block(g_xdt, rank), full_xdt)

    _, all_others = lax.optimization_barrier((gx_last, all_others))
    gn = line.sum_pieces(partial_of)
    gn = gn + dot_t(block(gbc, line.me), full_cat[:, inner + LANES :])

    out_own = dot_t(block(gated_out, line.me), full_out)
    if ranks > 1:
        out_own = out_own + dot_t(jnp.concatenate(mixed, axis=1), ring.join(all_others))
    block_own = (block(block_input, line.me).astype(f32) + out_own).astype(bf16)
    pieces = line.all_pieces(block_own)
    block_output = jnp.zeros((length, width), bf16)
    for m, first, piece in pieces:
        block_output = lax.dynamic_update_slice_in_dim(
            block_output, piece, line.source(m) * quarter + first, 0
        )

    x_own, inv_own = block(block_input, line.me).astype(f32), block(inverse, line.me)
    scaled = norm_gain * gn
    delta = inv_own * scaled - x_own * (inv_own * inv_own * inv_own) * jnp.mean(
        scaled * x_own, axis=1, keepdims=True
    )
    delta = lax.optimization_barrier(delta.astype(bf16))
    grad_norm_gain = jnp.sum(gn * x_own * inv_own, axis=0)
    pieces = line.all_pieces(delta, 2)
    back_pieces = pieces

    summed_bc = ring.reduce_rows(dot_tn(normed, gbc))
    summed_bc = range_ring.reduce_rows(summed_bc)

    last = jnp.pad(jnp.concatenate([grad_dt_bias[:LANES], grad_a_log]), (0, inner - 2 * LANES))[None, :]
    packed = jnp.concatenate(
        [
            jnp.concatenate([conv_acc[:CONV] + extra, conv_acc[CONV : CONV + 1], gate_acc[:2], last], axis=0),
            jnp.concatenate(
                [grad_conv_bc, grad_conv_bc_bias[None, :], jnp.zeros((3, 2 * STATE), f32)], axis=0
            ),
        ],
        axis=1,
    )
    wide_lanes = packed.shape[1]
    spare = (-width) % wide_lanes
    gain_rows = jnp.pad(grad_norm_gain, (0, spare)).reshape(-1, wide_lanes)
    parts = [gain_rows] + [line.send(gain_rows, m) for m in range(1, ranks)]
    ordered = jnp.zeros((ranks,) + gain_rows.shape, f32)
    for m in range(ranks):
        ordered = lax.dynamic_update_slice_in_dim(ordered, parts[m][None], line.source(m), 0)
    packed = range_ring.total(jnp.concatenate([packed, jnp.sum(ordered, axis=0)], axis=0))
    packed = ring.total(packed)
    sum_norm_gain = packed[8:].reshape(-1)[:width]
    input_grad = jnp.zeros((length, width), f32)
    for m, first, piece in back_pieces:
        first = line.source(m) * quarter + first
        kept = lax.dynamic_slice_in_dim(out_cotangent, first, piece.shape[0])
        input_grad = lax.dynamic_update_slice_in_dim(
            input_grad, kept.astype(f32) + piece.astype(f32), first, 0
        )
    return (
        block_output,
        input_grad,
        summed_z,
        summed_xdt[:, :inner],
        summed_bc,
        summed_xdt[:, inner : inner + heads],
        summed_out,
        sum_norm_gain,
        packed[:CONV, :inner],
        packed[CONV, :inner],
        packed[:CONV, inner:],
        packed[CONV, inner:],
        packed[7, :heads],
        packed[7, LANES : LANES + heads],
        jnp.sum(packed[6, :inner].reshape(heads, HEAD_DIM), axis=1),
        packed[5, :inner],
    )


def solution(mesh):
    in_specs = (
        P((SHARD, CONTEXT), None),
        P(),
        P(SHARD, TENSOR),
        P(SHARD, TENSOR),
        P(SHARD, None),
        P(SHARD, TENSOR),
        P(None, TENSOR),
        P(TENSOR),
        P(),
        P(),
        P(TENSOR),
        P(TENSOR),
        P(TENSOR),
        P(TENSOR),
        P(TENSOR, SHARD),
        P((SHARD, CONTEXT), None),
    )
    out_specs = (
        P((SHARD, CONTEXT), None),
        P((SHARD, CONTEXT), None),
        P((SHARD, CONTEXT), TENSOR),
        P((SHARD, CONTEXT), TENSOR),
        P((SHARD, CONTEXT), None),
        P((SHARD, CONTEXT), TENSOR),
        P(TENSOR, (SHARD, CONTEXT)),
        P(),
        P(None, TENSOR),
        P(TENSOR),
        P(),
        P(),
        P(TENSOR),
        P(TENSOR),
        P(TENSOR),
        P(TENSOR),
    )
    return jax.shard_map(body, mesh=mesh, in_specs=in_specs, out_specs=out_specs, check_vma=False)
```
